32 devices in a mesh: shot: 4 (over x, core), tm: 8 (over z, y).
Axes of the slice: x: 2, y: 2, z: 4, core: 2. Of those that a mesh axis runs over, the one named last changes fastest.
Arguments:
- features: bfloat16 [8, 2048, 1024], P('shot', 'tm'), may hold values from -6 to 6
- weight_pool: bfloat16 [64, 128, 128], replicated, may hold values from -0.25 to 0.25
- pattern_in: int32 [24, 4], replicated, may hold values from 0 to 7
- pattern_pool: int32 [24, 4], replicated, may hold values from 0 to 63, as said below
- gate_weight: bfloat16 [1024, 16], replicated, may hold values from -0.1875 to 0.1875
- decay_rate: float32 [8], replicated, may hold values from 5e-05 to 0.04
- beta_bias: float32 [8], replicated, may hold values from -8 to -4
- norm_gain: float32 [128], replicated, may hold values from 0.25 to 1.75
- out_weight: bfloat16 [1024, 1024], replicated, may hold values from -0.1875 to 0.1875
- cotangent: bfloat16 [8, 2048, 1024], P('shot', 'tm'), may hold values from -6 to 6
Outputs:
- output: bfloat16 [8, 2048, 1024], P('shot', 'tm')
- weight_grad: bfloat16 [1024, 1024], replicated
- gain_grad: float32 [128], replicated
The draws below stay inside these ranges and needn't reach their ends.
Inputs may be any that keep to these rules, and one draw needn't show every extreme that they name: `pattern_pool`: every weight block is used by some member.
All inputs are finite; a program needn't handle non-finite values.
Results may differ from the reference program's by a relative error of at most 0.0077.
Values sent between devices are 32-bit elements; how exact they have to be, the bound alone decides.
No kernel may reach another device: no remote copies, remote signals or barrier semaphores. Data moves between devices by JAX's collectives and lax.ppermute only.
A program may use at most 128 MiB of HBM per device.

```python
import math
import jax
import jax.numpy as jnp
from jax import lax

D = 1024
H = 8
DK = 128
DV = 128
NPOOL = 64
NNZ = 4
NSEQ = 8
LEN = 2048


def draw_pattern_pool(key, part):
    key_order = jax.random.fold_in(key, 11)
    key_extra = jax.random.fold_in(key, 12)
    key_mixed = jax.random.fold_in(key, 13)
    covered = jax.random.permutation(key_order, NPOOL).astype(jnp.int32)
    extra = jax.random.randint(key_extra, (3 * H * NNZ - NPOOL,), 0, NPOOL).astype(jnp.int32)
    joined = jnp.concatenate([covered, extra])
    return jax.random.permutation(key_mixed, joined).reshape(3 * H, NNZ).astype(jnp.int32)


def set_ends(result, key, low, high):
    spot = [jax.random.randint(jax.random.fold_in(key, axis), (), 0, length) for axis, length in enumerate(result.shape)]
    widest = result.shape.index(max(result.shape))
    neighbour = spot[:widest] + [(spot[widest] + 1) % result.shape[widest]] + spot[widest + 1:]
    return result.at[tuple(spot)].set(low).at[tuple(neighbour)].set(high)


def level_of(own_key, shape, shards, low, largest):
    gain = 1.0
    for dim, parts in shards:
        heights = jax.random.uniform(jax.random.fold_in(jax.random.fold_in(own_key, 6), dim), (parts,), jnp.float32, low / len(shards), largest / len(shards))
        gain = gain * jnp.repeat(jnp.exp(heights), shape[dim] // parts).reshape((-1,) + (1,) * (len(shape) - 1 - dim))
    return gain


def scatter_about(own_key, shape, scale, most, pieces=(), held_as=jnp.bfloat16):
    entries = scale * jax.random.normal(own_key, shape, jnp.float32)
    if pieces:
        entries = entries * level_of(own_key, shape, pieces, -0.22, 0.18)
    return jnp.clip(entries, -most, most).astype(held_as)


def setup_inputs(seed: int = 0) -> dict:
    streams_of = jax.random.split(jax.random.key(seed), 11)
    return {
        "features": scatter_about(streams_of[0], (NSEQ, LEN, D), 1.0, 6.0, ((0, 4), (1, 8))),
        "weight_pool": scatter_about(streams_of[1], (NPOOL, DK, DK), (NNZ * DK) ** -0.5, 0.25),
        "pattern_in": set_ends(jax.random.randint(streams_of[2], (3 * H, NNZ), 0, D // DK), jax.random.fold_in(streams_of[2], 1), 0, (D // DK) - 1).astype(jnp.int32),
        "pattern_pool": draw_pattern_pool(jax.random.fold_in(streams_of[10], 71), 0),
        "gate_weight": scatter_about(streams_of[4], (D, 2 * H), D ** -0.5, 0.1875),
        "decay_rate": jnp.clip(jnp.exp(jax.random.uniform(streams_of[5], (H,), jnp.float32, math.log(4.999999873689376e-05), math.log(0.04))), 4.999999873689376e-05, 0.04),
        "beta_bias": jnp.clip(jax.random.uniform(streams_of[6], (H,), jnp.float32, -8.0, -4.0), -8.0, -4.0),
        "norm_gain": jnp.clip(1.0 + 0.15 * jax.random.normal(streams_of[7], (DV,), jnp.float32), 0.25, 1.75),
        "out_weight": scatter_about(streams_of[8], (H * DV, D), (H * DV) ** -0.5, 0.1875),
        "cotangent": scatter_about(streams_of[9], (NSEQ, LEN, D), 1.0, 6.0, ((0, 4), (1, 8))),
    }


FULL_PRECISION = lax.Precision.HIGHEST

def project_blocks(features, weight_pool, pattern_in, pattern_pool):
    width = features.shape[-1]
    block_width = weight_pool.shape[1]
    rows = features.reshape(-1, width // block_width, block_width)
    outputs = []
    for target in range(pattern_in.shape[0]):
        total = jnp.zeros((rows.shape[0], block_width), jnp.float32)
        for member in range(pattern_in.shape[1]):
            source = jnp.take(rows, pattern_in[target, member], axis=1).astype(jnp.float32)
            matrix = jnp.take(weight_pool, pattern_pool[target, member], axis=0).astype(jnp.float32)
            total = total + jnp.dot(source, matrix, precision=FULL_PRECISION, preferred_element_type=jnp.float32)
        outputs.append(total.astype(jnp.bfloat16))
    return jnp.stack(outputs, axis=1)

def recurrence(queries, keys, values, logdecay, betas):

    def advance(state, inputs):
        query, key, value, rate, strength = inputs
        decay = jnp.exp(rate)[..., None, None]
        recall = jnp.einsum('nhc,nhcd->nhd', key, state, precision=FULL_PRECISION)
        scaled = strength[..., None, None] * key[..., :, None]
        state = decay * (state - scaled * recall[..., None, :]) + scaled * value[..., None, :]
        output = jnp.einsum('nhc,nhcd->nhd', query, state, precision=FULL_PRECISION)
        return (state, output)
    nseq, heads, dims = (keys.shape[0], keys.shape[2], keys.shape[3])
    initial = jnp.zeros((nseq, heads, dims, values.shape[3]), jnp.float32)
    inputs = tuple((jnp.swapaxes(array, 0, 1) for array in (queries, keys, values, logdecay, betas)))
    _, outputs = lax.scan(advance, initial, inputs)
    return jnp.swapaxes(outputs, 0, 1)

def reference(features, weight_pool, pattern_in, pattern_pool, gate_weight, decay_rate, beta_bias, norm_gain, out_weight, cotangent):
    nseq, length, width = features.shape
    heads = decay_rate.shape[0]
    count = nseq * length
    projected = project_blocks(features, weight_pool, pattern_in, pattern_pool)
    dims = projected.shape[-1]
    queries = projected[:, :heads].astype(jnp.float32)
    keys_raw = projected[:, heads:2 * heads].astype(jnp.float32)
    keys = keys_raw * lax.rsqrt(lax.optimization_barrier(jnp.sum(keys_raw * keys_raw, axis=-1, keepdims=True)) + 1e-06)
    values = projected[:, 2 * heads:].astype(jnp.float32)
    rows = features.reshape(count, width)
    gates = jnp.dot(rows.astype(jnp.float32), gate_weight.astype(jnp.float32), precision=FULL_PRECISION)
    logdecay = -decay_rate * jax.nn.softplus(gates[:, :heads])
    betas = jax.nn.sigmoid(gates[:, heads:] + beta_bias)
    core = recurrence(queries.reshape(nseq, length, heads, dims), keys.reshape(nseq, length, heads, dims), values.reshape(nseq, length, heads, dims), logdecay.reshape(nseq, length, heads), betas.reshape(nseq, length, heads))
    core = core.reshape(count, heads, dims)
    normal = core * lax.rsqrt(lax.optimization_barrier(jnp.mean(core * core, axis=-1, keepdims=True)) + 1e-05)
    mixed_in = (normal * norm_gain).astype(jnp.bfloat16).reshape(count, heads * dims)
    mixed_wide = mixed_in.astype(jnp.float32)
    weight_wide = out_weight.astype(jnp.float32)
    output = jnp.dot(mixed_wide, weight_wide, precision=FULL_PRECISION).astype(jnp.bfloat16).reshape(nseq, length, width)
    cot_rows = cotangent.reshape(count, width).astype(jnp.float32)
    back = jnp.dot(cot_rows, weight_wide.T, precision=FULL_PRECISION)
    scale = 1.0 / math.sqrt(count)
    gain_grad = lax.optimization_barrier(jnp.sum(back.reshape(count, heads, dims) * normal, axis=(0, 1))) * scale
    weight_grad = (jnp.dot(mixed_wide.T, cot_rows, precision=FULL_PRECISION) * scale).astype(jnp.bfloat16)
    return (output, weight_grad, gain_grad)
```

```python
import functools
import math

import jax
import jax.numpy as jnp
from jax import lax
from jax.experimental import pallas as pl
from jax.experimental.pallas import tpu as pltpu
from jax.sharding import PartitionSpec as P

GROUPS = 1
CORES = 2
PAIR = 2
F32 = jnp.float32
BF16 = jnp.bfloat16
VMEM_LIMIT = 40 * 1024 * 1024


def dot(a, b):
    return lax.dot_general(a, b, (((1,), (0,)), ((), ())), preferred_element_type=F32)


def dot_nt(a, b):
    return lax.dot_general(a, b, (((1,), (1,)), ((), ())), preferred_element_type=F32)


def dot_tn(a, b):
    return lax.dot_general(a, b, (((0,), (0,)), ((), ())), preferred_element_type=F32)


def halves(a):
    high = a.astype(BF16)
    return high, (a - high.astype(F32)).astype(BF16)


def dot3(a, b):
    ah, al = halves(a)
    bh, bl = halves(b)
    return dot(ah, bh) + (dot(ah, bl) + dot(al, bh))


def params(**more):
    return pltpu.CompilerParams(vmem_limit_bytes=VMEM_LIMIT, **more)


def whole(shape):
    return pl.BlockSpec(shape, lambda *_: (0,) * len(shape))


def cost(flops, size):
    return pl.CostEstimate(flops=flops, bytes_accessed=size, transcendentals=0)


def gates_kernel(span, x_ref, w_ref, rate_ref, bias_ref, out_ref):
    heads = rate_ref.shape[1]
    gates = dot(x_ref[...], w_ref[...])
    raw = gates[:, :heads]
    softplus = jnp.maximum(raw, 0.0) + jnp.log1p(jnp.exp(-jnp.abs(raw)))
    logdecay = -rate_ref[...] * softplus
    out_ref[:, heads : 2 * heads] = jax.nn.sigmoid(gates[:, heads:] + bias_ref[...])
    row = lax.broadcasted_iota(jnp.int32, (span, span), 0)
    col = lax.broadcasted_iota(jnp.int32, (span, span), 1)
    lower = jnp.where(row >= col, 1.0, 0.0).astype(F32)
    for first in range(0, x_ref.shape[0], span):
        piece = logdecay[first : first + span]
        out_ref[first : first + span, :heads] = lax.dot_general(
            lower, piece, (((1,), (0,)), ((), ())), precision=lax.Precision.HIGHEST, preferred_element_type=F32
        )


def gates_call(rows, gate_weight, decay_rate, beta_bias, span):
    count, width = rows.shape
    heads = decay_rate.shape[0]
    return pl.pallas_call(
        functools.partial(gates_kernel, span),
        out_shape=jax.ShapeDtypeStruct((count, 2 * heads), F32),
        compiler_params=params(),
        cost_estimate=cost(2 * count * width * 128, count * width * 2),
        name="gates",
    )(rows, gate_weight, decay_rate.reshape(1, heads), beta_bias.reshape(1, heads))


def inverse_times(system, right):
    span = system.shape[0]
    row = lax.broadcasted_iota(jnp.int32, (span, span), 0)
    col = lax.broadcasted_iota(jnp.int32, (span, span), 1)
    apart = row ^ col
    inv = jnp.where(row == col, 1.0, jnp.where(apart == 1, -system, 0.0)).astype(BF16)
    step = 2
    while step < span:
        band = jnp.where((apart >= step) & (apart < 2 * step), system, 0.0).astype(BF16)
        inner = dot(inv, band).astype(BF16)
        inv = inv - dot(inner, inv).astype(BF16)
        step *= 2
    rounded = right.astype(BF16)
    first = dot(inv, rounded) + (right - rounded.astype(F32))
    residual = (right - first) - dot3(system, first)
    return first + dot(inv, residual.astype(BF16))


def local_kernel(
    first_head, heads, span, info, pin, ppool, x_ref, pool_ref, gate_ref, own_ref, send_ref, core_ref, query_ref
):
    head = first_head + pl.program_id(0)
    members = pin.shape[0] // (3 * heads)
    dims = pool_ref.shape[1]
    lane = lax.broadcasted_iota(jnp.int32, (span, 2 * heads), 1)
    wide = lax.broadcasted_iota(jnp.int32, (span, dims), 1)
    row = lax.broadcasted_iota(jnp.int32, (span, span), 0)
    col = lax.broadcasted_iota(jnp.int32, (span, span), 1)
    eye = (
        lax.broadcasted_iota(jnp.int32, (dims, dims), 0) == lax.broadcasted_iota(jnp.int32, (dims, dims), 1)
    ).astype(F32)
    for part in range(2):
        seq = info[0] if part == 0 else 1 - info[0]
        rows = pl.ds(pl.multiple_of(seq * span, span), span)
        projected = []
        for kind in range(3):
            target = (kind * heads + head) * members
            picked = [
                x_ref[rows, pl.ds(pl.multiple_of(pin[target + j] * dims, dims), dims)] for j in range(members)
            ]
            chosen = [pool_ref[ppool[target + j]] for j in range(members)]
            projected.append(dot(jnp.concatenate(picked, 1), jnp.concatenate(chosen, 0)).astype(BF16))
        query, key, value = projected
        key_wide = key.astype(F32)
        gates = gate_ref[rows, :]
        cumulative = jnp.sum(jnp.where(lane == head, gates, 0.0), axis=1, keepdims=True)
        beta = jnp.sum(jnp.where(lane == heads + head, gates, 0.0), axis=1, keepdims=True)
        norm = lax.rsqrt(jnp.sum(key_wide * key_wide, axis=1, keepdims=True) + 1e-06)
        across = jnp.where(wide == 0, cumulative, norm).T
        cumulative_row, norm_row = across[0:1, :], across[1:2, :]
        ratio = jnp.where(row >= col, jnp.exp(jnp.minimum(cumulative - cumulative_row, 0.0)), 0.0) * norm_row
        attend = ratio * dot_nt(query, key)
        system = jnp.where(row > col, ratio * dot_nt(key, key), 0.0) * (beta * norm)
        growth = jnp.exp(cumulative)
        right = jnp.concatenate([(beta * growth * norm) * key_wide, beta * value.astype(F32)], axis=1)
        solved = inverse_times(system, right)
        last = cumulative[span - 1 : span, :]
        high, low = halves(solved * (norm * jnp.exp(last - cumulative)))
        pushed = dot_tn(key, high) + dot_tn(key, low)
        out = own_ref if part == 0 else send_ref
        out[0, :, :dims] = jnp.exp(last) * eye - pushed[:, :dims]
        out[0, :, dims:] = pushed[:, dims:]
        seen = dot3(attend, solved)
        query_ref[rows, :] = growth * query.astype(F32) - seen[:, :dims]
        core_ref[rows, :] = seen[:, dims:]


def local_call(info, pin, ppool, rows, pool, gates, first_head, count_heads, heads, span):
    count, width = rows.shape
    dims = pool.shape[1]
    maps = jax.ShapeDtypeStruct((count_heads, dims, 2 * dims), F32)
    wide = jax.ShapeDtypeStruct((count, count_heads * dims), F32)
    map_spec = pl.BlockSpec((1, dims, 2 * dims), lambda i, *_: (i, 0, 0))
    row_spec = pl.BlockSpec((count, dims), lambda i, *_: (0, i))
    return pl.pallas_call(
        functools.partial(local_kernel, first_head, heads, span),
        out_shape=(maps, maps, wide, wide),
        grid_spec=pltpu.PrefetchScalarGridSpec(
            num_scalar_prefetch=3,
            grid=(count_heads,),
            in_specs=[whole(rows.shape), whole(pool.shape), whole(gates.shape)],
            out_specs=(map_spec, map_spec, row_spec, row_spec),
        ),
        compiler_params=params(),
        cost_estimate=cost(count_heads * 2 * 2 * span * 256 * 256 * 24, 8 * 1024 * 1024),
        name="local",
    )(info, pin, ppool, rows, pool, gates)


def apply_map(maps, state):
    dims = maps.shape[0]
    return dot3(maps[:, :dims], state)


def combine_kernel(info, own_ref, got_ref, early_ref, both_ref):
    later_is_own = info[0] == 1
    for h in range(own_ref.shape[0]):
        own, got = own_ref[h], got_ref[h]
        early = jnp.where(later_is_own, got, own)
        late = jnp.where(later_is_own, own, got)
        dims = own.shape[0]
        early_ref[h] = early
        both = apply_map(late, early)
        both_ref[h, :, :dims] = both[:, :dims]
        both_ref[h, :, dims:] = both[:, dims:] + late[:, dims:]


def combine_call(info, own, got):
    shape = jax.ShapeDtypeStruct(own.shape, F32)
    return pl.pallas_call(
        combine_kernel,
        out_shape=(shape, shape),
        in_specs=[pl.BlockSpec(memory_space=pltpu.SMEM)] + [pl.BlockSpec(memory_space=pltpu.VMEM)] * 2,
        compiler_params=params(),
        cost_estimate=cost(own.shape[0] * 6 * 128 * 128 * 256, own.size * 16),
        name="combine",
    )(info, own, got)


def hop_kernel(maps_ref, state_ref, out_ref):
    for h in range(maps_ref.shape[0]):
        maps = maps_ref[h]
        dims = maps.shape[0]
        out_ref[h] = apply_map(maps, state_ref[h]) + maps[:, dims:]


def hop_call(maps, state):
    return pl.pallas_call(
        hop_kernel,
        out_shape=jax.ShapeDtypeStruct(state.shape, F32),
        compiler_params=params(),
        cost_estimate=cost(maps.shape[0] * 6 * 128 * 128 * 128, maps.size * 8),
        name="hop",
    )(maps, state)


def split_kernel(info, maps_ref, state_ref, keep_ref, send_ref):
    second = info[0] == 1
    for h in range(maps_ref.shape[0]):
        maps = maps_ref[h]
        state = state_ref[h]
        dims = maps.shape[0]
        middle = apply_map(maps, state) + maps[:, dims:]
        keep_ref[h] = jnp.where(second, middle, state)
        send_ref[h] = jnp.where(second, state, middle)


def split_call(info, maps, state):
    shape = jax.ShapeDtypeStruct(state.shape, F32)
    return pl.pallas_call(
        split_kernel,
        out_shape=(shape, shape),
        in_specs=[pl.BlockSpec(memory_space=pltpu.SMEM)] + [pl.BlockSpec(memory_space=pltpu.VMEM)] * 2,
        compiler_params=params(),
        cost_estimate=cost(maps.shape[0] * 6 * 128 * 128 * 128, maps.size * 8),
        name="split",
    )(info, maps, state)


def mix_kernel(span, info, core_ref, query_ref, keep_ref, got_ref, gain_ref, cot_ref, normal_ref, mixed_ref, wsend_ref, wkeep_ref):
    step = pl.program_id(0)
    half = wsend_ref.shape[0]
    for part in range(2):
        seq = info[0] if part == 0 else 1 - info[0]
        rows = pl.ds(pl.multiple_of(seq * span, span), span)
        state = (keep_ref if part == 0 else got_ref)[0]
        core = core_ref[rows, :] + dot3(query_ref[rows, :], state)
        normal = core * lax.rsqrt(jnp.mean(core * core, axis=1, keepdims=True) + 1e-05)
        normal_ref[rows, :] = normal
        mixed_ref[rows, :] = (normal * gain_ref[...]).astype(BF16)
    product = dot_tn(mixed_ref[...], cot_ref[...])

    @pl.when(step < half)
    def _():
        wsend_ref[step] = product

    @pl.when(step >= half)
    def _():
        wkeep_ref[step - half] = product


def mix_call(info, core, query, keep, got, gain, cot, span):
    count, width = cot.shape
    heads_here = keep.shape[0]
    dims = gain.shape[1]
    half = heads_here // 2

    def order(i, info):
        first = jnp.where(i < half, 1 - info[1], info[1])
        return first * half + lax.rem(i, half)

    row_spec = pl.BlockSpec((count, dims), lambda i, info: (0, order(i, info)))
    state_spec = pl.BlockSpec((1, dims, dims), lambda i, info: (order(i, info), 0, 0))
    weight = jax.ShapeDtypeStruct((half, dims, width), F32)
    return pl.pallas_call(
        functools.partial(mix_kernel, span),
        out_shape=(
            jax.ShapeDtypeStruct((count, heads_here * dims), F32),
            jax.ShapeDtypeStruct((count, heads_here * dims), BF16),
            weight,
            weight,
        ),
        grid_spec=pltpu.PrefetchScalarGridSpec(
            num_scalar_prefetch=1,
            grid=(heads_here,),
            in_specs=[row_spec, row_spec, state_spec, state_spec, whole(gain.shape), whole(cot.shape)],
            out_specs=(row_spec, row_spec, whole(weight.shape), whole(weight.shape)),
        ),
        compiler_params=params(),
        cost_estimate=cost(heads_here * 2 * 512 * 1024 * 128, 6 * 1024 * 1024),
        name="mix",
    )(info, core, query, keep, got, gain, cot)


def finish_kernel(groups, *refs):
    mixed, normal = refs[:groups], refs[groups : 2 * groups]
    weight_ref, cot_ref, out_ref, gain_ref = refs[2 * groups :]
    dims = gain_ref.shape[1]

    @pl.when(pl.program_id(0) == 0)
    def _():
        gain_ref[...] = jnp.zeros_like(gain_ref)

    stacked = jnp.concatenate([ref[...] for ref in mixed], axis=1)
    out_ref[...] = dot(stacked, weight_ref[...]).astype(BF16)
    back = dot_nt(cot_ref[...], weight_ref[...])
    total = jnp.zeros((out_ref.shape[0], dims), F32)
    first = 0
    for ref in normal:
        for lane in range(0, ref.shape[1], dims):
            total += back[:, first : first + dims] * ref[:, lane : lane + dims]
            first += dims
    gain_ref[...] += jnp.sum(total.reshape(-1, 8, dims), axis=0)


def finish_call(mixed, normal, weight, cot):
    count, width = cot.shape
    block = 128
    groups = len(mixed)
    part = mixed[0].shape[1]
    dims = 128
    part_spec = pl.BlockSpec((block, part), lambda i: (i, 0))
    row_spec = pl.BlockSpec((block, width), lambda i: (i, 0))
    return pl.pallas_call(
        functools.partial(finish_kernel, groups),
        out_shape=(jax.ShapeDtypeStruct((count, width), BF16), jax.ShapeDtypeStruct((8, dims), F32)),
        grid=(count // block,),
        in_specs=[part_spec] * (2 * groups) + [whole(weight.shape), row_spec],
        out_specs=(row_spec, whole((8, dims))),
        compiler_params=params(),
        cost_estimate=cost(4 * count * width * width, 7 * 1024 * 1024),
        name="finish",
    )(*mixed, *normal, weight, cot)


def shards(mesh, features, weight_pool, pattern_in, pattern_pool, gate_weight, decay_rate, beta_bias, norm_gain, out_weight, cotangent):
    n_shot, n_tm = mesh.shape["shot"], mesh.shape["tm"]
    n_x, n_z = n_shot // CORES, n_tm // PAIR
    seqs, span, width = features.shape
    heads = decay_rate.shape[0]
    dims = weight_pool.shape[1]
    count = seqs * span
    both = ("shot", "tm")
    shot, tm = lax.axis_index("shot"), lax.axis_index("tm")
    x, core, z, y = shot // CORES, shot % CORES, tm // PAIR, tm % PAIR

    def place(xi, ci, zi, yi):
        return (xi * CORES + ci) * n_tm + zi * PAIR + yi

    def moved(array, shift, wrap=True):
        dx, dc, dz, dy = shift
        route = []
        for xi in range(n_x):
            for ci in range(CORES):
                for zi in range(n_z):
                    for yi in range(PAIR):
                        if not wrap and zi + dz >= n_z:
                            continue
                        to = place((xi + dx) % n_x, (ci + dc) % CORES, (zi + dz) % n_z, (yi + dy) % PAIR)
                        route.append((place(xi, ci, zi, yi), to))
        return lax.ppermute(array, both, route)

    info = jnp.stack([y, core]).astype(jnp.int32)
    rows = features.reshape(count, width)
    cot = cotangent.reshape(count, width)
    gain = norm_gain.reshape(1, dims)
    pin, ppool = pattern_in.reshape(-1), pattern_pool.reshape(-1)
    gates = gates_call(rows, gate_weight, decay_rate, beta_bias, span)
    each = heads // GROUPS

    locals_ = [local_call(info, pin, ppool, rows, weight_pool, gates, g * each, each, heads, span) for g in range(GROUPS)]
    maps = []
    for own, send, _, _ in locals_:
        got = moved(send, (0, 0, 0, 1))
        maps.append(combine_call(info, own, got))
    states = [jnp.zeros((each, dims, dims), F32)] * GROUPS
    for _ in range(n_z - 1):
        states = [moved(hop_call(maps[g][1], states[g]), (0, 0, 1, 0), wrap=False) for g in range(GROUPS)]
    mixes = []
    for g in range(GROUPS):
        keep, send = split_call(info, maps[g][0], states[g])
        got = moved(send, (0, 0, 0, 1))
        mixes.append(mix_call(info, locals_[g][2], locals_[g][3], keep, got, gain, cot, span))
    output, gain_part = finish_call([m[1] for m in mixes], [m[0] for m in mixes], out_weight, cot)
    scale = 1.0 / math.sqrt(count * n_shot * n_tm)
    gain_grad = jnp.sum(lax.all_gather(gain_part, both, axis=0, tiled=True), axis=0) * scale

    plane = [(dx, dy) for dx in range(n_x) for dy in range(PAIR)]
    n_plane = len(plane)
    share = each * dims // (CORES * n_plane * n_z)

    def plane_index(dx, dy):
        return ((x + dx) % n_x) * PAIR + (y + dy) % PAIR

    def picked(array, index):
        return lax.dynamic_index_in_dim(array, index, 0, keepdims=False)

    grads = []
    for g in range(GROUPS):
        _, _, w_send, w_keep = mixes[g]
        summed = w_keep + moved(w_send, (0, 1, 0, 0))
        summed = summed.reshape(n_plane, n_z, share, width)
        total = picked(summed, plane_index(0, 0))
        for dx, dy in plane[1:]:
            total = total + moved(picked(summed, plane_index(dx, dy)), (dx, 0, 0, dy))
        final = picked(total, z)
        for dz in range(1, n_z):
            final = final + moved(picked(total, (z + dz) % n_z), (0, 0, dz, 0))
        grads.append(final)
    pieces = []
    for g in range(GROUPS):
        along = jnp.zeros((n_z, share, width), F32)
        for dz in range(n_z):
            piece = grads[g] if dz == 0 else moved(grads[g], (0, 0, dz, 0))
            along = lax.dynamic_update_index_in_dim(along, piece, (z - dz) % n_z, 0)
        wide = jnp.zeros((n_plane, n_z, share, width), F32)
        for dx, dy in plane:
            piece = along if (dx, dy) == (0, 0) else moved(along, (dx, 0, 0, dy))
            wide = lax.dynamic_update_index_in_dim(wide, piece, plane_index(-dx, -dy), 0)
        other = moved(wide, (0, 1, 0, 0))
        first = jnp.where(core == 0, wide, other)
        second = jnp.where(core == 0, other, wide)
        pieces += [first.reshape(-1, width), second.reshape(-1, width)]
    weight_grad = (jnp.concatenate(pieces, axis=0) * scale).astype(BF16)
    return (output.reshape(seqs, span, width), weight_grad, gain_grad)


def solution(mesh):
    placed = (P("shot", "tm", None), P(), P(), P(), P(), P(), P(), P(), P(), P("shot", "tm", None))
    return jax.shard_map(
        functools.partial(shards, mesh),
        mesh=mesh,
        in_specs=placed,
        out_specs=(P("shot", "tm", None), P(), P()),
        check_vma=False,
    )
```

```python
import functools
import math

import jax
import jax.numpy as jnp
from jax import lax
from jax.experimental import pallas as pl
from jax.experimental.pallas import tpu as pltpu
from jax.sharding import PartitionSpec as P

GROUPS = 2
CORES = 2
PAIR = 2
PER_STEP = 2
F32 = jnp.float32
BF16 = jnp.bfloat16
VMEM_LIMIT = 40 * 1024 * 1024


def dot(a, b):
    return lax.dot_general(a, b, (((1,), (0,)), ((), ())), preferred_element_type=F32)


def dot_nt(a, b):
    return lax.dot_general(a, b, (((1,), (1,)), ((), ())), preferred_element_type=F32)


def dot_tn(a, b):
    return lax.dot_general(a, b, (((0,), (0,)), ((), ())), preferred_element_type=F32)


def halves(a):
    high = a.astype(BF16)
    return high, (a - high.astype(F32)).astype(BF16)


def dot3(a, b):
    ah, al = halves(a)
    bh, bl = halves(b)
    return dot(ah, bh) + (dot(ah, bl) + dot(al, bh))


def params(**more):
    return pltpu.CompilerParams(vmem_limit_bytes=VMEM_LIMIT, **more)


def whole(shape):
    return pl.BlockSpec(shape, lambda *_: (0,) * len(shape))


def cost(flops, size):
    return pl.CostEstimate(flops=flops, bytes_accessed=size, transcendentals=0)


def gates_kernel(span, x_ref, w_ref, rate_ref, bias_ref, out_ref):
    heads = rate_ref.shape[1]
    gates = dot(x_ref[...], w_ref[...])
    raw = gates[:, :heads]
    softplus = jnp.maximum(raw, 0.0) + jnp.log1p(jnp.exp(-jnp.abs(raw)))
    logdecay = -rate_ref[...] * softplus
    out_ref[:, heads : 2 * heads] = jax.nn.sigmoid(gates[:, heads:] + bias_ref[...])
    row = lax.broadcasted_iota(jnp.int32, (span, span), 0)
    col = lax.broadcasted_iota(jnp.int32, (span, span), 1)
    lower = jnp.where(row >= col, 1.0, 0.0).astype(F32)
    for first in range(0, x_ref.shape[0], span):
        piece = logdecay[first : first + span]
        out_ref[first : first + span, :heads] = lax.dot_general(
            lower, piece, (((1,), (0,)), ((), ())), precision=lax.Precision.HIGHEST, preferred_element_type=F32
        )


def gates_call(rows, gate_weight, decay_rate, beta_bias, span):
    count, width = rows.shape
    heads = decay_rate.shape[0]
    return pl.pallas_call(
        functools.partial(gates_kernel, span),
        out_shape=jax.ShapeDtypeStruct((count, 2 * heads), F32),
        compiler_params=params(),
        cost_estimate=cost(2 * count * width * 128, count * width * 2),
        name="gates",
    )(rows, gate_weight, decay_rate.reshape(1, heads), beta_bias.reshape(1, heads))


def solve_lower(systems, rights):
    span = systems[0].shape[0]
    row = lax.broadcasted_iota(jnp.int32, (span, span), 0)
    col = lax.broadcasted_iota(jnp.int32, (span, span), 1)
    apart = row ^ col
    invs = [jnp.where(row == col, 1.0, jnp.where(apart == 1, -s, 0.0)).astype(BF16) for s in systems]
    step = 2
    while step < span:
        keep = (apart >= step) & (apart < 2 * step)
        bands = [jnp.where(keep, s, 0.0).astype(BF16) for s in systems]
        inners = [dot(i, b).astype(BF16) for i, b in zip(invs, bands)]
        invs = [i - dot(n, i).astype(BF16) for n, i in zip(inners, invs)]
        step *= 2
    rounded = [r.astype(BF16) for r in rights]
    firsts = [dot(i, b) + (r - b.astype(F32)) for i, b, r in zip(invs, rounded, rights)]
    residuals = [(r - f) - dot3(s, f) for r, f, s in zip(rights, firsts, systems)]
    return [f + dot(i, r.astype(BF16)) for f, i, r in zip(firsts, invs, residuals)]


def local_kernel(
    first_head, heads, span, per_step, info, pin, ppool, x_ref, pool_ref, gate_ref, own_ref, send_ref, core_ref, query_ref
):
    members = pin.shape[0] // (3 * heads)
    dims = pool_ref.shape[1]
    lane = lax.broadcasted_iota(jnp.int32, (span, 2 * heads), 1)
    wide = lax.broadcasted_iota(jnp.int32, (span, dims), 1)
    row = lax.broadcasted_iota(jnp.int32, (span, span), 0)
    col = lax.broadcasted_iota(jnp.int32, (span, span), 1)
    eye = (
        lax.broadcasted_iota(jnp.int32, (dims, dims), 0) == lax.broadcasted_iota(jnp.int32, (dims, dims), 1)
    ).astype(F32)
    where = []
    heads_in = []
    for local in range(per_step):
        head = first_head + pl.program_id(0) * per_step + local
        chosen = []
        for kind in range(3):
            target = (kind * heads + head) * members
            chosen.append(jnp.concatenate([pool_ref[ppool[target + j]] for j in range(members)], 0))
        for part in range(2):
            seq = info[0] if part == 0 else 1 - info[0]
            where.append((local, part, pl.ds(pl.multiple_of(seq * span, span), span)))
            projected = []
            for kind in range(3):
                target = (kind * heads + head) * members
                picked = [
                    x_ref[where[-1][2], pl.ds(pl.multiple_of(pin[target + j] * dims, dims), dims)]
                    for j in range(members)
                ]
                projected.append(dot(jnp.concatenate(picked, 1), chosen[kind]).astype(BF16))
            heads_in.append((head, projected))
    kept, systems, rights = [], [], []
    for (local, part, rows), (head, (query, key, value)) in zip(where, heads_in):
        key_wide = key.astype(F32)
        gates = gate_ref[rows, :]
        cumulative = jnp.sum(jnp.where(lane == head, gates, 0.0), axis=1, keepdims=True)
        beta = jnp.sum(jnp.where(lane == heads + head, gates, 0.0), axis=1, keepdims=True)
        norm = lax.rsqrt(jnp.sum(key_wide * key_wide, axis=1, keepdims=True) + 1e-06)
        across = jnp.where(wide == 0, cumulative, norm).T
        cumulative_row, norm_row = across[0:1, :], across[1:2, :]
        ratio = jnp.where(row >= col, jnp.exp(jnp.minimum(cumulative - cumulative_row, 0.0)), 0.0) * norm_row
        attend = ratio * dot_nt(query, key)
        systems.append(jnp.where(row > col, ratio * dot_nt(key, key), 0.0) * (beta * norm))
        growth = jnp.exp(cumulative)
        rights.append(jnp.concatenate([(beta * growth * norm) * key_wide, beta * value.astype(F32)], axis=1))
        last = cumulative[span - 1 : span, :]
        kept.append((query, key, attend, growth, norm * jnp.exp(last - cumulative), jnp.exp(last)))
    solutions = solve_lower(systems, rights)
    for (local, part, rows), (query, key, attend, growth, tail, final), solved in zip(where, kept, solutions):
        high, low = halves(solved * tail)
        pushed = dot_tn(key, high) + dot_tn(key, low)
        out = own_ref if part == 0 else send_ref
        out[local, :, :dims] = final * eye - pushed[:, :dims]
        out[local, :, dims:] = pushed[:, dims:]
        seen = dot3(attend, solved)
        lanes = slice(local * dims, (local + 1) * dims)
        query_ref[rows, lanes] = growth * query.astype(F32) - seen[:, :dims]
        core_ref[rows, lanes] = seen[:, dims:]


def local_call(info, pin, ppool, rows, pool, gates, first_head, count_heads, heads, span):
    count, width = rows.shape
    dims = pool.shape[1]
    maps = jax.ShapeDtypeStruct((count_heads, dims, 2 * dims), F32)
    wide = jax.ShapeDtypeStruct((count, count_heads * dims), F32)
    map_spec = pl.BlockSpec((PER_STEP, dims, 2 * dims), lambda i, *_: (i, 0, 0))
    row_spec = pl.BlockSpec((count, PER_STEP * dims), lambda i, *_: (0, i))
    return pl.pallas_call(
        functools.partial(local_kernel, first_head, heads, span, PER_STEP),
        out_shape=(maps, maps, wide, wide),
        grid_spec=pltpu.PrefetchScalarGridSpec(
            num_scalar_prefetch=3,
            grid=(count_heads // PER_STEP,),
            in_specs=[whole(rows.shape), whole(pool.shape), whole(gates.shape)],
            out_specs=(map_spec, map_spec, row_spec, row_spec),
        ),
        compiler_params=params(),
        cost_estimate=cost(count_heads * 2 * 2 * span * 256 * 256 * 24, 8 * 1024 * 1024),
        name="local",
    )(info, pin, ppool, rows, pool, gates)


def apply_map(maps, state):
    dims = maps.shape[0]
    return dot3(maps[:, :dims], state)


def combine_kernel(info, own_ref, got_ref, early_ref, both_ref):
    later_is_own = info[0] == 1
    for h in range(own_ref.shape[0]):
        own, got = own_ref[h], got_ref[h]
        early = jnp.where(later_is_own, got, own)
        late = jnp.where(later_is_own, own, got)
        dims = own.shape[0]
        early_ref[h] = early
        both = apply_map(late, early)
        both_ref[h, :, :dims] = both[:, :dims]
        both_ref[h, :, dims:] = both[:, dims:] + late[:, dims:]


def combine_call(info, own, got):
    shape = jax.ShapeDtypeStruct(own.shape, F32)
    return pl.pallas_call(
        combine_kernel,
        out_shape=(shape, shape),
        in_specs=[pl.BlockSpec(memory_space=pltpu.SMEM)] + [pl.BlockSpec(memory_space=pltpu.VMEM)] * 2,
        compiler_params=params(),
        cost_estimate=cost(own.shape[0] * 6 * 128 * 128 * 256, own.size * 16),
        name="combine",
    )(info, own, got)


def hop_kernel(maps_ref, state_ref, out_ref):
    for h in range(maps_ref.shape[0]):
        maps = maps_ref[h]
        dims = maps.shape[0]
        out_ref[h] = apply_map(maps, state_ref[h]) + maps[:, dims:]


def hop_call(maps, state):
    return pl.pallas_call(
        hop_kernel,
        out_shape=jax.ShapeDtypeStruct(state.shape, F32),
        compiler_params=params(),
        cost_estimate=cost(maps.shape[0] * 6 * 128 * 128 * 128, maps.size * 8),
        name="hop",
    )(maps, state)


def split_kernel(info, maps_ref, state_ref, keep_ref, send_ref):
    second = info[0] == 1
    for h in range(maps_ref.shape[0]):
        maps = maps_ref[h]
        state = state_ref[h]
        dims = maps.shape[0]
        middle = apply_map(maps, state) + maps[:, dims:]
        keep_ref[h] = jnp.where(second, middle, state)
        send_ref[h] = jnp.where(second, state, middle)


def split_call(info, maps, state):
    shape = jax.ShapeDtypeStruct(state.shape, F32)
    return pl.pallas_call(
        split_kernel,
        out_shape=(shape, shape),
        in_specs=[pl.BlockSpec(memory_space=pltpu.SMEM)] + [pl.BlockSpec(memory_space=pltpu.VMEM)] * 2,
        compiler_params=params(),
        cost_estimate=cost(maps.shape[0] * 6 * 128 * 128 * 128, maps.size * 8),
        name="split",
    )(info, maps, state)


def mix_kernel(span, info, core_ref, query_ref, keep_ref, got_ref, gain_ref, cot_ref, normal_ref, mixed_ref, wsend_ref, wkeep_ref):
    step = pl.program_id(0)
    half = wsend_ref.shape[0]
    for part in range(2):
        seq = info[0] if part == 0 else 1 - info[0]
        rows = pl.ds(pl.multiple_of(seq * span, span), span)
        state = (keep_ref if part == 0 else got_ref)[0]
        core = core_ref[rows, :] + dot3(query_ref[rows, :], state)
        normal = core * lax.rsqrt(jnp.mean(core * core, axis=1, keepdims=True) + 1e-05)
        normal_ref[rows, :] = normal
        mixed_ref[rows, :] = (normal * gain_ref[...]).astype(BF16)
    product = dot_tn(mixed_ref[...], cot_ref[...])

    @pl.when(step < half)
    def _():
        wsend_ref[step] = product

    @pl.when(step >= half)
    def _():
        wkeep_ref[step - half] = product


def mix_call(info, core, query, keep, got, gain, cot, span):
    count, width = cot.shape
    heads_here = keep.shape[0]
    dims = gain.shape[1]
    half = heads_here // 2

    def order(i, info):
        first = jnp.where(i < half, 1 - info[1], info[1])
        return first * half + lax.rem(i, half)

    row_spec = pl.BlockSpec((count, dims), lambda i, info: (0, order(i, info)))
    state_spec = pl.BlockSpec((1, dims, dims), lambda i, info: (order(i, info), 0, 0))
    weight = jax.ShapeDtypeStruct((half, dims, width), F32)
    return pl.pallas_call(
        functools.partial(mix_kernel, span),
        out_shape=(
            jax.ShapeDtypeStruct((count, heads_here * dims), F32),
            jax.ShapeDtypeStruct((count, heads_here * dims), BF16),
            weight,
            weight,
        ),
        grid_spec=pltpu.PrefetchScalarGridSpec(
            num_scalar_prefetch=1,
            grid=(heads_here,),
            in_specs=[row_spec, row_spec, state_spec, state_spec, whole(gain.shape), whole(cot.shape)],
            out_specs=(row_spec, row_spec, whole(weight.shape), whole(weight.shape)),
        ),
        compiler_params=params(),
        cost_estimate=cost(heads_here * 2 * 512 * 1024 * 128, 6 * 1024 * 1024),
        name="mix",
    )(info, core, query, keep, got, gain, cot)


def finish_kernel(groups, *refs):
    mixed, normal = refs[:groups], refs[groups : 2 * groups]
    weight_ref, cot_ref, out_ref, gain_ref = refs[2 * groups :]
    dims = gain_ref.shape[1]

    @pl.when(pl.program_id(0) == 0)
    def _():
        gain_ref[...] = jnp.zeros_like(gain_ref)

    stacked = jnp.concatenate([ref[...] for ref in mixed], axis=1)
    out_ref[...] = dot(stacked, weight_ref[...]).astype(BF16)
    back = dot_nt(cot_ref[...], weight_ref[...])
    total = jnp.zeros((out_ref.shape[0], dims), F32)
    first = 0
    for ref in normal:
        for lane in range(0, ref.shape[1], dims):
            total += back[:, first : first + dims] * ref[:, lane : lane + dims]
            first += dims
    gain_ref[...] += jnp.sum(total.reshape(-1, 8, dims), axis=0)


def finish_call(mixed, normal, weight, cot):
    count, width = cot.shape
    block = 128
    groups = len(mixed)
    part = mixed[0].shape[1]
    dims = 128
    part_spec = pl.BlockSpec((block, part), lambda i: (i, 0))
    row_spec = pl.BlockSpec((block, width), lambda i: (i, 0))
    return pl.pallas_call(
        functools.partial(finish_kernel, groups),
        out_shape=(jax.ShapeDtypeStruct((count, width), BF16), jax.ShapeDtypeStruct((8, dims), F32)),
        grid=(count // block,),
        in_specs=[part_spec] * (2 * groups) + [whole(weight.shape), row_spec],
        out_specs=(row_spec, whole((8, dims))),
        compiler_params=params(),
        cost_estimate=cost(4 * count * width * width, 7 * 1024 * 1024),
        name="finish",
    )(*mixed, *normal, weight, cot)


def shards(mesh, features, weight_pool, pattern_in, pattern_pool, gate_weight, decay_rate, beta_bias, norm_gain, out_weight, cotangent):
    n_shot, n_tm = mesh.shape["shot"], mesh.shape["tm"]
    n_x, n_z = n_shot // CORES, n_tm // PAIR
    seqs, span, width = features.shape
    heads = decay_rate.shape[0]
    dims = weight_pool.shape[1]
    count = seqs * span
    both = ("shot", "tm")
    shot, tm = lax.axis_index("shot"), lax.axis_index("tm")
    x, core, z, y = shot // CORES, shot % CORES, tm // PAIR, tm % PAIR

    def place(xi, ci, zi, yi):
        return (xi * CORES + ci) * n_tm + zi * PAIR + yi

    def moved(array, shift, wrap=True):
        dx, dc, dz, dy = shift
        route = []
        for xi in range(n_x):
            for ci in range(CORES):
                for zi in range(n_z):
                    for yi in range(PAIR):
                        if not wrap and zi + dz >= n_z:
                            continue
                        to = place((xi + dx) % n_x, (ci + dc) % CORES, (zi + dz) % n_z, (yi + dy) % PAIR)
                        route.append((place(xi, ci, zi, yi), to))
        return lax.ppermute(array, both, route)

    info = jnp.stack([y, core]).astype(jnp.int32)
    rows = features.reshape(count, width)
    cot = cotangent.reshape(count, width)
    gain = norm_gain.reshape(1, dims)
    pin, ppool = pattern_in.reshape(-1), pattern_pool.reshape(-1)
    gates = gates_call(rows, gate_weight, decay_rate, beta_bias, span)
    each = heads // GROUPS

    locals_ = [local_call(info, pin, ppool, rows, weight_pool, gates, g * each, each, heads, span) for g in range(GROUPS)]
    maps = []
    for own, send, _, _ in locals_:
        got = moved(send, (0, 0, 0, 1))
        maps.append(combine_call(info, own, got))
    states = [jnp.zeros((each, dims, dims), F32)] * GROUPS
    for _ in range(n_z - 1):
        states = [moved(hop_call(maps[g][1], states[g]), (0, 0, 1, 0), wrap=False) for g in range(GROUPS)]
    mixes = []
    for g in range(GROUPS):
        keep, send = split_call(info, maps[g][0], states[g])
        got = moved(send, (0, 0, 0, 1))
        mixes.append(mix_call(info, locals_[g][2], locals_[g][3], keep, got, gain, cot, span))
    output, gain_part = finish_call([m[1] for m in mixes], [m[0] for m in mixes], out_weight, cot)
    scale = 1.0 / math.sqrt(count * n_shot * n_tm)
    swaps = [(axis, 1 << bit) for axis, size in (("shot", n_shot), ("tm", n_tm)) for bit in range(size.bit_length() - 1)]
    per_stage = -(-len(swaps) // 5)

    def spread(value, part, stage):
        for axis, reach in swaps[stage * per_stage : (stage + 1) * per_stage]:
            size = lax.axis_size(axis)
            part = part + lax.ppermute(part, axis, [(i, i ^ reach) for i in range(size)])
        return lax.optimization_barrier((value, part))

    plane = [(dx, dy) for dx in range(n_x) for dy in range(PAIR)]
    n_plane = len(plane)
    share = each * dims // (CORES * n_plane * n_z)

    def plane_index(dx, dy):
        return ((x + dx) % n_x) * PAIR + (y + dy) % PAIR

    def picked(array, index):
        return lax.dynamic_index_in_dim(array, index, 0, keepdims=False)

    crossed = [moved(mixes[g][2], (0, 1, 0, 0)) for g in range(GROUPS)]
    crossed[-1], gain_part, output = lax.optimization_barrier((crossed[-1], gain_part, output))
    grads = []
    for g in range(GROUPS):
        summed = (mixes[g][3] + crossed[g]).reshape(n_plane, n_z, share, width)
        total = picked(summed, plane_index(0, 0))
        for dx, dy in plane[1:]:
            total = total + moved(picked(summed, plane_index(dx, dy)), (dx, 0, 0, dy))
        if g == GROUPS - 1:
            total, gain_part = spread(total, gain_part, 0)
        final = picked(total, z)
        for dz in range(1, n_z):
            final = final + moved(picked(total, (z + dz) % n_z), (0, 0, dz, 0))
        if g == GROUPS - 1:
            final, gain_part = spread(final, gain_part, 1)
        grads.append(final)
    pieces = []
    for g in range(GROUPS):
        along = jnp.zeros((n_z, share, width), F32)
        for dz in range(n_z):
            piece = grads[g] if dz == 0 else moved(grads[g], (0, 0, dz, 0))
            along = lax.dynamic_update_index_in_dim(along, piece, (z - dz) % n_z, 0)
        if g == GROUPS - 1:
            along, gain_part = spread(along, gain_part, 2)
        wide = jnp.zeros((n_plane, n_z, share, width), F32)
        for dx, dy in plane:
            piece = along if (dx, dy) == (0, 0) else moved(along, (dx, 0, 0, dy))
            wide = lax.dynamic_update_index_in_dim(wide, piece, plane_index(-dx, -dy), 0)
        if g == GROUPS - 1:
            wide, gain_part = spread(wide, gain_part, 3)
        other = moved(wide, (0, 1, 0, 0))
        if g == GROUPS - 1:
            other, gain_part = spread(other, gain_part, 4)
        first = jnp.where(core == 0, wide, other)
        second = jnp.where(core == 0, other, wide)
        pieces += [first.reshape(-1, width), second.reshape(-1, width)]
    gain_grad = jnp.sum(gain_part, axis=0) * scale
    weight_grad = (jnp.concatenate(pieces, axis=0) * scale).astype(BF16)
    return (output.reshape(seqs, span, width), weight_grad, gain_grad)


def solution(mesh):
    placed = (P("shot", "tm", None), P(), P(), P(), P(), P(), P(), P(), P(), P("shot", "tm", None))
    return jax.shard_map(
        functools.partial(shards, mesh),
        mesh=mesh,
        in_specs=placed,
        out_specs=(P("shot", "tm", None), P(), P()),
        check_vma=False,
    )
```

```python
import functools
import math

import jax
import jax.numpy as jnp
from jax import lax
from jax.experimental import pallas as pl
from jax.experimental.pallas import tpu as pltpu
from jax.sharding import PartitionSpec as P

GROUPS = 2
CORES = 2
PAIR = 2
PER_STEP = 2
F32 = jnp.float32
BF16 = jnp.bfloat16
MIB = 1024 * 1024


def dot(a, b):
    return lax.dot_general(a, b, (((1,), (0,)), ((), ())), preferred_element_type=F32)


def dot_nt(a, b):
    return lax.dot_general(a, b, (((1,), (1,)), ((), ())), preferred_element_type=F32)


def dot_tn(a, b):
    return lax.dot_general(a, b, (((0,), (0,)), ((), ())), preferred_element_type=F32)


def halves(a):
    high = a.astype(BF16)
    return high, (a - high.astype(F32)).astype(BF16)


def dot3(a, b):
    ah, al = halves(a)
    bh, bl = halves(b)
    return dot(ah, bh) + (dot(ah, bl) + dot(al, bh))


def params(mib):
    return pltpu.CompilerParams(vmem_limit_bytes=mib * MIB)


def smem():
    return pl.BlockSpec(memory_space=pltpu.SMEM)


def vmem():
    return pl.BlockSpec(memory_space=pltpu.VMEM)


def whole(shape):
    return pl.BlockSpec(shape, lambda *_: (0,) * len(shape))


def cost(flops, size):
    return pl.CostEstimate(flops=flops, bytes_accessed=size, transcendentals=0)


def gates_kernel(span, heads, x_ref, w_ref, rate_ref, bias_ref, out_ref):
    lane = lax.broadcasted_iota(jnp.int32, (1, heads), 1)
    rate = jnp.zeros((1, heads), F32)
    bias = jnp.zeros((1, heads), F32)
    for h in range(heads):
        rate = jnp.where(lane == h, rate_ref[h], rate)
        bias = jnp.where(lane == h, bias_ref[h], bias)
    gates = dot_nt(x_ref[...], w_ref[...])
    raw = gates[:, :heads]
    softplus = jnp.maximum(raw, 0.0) + jnp.log1p(jnp.exp(-jnp.abs(raw)))
    logdecay = -rate * softplus
    out_ref[:, heads : 2 * heads] = jax.nn.sigmoid(gates[:, heads:] + bias)
    row = lax.broadcasted_iota(jnp.int32, (span, span), 0)
    col = lax.broadcasted_iota(jnp.int32, (span, span), 1)
    lower = jnp.where(row >= col, 1.0, 0.0).astype(F32)
    for first in range(0, x_ref.shape[0], span):
        piece = logdecay[first : first + span]
        out_ref[first : first + span, :heads] = lax.dot_general(
            lower, piece, (((1,), (0,)), ((), ())), precision=lax.Precision.HIGHEST, preferred_element_type=F32
        )


def gates_call(rows, gate_weight, decay_rate, beta_bias, span):
    count, width = rows.shape
    heads = decay_rate.shape[0]
    return pl.pallas_call(
        functools.partial(gates_kernel, span, heads),
        out_shape=jax.ShapeDtypeStruct((count, 2 * heads), F32),
        in_specs=[vmem(), vmem(), smem(), smem()],
        compiler_params=params(12),
        cost_estimate=cost(2 * count * width * 128, count * width * 2),
        name="gates",
    )(rows, gate_weight.T, decay_rate, beta_bias)


def solve_lower(systems, rights):
    span = systems[0].shape[0]
    row = lax.broadcasted_iota(jnp.int32, (span, span), 0)
    col = lax.broadcasted_iota(jnp.int32, (span, span), 1)
    apart = row ^ col
    invs = [jnp.where(row == col, 1.0, jnp.where(apart == 1, -s, 0.0)).astype(BF16) for s in systems]
    step = 2
    while step < span:
        keep = (apart >= step) & (apart < 2 * step)
        bands = [jnp.where(keep, s, 0.0).astype(BF16) for s in systems]
        inners = [dot(i, b).astype(BF16) for i, b in zip(invs, bands)]
        invs = [i - dot(n, i).astype(BF16) for n, i in zip(inners, invs)]
        step *= 2
    rounded = [r.astype(BF16) for r in rights]
    firsts = [dot(i, b) + (r - b.astype(F32)) for i, b, r in zip(invs, rounded, rights)]
    residuals = [(r - f) - dot3(s, f) for r, f, s in zip(rights, firsts, systems)]
    return [f + dot(i, r.astype(BF16)) for f, i, r in zip(firsts, invs, residuals)]


def local_kernel(
    first_head, heads, span, per_step, info, pin, ppool, x_ref, pool_ref, gate_ref, own_ref, send_ref, core_ref, query_ref
):
    members = pin.shape[0]
    dims = pool_ref.shape[1]
    lane = lax.broadcasted_iota(jnp.int32, (span, 2 * heads), 1)
    wide = lax.broadcasted_iota(jnp.int32, (span, dims), 1)
    row = lax.broadcasted_iota(jnp.int32, (span, span), 0)
    col = lax.broadcasted_iota(jnp.int32, (span, span), 1)
    eye = (
        lax.broadcasted_iota(jnp.int32, (dims, dims), 0) == lax.broadcasted_iota(jnp.int32, (dims, dims), 1)
    ).astype(F32)
    where = []
    heads_in = []
    for local in range(per_step):
        head = first_head + pl.program_id(0) * per_step + local
        chosen = []
        for kind in range(3):
            target = kind * heads + head
            chosen.append(jnp.concatenate([pool_ref[ppool[j, target]] for j in range(members)], 0))
        for part in range(2):
            seq = info[0] if part == 0 else 1 - info[0]
            where.append((local, part, pl.ds(pl.multiple_of(seq * span, span), span)))
            projected = []
            for kind in range(3):
                target = kind * heads + head
                picked = [
                    x_ref[where[-1][2], pl.ds(pl.multiple_of(pin[j, target] * dims, dims), dims)]
                    for j in range(members)
                ]
                projected.append(dot(jnp.concatenate(picked, 1), chosen[kind]).astype(BF16))
            heads_in.append((head, projected))
    kept, systems, rights = [], [], []
    for (local, part, rows), (head, (query, key, value)) in zip(where, heads_in):
        key_wide = key.astype(F32)
        gates = gate_ref[rows, :]
        cumulative = jnp.sum(jnp.where(lane == head, gates, 0.0), axis=1, keepdims=True)
        beta = jnp.sum(jnp.where(lane == heads + head, gates, 0.0), axis=1, keepdims=True)
        norm = lax.rsqrt(jnp.sum(key_wide * key_wide, axis=1, keepdims=True) + 1e-06)
        across = jnp.where(wide == 0, cumulative, norm).T
        cumulative_row, norm_row = across[0:1, :], across[1:2, :]
        ratio = jnp.where(row >= col, jnp.exp(jnp.minimum(cumulative - cumulative_row, 0.0)), 0.0) * norm_row
        attend = ratio * dot_nt(query, key)
        systems.append(jnp.where(row > col, ratio * dot_nt(key, key), 0.0) * (beta * norm))
        growth = jnp.exp(cumulative)
        rights.append(jnp.concatenate([(beta * growth * norm) * key_wide, beta * value.astype(F32)], axis=1))
        last = cumulative[span - 1 : span, :]
        kept.append((query, key, attend, growth, norm * jnp.exp(last - cumulative), jnp.exp(last)))
    solutions = solve_lower(systems, rights)
    for (local, part, rows), (query, key, attend, growth, tail, final), solved in zip(where, kept, solutions):
        high, low = halves(solved * tail)
        pushed = dot_tn(key, high) + dot_tn(key, low)
        out = own_ref if part == 0 else send_ref
        out[local, :, :dims] = final * eye - pushed[:, :dims]
        out[local, :, dims:] = pushed[:, dims:]
        seen = dot3(attend, solved)
        lanes = slice(local * dims, (local + 1) * dims)
        query_ref[rows, lanes] = growth * query.astype(F32) - seen[:, :dims]
        core_ref[rows, lanes] = seen[:, dims:]


def local_call(info, pin, ppool, rows, pool, gates, first_head, count_heads, heads, span):
    count, width = rows.shape
    dims = pool.shape[1]
    maps = jax.ShapeDtypeStruct((count_heads, dims, 2 * dims), F32)
    wide = jax.ShapeDtypeStruct((count, count_heads * dims), F32)
    map_spec = pl.BlockSpec((PER_STEP, dims, 2 * dims), lambda i, *_: (i, 0, 0))
    row_spec = pl.BlockSpec((count, PER_STEP * dims), lambda i, *_: (0, i))
    return pl.pallas_call(
        functools.partial(local_kernel, first_head, heads, span, PER_STEP),
        out_shape=(maps, maps, wide, wide),
        grid_spec=pltpu.PrefetchScalarGridSpec(
            num_scalar_prefetch=3,
            grid=(count_heads // PER_STEP,),
            in_specs=[whole(rows.shape), whole(pool.shape), whole(gates.shape)],
            out_specs=(map_spec, map_spec, row_spec, row_spec),
        ),
        compiler_params=params(28),
        cost_estimate=cost(count_heads * 2 * 2 * span * 256 * 256 * 24, 8 * 1024 * 1024),
        name="local",
    )(info, pin, ppool, rows, pool, gates)


def apply_map(maps, state):
    dims = maps.shape[0]
    return dot3(maps[:, :dims], state)


def combine_kernel(info, own_ref, got_ref, early_ref, both_ref, push_ref):
    later_is_own = info[0] == 1
    for h in range(own_ref.shape[0]):
        own, got = own_ref[h], got_ref[h]
        early = jnp.where(later_is_own, got, own)
        late = jnp.where(later_is_own, own, got)
        dims = own.shape[0]
        early_ref[h] = early
        both = apply_map(late, early)
        push = both[:, dims:] + late[:, dims:]
        both_ref[h, :, :dims] = both[:, :dims]
        both_ref[h, :, dims:] = push
        push_ref[h] = push


def combine_call(info, own, got):
    shape = jax.ShapeDtypeStruct(own.shape, F32)
    push = jax.ShapeDtypeStruct(own.shape[:2] + (own.shape[1],), F32)
    return pl.pallas_call(
        combine_kernel,
        out_shape=(shape, shape, push),
        in_specs=[smem(), vmem(), vmem()],
        compiler_params=params(12),
        cost_estimate=cost(own.shape[0] * 6 * 128 * 128 * 256, own.size * 16),
        name="combine",
    )(info, own, got)


def hop_kernel(level, info, maps_ref, got_ref, state_ref, kept_ref, out_ref):
    arrived = info[2] == level
    for h in range(maps_ref.shape[0]):
        maps = maps_ref[h]
        dims = maps.shape[0]
        state = jnp.where(arrived, got_ref[h], state_ref[h])
        kept_ref[h] = state
        out_ref[h] = apply_map(maps, state) + maps[:, dims:]


def hop_call(level, info, maps, got, state):
    shape = jax.ShapeDtypeStruct(state.shape, F32)
    return pl.pallas_call(
        functools.partial(hop_kernel, level),
        out_shape=(shape, shape),
        in_specs=[smem(), vmem(), vmem(), vmem()],
        compiler_params=params(12),
        cost_estimate=cost(maps.shape[0] * 6 * 128 * 128 * 128, maps.size * 8),
        name="hop",
    )(info, maps, got, state)


def split_kernel(level, info, maps_ref, got_ref, state_ref, keep_ref, send_ref):
    second = info[0] == 1
    arrived = info[2] == level
    for h in range(maps_ref.shape[0]):
        maps = maps_ref[h]
        state = jnp.where(arrived, got_ref[h], state_ref[h])
        dims = maps.shape[0]
        middle = apply_map(maps, state) + maps[:, dims:]
        keep_ref[h] = jnp.where(second, middle, state)
        send_ref[h] = jnp.where(second, state, middle)


def split_call(level, info, maps, got, state):
    shape = jax.ShapeDtypeStruct(state.shape, F32)
    return pl.pallas_call(
        functools.partial(split_kernel, level),
        out_shape=(shape, shape),
        in_specs=[smem(), vmem(), vmem(), vmem()],
        compiler_params=params(12),
        cost_estimate=cost(maps.shape[0] * 6 * 128 * 128 * 128, maps.size * 8),
        name="split",
    )(info, maps, got, state)


def mix_kernel(
    span, info, core_ref, query_ref, keep_ref, got_ref, back_ref, gain_ref, cot_ref, mixed_ref, wsend_ref, wkeep_ref, part_ref
):
    step = pl.program_id(0)
    half = wsend_ref.shape[0]

    @pl.when(step == 0)
    def _():
        part_ref[...] = jnp.zeros_like(part_ref)

    for part in range(2):
        seq = info[0] if part == 0 else 1 - info[0]
        rows = pl.ds(pl.multiple_of(seq * span, span), span)
        state = (keep_ref if part == 0 else got_ref)[0]
        core = core_ref[rows, :] + dot3(query_ref[rows, :], state)
        normal = core * lax.rsqrt(jnp.mean(core * core, axis=1, keepdims=True) + 1e-05)
        part_ref[...] += jnp.sum((normal * back_ref[rows, :]).reshape(-1, 8, core.shape[1]), axis=0)
        mixed_ref[rows, :] = (normal * gain_ref[...]).astype(BF16)
    product = dot_tn(mixed_ref[...], cot_ref[...])

    @pl.when(step < half)
    def _():
        wsend_ref[step] = product

    @pl.when(step >= half)
    def _():
        wkeep_ref[step - half] = product


def mix_call(info, first_head, core, query, keep, got, back, gain, cot, span):
    count, width = cot.shape
    heads_here = keep.shape[0]
    dims = gain.shape[1]
    half = heads_here // 2

    def order(i, info):
        first = jnp.where(i < half, 1 - info[1], info[1])
        return first * half + lax.rem(i, half)

    row_spec = pl.BlockSpec((count, dims), lambda i, info: (0, order(i, info)))
    back_spec = pl.BlockSpec((count, dims), lambda i, info: (0, first_head + order(i, info)))
    state_spec = pl.BlockSpec((1, dims, dims), lambda i, info: (order(i, info), 0, 0))
    weight = jax.ShapeDtypeStruct((half, dims, width), F32)
    return pl.pallas_call(
        functools.partial(mix_kernel, span),
        out_shape=(
            jax.ShapeDtypeStruct((count, heads_here * dims), BF16),
            weight,
            weight,
            jax.ShapeDtypeStruct((8, dims), F32),
        ),
        grid_spec=pltpu.PrefetchScalarGridSpec(
            num_scalar_prefetch=1,
            grid=(heads_here,),
            in_specs=[row_spec, row_spec, state_spec, state_spec, back_spec, whole(gain.shape), whole(cot.shape)],
            out_specs=(row_spec, whole(weight.shape), whole(weight.shape), whole((8, dims))),
        ),
        compiler_params=params(20),
        cost_estimate=cost(heads_here * 2 * 512 * 1024 * 128, 6 * MIB),
        name="mix",
    )(info, core, query, keep, got, back, gain, cot)


def back_kernel(cot_ref, weight_ref, out_ref):
    out_ref[...] = dot_nt(cot_ref[...], weight_ref[...])


def back_call(cot, weight):
    count, width = cot.shape
    row_spec = pl.BlockSpec((128, width), lambda i: (i, 0))
    return pl.pallas_call(
        back_kernel,
        out_shape=jax.ShapeDtypeStruct((count, width), F32),
        grid=(count // 128,),
        in_specs=[row_spec, whole(weight.shape)],
        out_specs=row_spec,
        compiler_params=params(12),
        cost_estimate=cost(2 * count * width * width, 5 * MIB),
        name="back",
    )(cot, weight)


def finish_kernel(groups, *refs):
    weight_ref, out_ref = refs[groups:]
    stacked = jnp.concatenate([ref[...] for ref in refs[:groups]], axis=1)
    out_ref[...] = dot(stacked, weight_ref[...]).astype(BF16)


def finish_call(mixed, weight):
    count = mixed[0].shape[0]
    width = weight.shape[1]
    part_spec = pl.BlockSpec((128, mixed[0].shape[1]), lambda i: (i, 0))
    row_spec = pl.BlockSpec((128, width), lambda i: (i, 0))
    return pl.pallas_call(
        functools.partial(finish_kernel, len(mixed)),
        out_shape=jax.ShapeDtypeStruct((count, width), BF16),
        grid=(count // 128,),
        in_specs=[part_spec] * len(mixed) + [whole(weight.shape)],
        out_specs=row_spec,
        compiler_params=params(12),
        cost_estimate=cost(2 * count * width * width, 4 * MIB),
        name="finish",
    )(*mixed, weight)


def join_kernel(groups, scale, info, *refs):
    out_ref = refs[-1]
    rows = refs[0].shape[0]
    for g in range(groups):
        for part, ref in enumerate(refs[2 * g : 2 * g + 2]):
            side = info[1] if part == 0 else 1 - info[1]
            first = pl.multiple_of((2 * g + side) * rows, rows)
            out_ref[pl.ds(first, rows), :] = (ref[...] * scale).astype(BF16)


def join_call(info, parts, scale):
    rows, width = parts[0].shape
    return pl.pallas_call(
        functools.partial(join_kernel, len(parts) // 2, scale),
        out_shape=jax.ShapeDtypeStruct((rows * len(parts), width), BF16),
        in_specs=[smem()] + [vmem()] * len(parts),
        compiler_params=params(16),
        name="join",
    )(info, *parts)


def shards(mesh, features, weight_pool, pattern_in, pattern_pool, gate_weight, decay_rate, beta_bias, norm_gain, out_weight, cotangent):
    n_shot, n_tm = mesh.shape["shot"], mesh.shape["tm"]
    n_x, n_z = n_shot // CORES, n_tm // PAIR
    seqs, span, width = features.shape
    heads = decay_rate.shape[0]
    dims = weight_pool.shape[1]
    count = seqs * span
    both = ("shot", "tm")
    shot, tm = lax.axis_index("shot"), lax.axis_index("tm")
    x, core, z, y = shot // CORES, shot % CORES, tm // PAIR, tm % PAIR

    def place(xi, ci, zi, yi):
        return (xi * CORES + ci) * n_tm + zi * PAIR + yi

    def moved(array, shift):
        dx, dc, dz, dy = shift
        route = []
        for xi in range(n_x):
            for ci in range(CORES):
                for zi in range(n_z):
                    for yi in range(PAIR):
                        route.append((place(xi, ci, zi, yi), place(xi ^ dx, ci ^ dc, zi ^ dz, yi ^ dy)))
        return lax.ppermute(array, both, route)

    def lifted(array, level):
        ends = ((level, level + 1), (level + 1, level))
        route = [(a * PAIR + yi, b * PAIR + yi) for a, b in ends for yi in range(PAIR)]
        return lax.ppermute(array, "tm", route)

    info = jnp.stack([y, core, z]).astype(jnp.int32)
    rows = features.reshape(count, width)
    cot = cotangent.reshape(count, width)
    gain = norm_gain.reshape(1, dims)
    pin, ppool = pattern_in.T, pattern_pool.T
    gates = gates_call(rows, gate_weight, decay_rate, beta_bias, span)
    each = heads // GROUPS

    locals_ = [local_call(info, pin, ppool, rows, weight_pool, gates, g * each, each, heads, span) for g in range(GROUPS)]
    maps = []
    for own, send, _, _ in locals_:
        got = moved(send, (0, 0, 0, 1))
        maps.append(combine_call(info, own, got))
    back = back_call(cot, out_weight)
    states = [jnp.zeros((each, dims, dims), F32)] * GROUPS
    sends = [m[2] for m in maps]
    for level in range(1, n_z):
        gots = [lifted(send, level - 1) for send in sends]
        if level == 1:
            gots[0], back = lax.optimization_barrier((gots[0], back))
        if level == n_z - 1:
            break
        for g in range(GROUPS):
            states[g], sends[g] = hop_call(level, info, maps[g][1], gots[g], states[g])
    mixes = []
    for g in range(GROUPS):
        keep, send = split_call(n_z - 1, info, maps[g][0], gots[g], states[g])
        got = moved(send, (0, 0, 0, 1))
        mixes.append(mix_call(info, g * each, locals_[g][2], locals_[g][3], keep, got, back, gain, cot, span))
    gain_part = sum(m[3] for m in mixes)
    output = finish_call([m[0] for m in mixes], out_weight)
    scale = 1.0 / math.sqrt(count * n_shot * n_tm)
    swaps = [(axis, 1 << bit) for axis, size in (("shot", n_shot), ("tm", n_tm)) for bit in range(size.bit_length() - 1)]
    per_stage = -(-len(swaps) // 5)

    def spread(value, part, stage):
        for axis, reach in swaps[stage * per_stage : (stage + 1) * per_stage]:
            size = lax.axis_size(axis)
            part = part + lax.ppermute(part, axis, [(i, i ^ reach) for i in range(size)])
        return lax.optimization_barrier((value, part))

    plane = [(dx, dy) for dx in range(n_x) for dy in range(PAIR)]
    n_plane = len(plane)
    share = each * dims // (CORES * n_plane * n_z)

    def plane_index(dx, dy):
        return (x ^ dx) * PAIR + (y ^ dy)

    def picked(array, index):
        return lax.dynamic_index_in_dim(array, index, 0, keepdims=False)

    crossed = [moved(mixes[g][1], (0, 1, 0, 0)) for g in range(GROUPS)]
    grads = []
    for g in range(GROUPS):
        summed = (mixes[g][2] + crossed[g]).reshape(n_plane, n_z, share, width)
        total = picked(summed, plane_index(0, 0))
        for dx, dy in plane[1:]:
            total = total + moved(picked(summed, plane_index(dx, dy)), (dx, 0, 0, dy))
        if g == GROUPS - 1:
            total, gain_part = spread(total, gain_part, 0)
            total, output = lax.optimization_barrier((total, output))
        final = picked(total, z)
        for dz in range(1, n_z):
            final = final + moved(picked(total, z ^ dz), (0, 0, dz, 0))
        if g == GROUPS - 1:
            final, gain_part = spread(final, gain_part, 1)
        grads.append(final)
    pieces = []
    for g in range(GROUPS):
        along = jnp.zeros((n_z, share, width), F32)
        for dz in range(n_z):
            piece = grads[g] if dz == 0 else moved(grads[g], (0, 0, dz, 0))
            along = lax.dynamic_update_index_in_dim(along, piece, z ^ dz, 0)
        if g == GROUPS - 1:
            along, gain_part = spread(along, gain_part, 2)
        wide = jnp.zeros((n_plane, n_z, share, width), F32)
        for dx, dy in plane:
            piece = along if (dx, dy) == (0, 0) else moved(along, (dx, 0, 0, dy))
            wide = lax.dynamic_update_index_in_dim(wide, piece, plane_index(dx, dy), 0)
        if g == GROUPS - 1:
            wide, gain_part = spread(wide, gain_part, 3)
        other = moved(wide, (0, 1, 0, 0))
        if g == GROUPS - 1:
            other, gain_part = spread(other, gain_part, 4)
        pieces += [wide.reshape(-1, width), other.reshape(-1, width)]
    gain_grad = jnp.sum(gain_part, axis=0) * scale
    weight_grad = join_call(info, pieces, scale)
    return (output.reshape(seqs, span, width), weight_grad, gain_grad)


def solution(mesh):
    placed = (P("shot", "tm", None), P(), P(), P(), P(), P(), P(), P(), P(), P("shot", "tm", None))
    return jax.shard_map(
        functools.partial(shards, mesh),
        mesh=mesh,
        in_specs=placed,
        out_specs=(P("shot", "tm", None), P(), P()),
        check_vma=False,
    )
```

```python
import functools
import math

import jax
import jax.numpy as jnp
from jax import lax
from jax.experimental import pallas as pl
from jax.experimental.pallas import tpu as pltpu
from jax.sharding import PartitionSpec as P

GROUPS = 4
SUMS = 2
CORES = 2
PAIR = 2
PER_STEP = 2
AHEAD = 3
F32 = jnp.float32
BF16 = jnp.bfloat16
MIB = 1024 * 1024


def dot(a, b):
    return lax.dot_general(a, b, (((1,), (0,)), ((), ())), preferred_element_type=F32)


def dot_nt(a, b):
    return lax.dot_general(a, b, (((1,), (1,)), ((), ())), preferred_element_type=F32)


def dot_tn(a, b):
    return lax.dot_general(a, b, (((0,), (0,)), ((), ())), preferred_element_type=F32)


def halves(a):
    high = a.astype(BF16)
    return high, (a - high.astype(F32)).astype(BF16)


def dot3(a, b):
    ah, al = halves(a)
    bh, bl = halves(b)
    return dot(ah, bh) + (dot(ah, bl) + dot(al, bh))


def params(mib):
    return pltpu.CompilerParams(vmem_limit_bytes=mib * MIB)


def smem():
    return pl.BlockSpec(memory_space=pltpu.SMEM)


def vmem():
    return pl.BlockSpec(memory_space=pltpu.VMEM)


def whole(shape):
    return pl.BlockSpec(shape, lambda *_: (0,) * len(shape))


def cost(flops, size):
    return pl.CostEstimate(flops=flops, bytes_accessed=size, transcendentals=0)


def write_gates(span, heads, x_ref, w_ref, level_ref, out_ref):
    lane = lax.broadcasted_iota(jnp.int32, (1, heads), 1)
    rate = jnp.zeros((1, heads), F32)
    bias = jnp.zeros((1, heads), F32)
    for h in range(heads):
        rate = jnp.where(lane == h, level_ref[0, h], rate)
        bias = jnp.where(lane == h, level_ref[1, h], bias)
    gates = dot_nt(x_ref[...], w_ref[...])
    raw = gates[:, :heads]
    softplus = jnp.maximum(raw, 0.0) + jnp.log1p(jnp.exp(-jnp.abs(raw)))
    logdecay = -rate * softplus
    out_ref[:, heads : 2 * heads] = jax.nn.sigmoid(gates[:, heads:] + bias)
    row = lax.broadcasted_iota(jnp.int32, (span, span), 0)
    col = lax.broadcasted_iota(jnp.int32, (span, span), 1)
    lower = jnp.where(row >= col, 1.0, 0.0).astype(F32)
    for first in range(0, x_ref.shape[0], span):
        piece = logdecay[first : first + span]
        out_ref[first : first + span, :heads] = lax.dot_general(
            lower, piece, (((1,), (0,)), ((), ())), precision=lax.Precision.HIGHEST, preferred_element_type=F32
        )


def solve_lower(systems, rights):
    span = systems[0].shape[0]
    row = lax.broadcasted_iota(jnp.int32, (span, span), 0)
    col = lax.broadcasted_iota(jnp.int32, (span, span), 1)
    apart = row ^ col
    invs = [jnp.where(row == col, 1.0, jnp.where(apart == 1, -s, 0.0)).astype(BF16) for s in systems]
    step = 2
    while step < span:
        keep = (apart >= step) & (apart < 2 * step)
        bands = [jnp.where(keep, s, 0.0).astype(BF16) for s in systems]
        inners = [dot(i, b).astype(BF16) for i, b in zip(invs, bands)]
        invs = [i - dot(n, i).astype(BF16) for n, i in zip(inners, invs)]
        step *= 2
    rounded = [r.astype(BF16) for r in rights]
    firsts = [dot(i, b) + (r - b.astype(F32)) for i, b, r in zip(invs, rounded, rights)]
    residuals = [(r - f) - dot3(s, f) for r, f, s in zip(rights, firsts, systems)]
    return [f + dot(i, r.astype(BF16)) for f, i, r in zip(firsts, invs, residuals)]


def local_kernel(first_head, heads, span, per_step, opening, info, table, x_ref, pool_ref, *refs):
    if opening:
        w_ref, level_ref, own_ref, send_ref, core_ref, query_ref, gate_ref = refs

        @pl.when(pl.program_id(0) == 0)
        def _():
            write_gates(span, heads, x_ref, w_ref, level_ref, gate_ref)

    else:
        gate_ref, own_ref, send_ref, core_ref, query_ref = refs
    members = table.shape[1]
    dims = pool_ref.shape[1]
    lane = lax.broadcasted_iota(jnp.int32, (span, 2 * heads), 1)
    wide = lax.broadcasted_iota(jnp.int32, (span, dims), 1)
    row = lax.broadcasted_iota(jnp.int32, (span, span), 0)
    col = lax.broadcasted_iota(jnp.int32, (span, span), 1)
    eye = (
        lax.broadcasted_iota(jnp.int32, (dims, dims), 0) == lax.broadcasted_iota(jnp.int32, (dims, dims), 1)
    ).astype(F32)
    where = []
    heads_in = []
    for local in range(per_step):
        head = first_head + pl.program_id(0) * per_step + local
        chosen = []
        for kind in range(3):
            target = kind * heads + head
            chosen.append(jnp.concatenate([pool_ref[table[1, j, target]] for j in range(members)], 0))
        for part in range(2):
            seq = info[0] if part == 0 else 1 - info[0]
            where.append((local, part, pl.ds(pl.multiple_of(seq * span, span), span)))
            projected = []
            for kind in range(3):
                target = kind * heads + head
                picked = [
                    x_ref[where[-1][2], pl.ds(pl.multiple_of(table[0, j, target] * dims, dims), dims)]
                    for j in range(members)
                ]
                projected.append(dot(jnp.concatenate(picked, 1), chosen[kind]).astype(BF16))
            heads_in.append((head, projected))
    kept, systems, rights = [], [], []
    for (local, part, rows), (head, (query, key, value)) in zip(where, heads_in):
        key_wide = key.astype(F32)
        gates = gate_ref[rows, :]
        cumulative = jnp.sum(jnp.where(lane == head, gates, 0.0), axis=1, keepdims=True)
        beta = jnp.sum(jnp.where(lane == heads + head, gates, 0.0), axis=1, keepdims=True)
        norm = lax.rsqrt(jnp.sum(key_wide * key_wide, axis=1, keepdims=True) + 1e-06)
        across = jnp.where(wide == 0, cumulative, norm).T
        cumulative_row, norm_row = across[0:1, :], across[1:2, :]
        ratio = jnp.where(row >= col, jnp.exp(jnp.minimum(cumulative - cumulative_row, 0.0)), 0.0) * norm_row
        attend = ratio * dot_nt(query, key)
        systems.append(jnp.where(row > col, ratio * dot_nt(key, key), 0.0) * (beta * norm))
        growth = jnp.exp(cumulative)
        rights.append(jnp.concatenate([(beta * growth * norm) * key_wide, beta * value.astype(F32)], axis=1))
        last = cumulative[span - 1 : span, :]
        kept.append((query, key, attend, growth, norm * jnp.exp(last - cumulative), jnp.exp(last)))
    solutions = solve_lower(systems, rights)
    for (local, part, rows), (query, key, attend, growth, tail, final), solved in zip(where, kept, solutions):
        high, low = halves(solved * tail)
        pushed = dot_tn(key, high) + dot_tn(key, low)
        out = own_ref if part == 0 else send_ref
        out[local, :, :dims] = final * eye - pushed[:, :dims]
        out[local, :, dims:] = pushed[:, dims:]
        seen = dot3(attend, solved)
        lanes = slice(local * dims, (local + 1) * dims)
        query_ref[rows, lanes] = growth * query.astype(F32) - seen[:, :dims]
        core_ref[rows, lanes] = seen[:, dims:]


def local_call(info, table, rows, pool, extra, first_head, count_heads, heads, span):
    count, width = rows.shape
    dims = pool.shape[1]
    opening = isinstance(extra, tuple)
    maps = jax.ShapeDtypeStruct((count_heads, dims, 2 * dims), F32)
    wide = jax.ShapeDtypeStruct((count, count_heads * dims), F32)
    gates = jax.ShapeDtypeStruct((count, 2 * heads), F32)
    map_spec = pl.BlockSpec((PER_STEP, dims, 2 * dims), lambda i, *_: (i, 0, 0))
    row_spec = pl.BlockSpec((count, PER_STEP * dims), lambda i, *_: (0, i))
    if opening:
        more_in = [whole(extra[0].shape), smem()]
        more_out, more_out_specs = (gates,), (whole(gates.shape),)
    else:
        more_in, more_out, more_out_specs, extra = [whole(gates.shape)], (), (), (extra,)
    return pl.pallas_call(
        functools.partial(local_kernel, first_head, heads, span, PER_STEP, opening),
        out_shape=(maps, maps, wide, wide) + more_out,
        grid_spec=pltpu.PrefetchScalarGridSpec(
            num_scalar_prefetch=2,
            grid=(count_heads // PER_STEP,),
            in_specs=[whole(rows.shape), whole(pool.shape)] + more_in,
            out_specs=(map_spec, map_spec, row_spec, row_spec) + more_out_specs,
        ),
        compiler_params=params(28),
        cost_estimate=cost(count_heads * 2 * 2 * span * 256 * 256 * 24, 8 * MIB),
        name="local",
    )(info, table, rows, pool, *extra)


def apply_map(maps, state):
    dims = maps.shape[0]
    return dot3(maps[:, :dims], state)


def combine_kernel(info, own_ref, got_ref, early_ref, both_ref, push_ref):
    later_is_own = info[0] == 1
    for h in range(own_ref.shape[0]):
        own, got = own_ref[h], got_ref[h]
        early = jnp.where(later_is_own, got, own)
        late = jnp.where(later_is_own, own, got)
        dims = own.shape[0]
        early_ref[h] = early
        both = apply_map(late, early)
        push = both[:, dims:] + late[:, dims:]
        both_ref[h, :, :dims] = both[:, :dims]
        both_ref[h, :, dims:] = push
        push_ref[h] = push


def combine_call(info, own, got):
    shape = jax.ShapeDtypeStruct(own.shape, F32)
    push = jax.ShapeDtypeStruct(own.shape[:2] + (own.shape[1],), F32)
    return pl.pallas_call(
        combine_kernel,
        out_shape=(shape, shape, push),
        in_specs=[smem(), vmem(), vmem()],
        compiler_params=params(12),
        cost_estimate=cost(own.shape[0] * 6 * 128 * 128 * 256, own.size * 16),
        name="combine",
    )(info, own, got)


def hop_kernel(level, info, maps_ref, got_ref, state_ref, kept_ref, out_ref):
    arrived = info[2] == level
    for h in range(maps_ref.shape[0]):
        maps = maps_ref[h]
        dims = maps.shape[0]
        state = jnp.where(arrived, got_ref[h], state_ref[h])
        kept_ref[h] = state
        out_ref[h] = apply_map(maps, state) + maps[:, dims:]


def hop_call(level, info, maps, got, state):
    shape = jax.ShapeDtypeStruct(state.shape, F32)
    return pl.pallas_call(
        functools.partial(hop_kernel, level),
        out_shape=(shape, shape),
        in_specs=[smem(), vmem(), vmem(), vmem()],
        compiler_params=params(12),
        cost_estimate=cost(maps.shape[0] * 6 * 128 * 128 * 128, maps.size * 8),
        name="hop",
    )(info, maps, got, state)


def split_kernel(level, info, maps_ref, got_ref, state_ref, keep_ref, send_ref):
    second = info[0] == 1
    arrived = info[2] == level
    for h in range(maps_ref.shape[0]):
        maps = maps_ref[h]
        state = jnp.where(arrived, got_ref[h], state_ref[h])
        dims = maps.shape[0]
        middle = apply_map(maps, state) + maps[:, dims:]
        keep_ref[h] = jnp.where(second, middle, state)
        send_ref[h] = jnp.where(second, state, middle)


def split_call(level, info, maps, got, state):
    shape = jax.ShapeDtypeStruct(state.shape, F32)
    return pl.pallas_call(
        functools.partial(split_kernel, level),
        out_shape=(shape, shape),
        in_specs=[smem(), vmem(), vmem(), vmem()],
        compiler_params=params(12),
        cost_estimate=cost(maps.shape[0] * 6 * 128 * 128 * 128, maps.size * 8),
        name="split",
    )(info, maps, got, state)


def mix_kernel(span, info, core_ref, query_ref, keep_ref, got_ref, back_ref, gain_ref, cot_ref, mixed_ref, wsend_ref, wkeep_ref):
    step = pl.program_id(0)
    half = pl.num_programs(0) // 2
    dims = gain_ref.shape[1]
    tiles = wsend_ref.shape[0] - 1
    each = tiles // half
    gain_part = jnp.zeros((8, dims), F32)
    for part in range(2):
        seq = info[0] if part == 0 else 1 - info[0]
        rows = pl.ds(pl.multiple_of(seq * span, span), span)
        state = (keep_ref if part == 0 else got_ref)[0]
        core = core_ref[rows, :] + dot3(query_ref[rows, :], state)
        normal = core * lax.rsqrt(jnp.mean(core * core, axis=1, keepdims=True) + 1e-05)
        gain_part += jnp.sum((normal * back_ref[rows, :]).reshape(-1, 8, dims), axis=0)
        mixed_ref[rows, :] = (normal * gain_ref[...]).astype(BF16)
    product = dot_tn(mixed_ref[...], cot_ref[...])
    stripe = dims // 8
    pieces = [
        product[:, first : first + 128].reshape(stripe, 8, 128) for first in range(0, product.shape[1], 128)
    ]

    @pl.when(step == 0)
    def _():
        wkeep_ref[tiles] = gain_part

    @pl.when(step > 0)
    def _():
        wkeep_ref[tiles] += gain_part

    @pl.when(step == 2 * half - 1)
    def _():
        wsend_ref[tiles] = wkeep_ref[tiles]

    @pl.when(step < half)
    def _():
        for i, piece in enumerate(pieces):
            wsend_ref[pl.ds(step * each + i * stripe, stripe)] = piece

    @pl.when(step >= half)
    def _():
        for i, piece in enumerate(pieces):
            wkeep_ref[pl.ds((step - half) * each + i * stripe, stripe)] = piece


def mix_call(info, first_head, core, query, keep, got, back, gain, cot, span):
    count, width = cot.shape
    heads_here = keep.shape[0]
    dims = gain.shape[1]
    half = heads_here // 2

    def order(i, info):
        first = jnp.where(i < half, 1 - info[1], info[1])
        return first * half + lax.rem(i, half)

    row_spec = pl.BlockSpec((count, dims), lambda i, info: (0, order(i, info)))
    back_spec = pl.BlockSpec((count, dims), lambda i, info: (0, first_head + order(i, info)))
    state_spec = pl.BlockSpec((1, dims, dims), lambda i, info: (order(i, info), 0, 0))
    weight = jax.ShapeDtypeStruct((half * dims * width // 1024 + 1, 8, 128), F32)
    return pl.pallas_call(
        functools.partial(mix_kernel, span),
        out_shape=(jax.ShapeDtypeStruct((count, heads_here * dims), BF16), weight, weight),
        grid_spec=pltpu.PrefetchScalarGridSpec(
            num_scalar_prefetch=1,
            grid=(heads_here,),
            in_specs=[row_spec, row_spec, state_spec, state_spec, back_spec, whole(gain.shape), whole(cot.shape)],
            out_specs=(row_spec, whole(weight.shape), whole(weight.shape)),
        ),
        compiler_params=params(16),
        cost_estimate=cost(heads_here * 2 * 512 * 1024 * 128, 3 * MIB),
        name="mix",
    )(info, core, query, keep, got, back, gain, cot)


def back_kernel(cot_ref, weight_ref, out_ref):
    out_ref[...] = dot_nt(cot_ref[...], weight_ref[...])


def back_call(cot, weight):
    count, width = cot.shape
    row_spec = pl.BlockSpec((128, width), lambda i: (i, 0))
    return pl.pallas_call(
        back_kernel,
        out_shape=jax.ShapeDtypeStruct((count, width), F32),
        grid=(count // 128,),
        in_specs=[row_spec, whole(weight.shape)],
        out_specs=row_spec,
        compiler_params=params(12),
        cost_estimate=cost(2 * count * width * width, 5 * MIB),
        name="back",
    )(cot, weight)


def finish_kernel(groups, *refs):
    weight_ref, out_ref = refs[groups:]
    stacked = jnp.concatenate([ref[...] for ref in refs[:groups]], axis=1)
    out_ref[...] = dot(stacked, weight_ref[...]).astype(BF16)


def finish_call(mixed, weight):
    count = mixed[0].shape[0]
    width = weight.shape[1]
    part_spec = pl.BlockSpec((128, mixed[0].shape[1]), lambda i: (i, 0))
    row_spec = pl.BlockSpec((128, width), lambda i: (i, 0))
    return pl.pallas_call(
        functools.partial(finish_kernel, len(mixed)),
        out_shape=jax.ShapeDtypeStruct((count, width), BF16),
        grid=(count // 128,),
        in_specs=[part_spec] * len(mixed) + [whole(weight.shape)],
        out_specs=row_spec,
        compiler_params=params(12),
        cost_estimate=cost(2 * count * width * width, 4 * MIB),
        name="finish",
    )(*mixed, weight)


def fold_kernel(parts, terms, where, flips, info, *refs):
    ins, outs = refs[: parts * terms], refs[parts * terms :]
    size = ins[0].shape[0] - 1
    share = outs[0].shape[0] - 1
    last = sum(ref[size] for ref in ins)
    for flip, out in zip(flips, outs):
        first = (info[where] ^ flip) * share
        if parts == 1:
            out[:share] = sum(ref[pl.ds(first, share)] for ref in ins)
        else:
            for part in range(parts):

                @pl.when((first >= part * size) & (first < (part + 1) * size))
                def _(part=part, out=out, first=first):
                    out[:share] = sum(ref[pl.ds(first - part * size, share)] for ref in ins[part * terms : (part + 1) * terms])

        out[share] = last


def fold_call(info, where, flips, arrays, parts):
    terms = len(arrays) // parts
    size = arrays[0].shape[0] - 1
    share = size * parts // len(flips)
    shape = jax.ShapeDtypeStruct((share + 1, 8, 128), F32)
    return pl.pallas_call(
        functools.partial(fold_kernel, parts, terms, where, flips),
        out_shape=[shape] * len(flips),
        in_specs=[smem()] + [vmem()] * len(arrays),
        compiler_params=params(12),
        cost_estimate=cost(size * 1024 * len(arrays), size * 4096 * (len(arrays) + 1)),
        name="fold",
    )(info, *arrays)


def total_kernel(*refs):
    ins, (piece_ref, last_ref) = refs[:-2], refs[-2:]
    size = piece_ref.shape[0]
    piece_ref[...] = sum(ref[:size] for ref in ins)
    last_ref[...] = sum(ref[size] for ref in ins)


def total_call(arrays):
    size = arrays[0].shape[0] - 1
    return pl.pallas_call(
        total_kernel,
        out_shape=(jax.ShapeDtypeStruct((size, 8, 128), F32), jax.ShapeDtypeStruct((8, 128), F32)),
        in_specs=[vmem()] * len(arrays),
        out_specs=(vmem(), vmem()),
        compiler_params=params(12),
        cost_estimate=cost(size * 4096, size * 4096 * 5),
        name="total",
    )(*arrays)


def lay_kernel(where, flips, info, *refs):
    out = refs[-1]
    share = refs[0].shape[0]
    for flip, ref in zip(flips, refs):
        out[pl.ds((info[where] ^ flip) * share, share)] = ref[...]


def lay_call(info, where, flips, arrays):
    share = arrays[0].shape[0]
    return pl.pallas_call(
        functools.partial(lay_kernel, where, flips),
        out_shape=jax.ShapeDtypeStruct((share * len(flips), 8, 128), F32),
        in_specs=[smem()] + [vmem()] * len(arrays),
        compiler_params=params(12),
        cost_estimate=cost(0, share * len(flips) * 8192),
        name="lay",
    )(info, *arrays)


def join_kernel(scale, stripe, info, *refs):
    sums = (len(refs) - 2) // 3
    lasts, (out_ref, gain_ref) = refs[2 * sums : 3 * sums], refs[-2:]
    columns = out_ref.shape[1] // 128
    dims = stripe * 8
    blocks = refs[0].shape[0] // (columns * stripe)
    for g in range(sums):
        for part, ref in enumerate(refs[2 * g : 2 * g + 2]):
            side = info[1] if part == 0 else 1 - info[1]
            for block in range(blocks):
                head = (g * blocks + block) * 2 + side
                for col in range(columns):
                    first = (block * columns + col) * stripe
                    values = ref[first : first + stripe].reshape(dims, 128) * scale
                    out_ref[pl.ds(pl.multiple_of(head * dims, dims), dims), col * 128 : (col + 1) * 128] = values.astype(BF16)
    gain_ref[...] = jnp.sum(sum(ref[...] for ref in lasts), axis=0, keepdims=True) * scale


def join_call(info, parts, lasts, scale, dims, width):
    total = sum(p.shape[0] for p in parts) * 1024 // width
    return pl.pallas_call(
        functools.partial(join_kernel, scale, dims // 8),
        out_shape=(jax.ShapeDtypeStruct((total, width), BF16), jax.ShapeDtypeStruct((1, 128), F32)),
        in_specs=[smem()] + [vmem()] * (len(parts) + len(lasts)),
        out_specs=(vmem(), vmem()),
        compiler_params=params(16),
        name="join",
    )(info, *parts, *lasts)


def shards(mesh, features, weight_pool, pattern_in, pattern_pool, gate_weight, decay_rate, beta_bias, norm_gain, out_weight, cotangent):
    n_shot, n_tm = mesh.shape["shot"], mesh.shape["tm"]
    n_x, n_z = n_shot // CORES, n_tm // PAIR
    seqs, span, width = features.shape
    heads = decay_rate.shape[0]
    dims = weight_pool.shape[1]
    count = seqs * span
    both = ("shot", "tm")
    shot, tm = lax.axis_index("shot"), lax.axis_index("tm")
    x, core, z, y = shot // CORES, shot % CORES, tm // PAIR, tm % PAIR

    def place(xi, ci, zi, yi):
        return (xi * CORES + ci) * n_tm + zi * PAIR + yi

    def moved(array, shift):
        dx, dc, dz, dy = shift
        route = []
        for xi in range(n_x):
            for ci in range(CORES):
                for zi in range(n_z):
                    for yi in range(PAIR):
                        route.append((place(xi, ci, zi, yi), place(xi ^ dx, ci ^ dc, zi ^ dz, yi ^ dy)))
        return lax.ppermute(array, both, route)

    def lifted(array, level):
        ends = ((level, level + 1), (level + 1, level))
        route = [(a * PAIR + yi, b * PAIR + yi) for a, b in ends for yi in range(PAIR)]
        return lax.ppermute(array, "tm", route)

    plane = [(dx, dy) for dx in range(n_x) for dy in range(PAIR)]
    info = jnp.stack([y, core, z, x * PAIR + y]).astype(jnp.int32)
    table = jnp.stack([pattern_in.T, pattern_pool.T])
    levels = jnp.stack([decay_rate, beta_bias])
    rows = features.reshape(count, width)
    cot = cotangent.reshape(count, width)
    gain = norm_gain.reshape(1, dims)
    each = heads // GROUPS
    per_sum = GROUPS // SUMS

    gates = None
    locals_, maps = [], []
    for g in range(GROUPS):
        told = info
        if g >= AHEAD:
            told, maps[g - AHEAD] = lax.optimization_barrier((info, maps[g - AHEAD]))
        extra = (gate_weight.T, levels) if g == 0 else gates
        own, send, *rest = local_call(told, table, rows, weight_pool, extra, g * each, each, heads, span)
        if g == 0:
            gates = rest.pop()
        locals_.append(rest)
        maps.append(list(combine_call(info, own, moved(send, (0, 0, 0, 1)))))
    back = back_call(cot, out_weight)
    states = [jnp.zeros((each, dims, dims), F32)] * GROUPS
    sends = [m[2] for m in maps]
    for level in range(1, n_z):
        gots = [lifted(send, level - 1) for send in sends]
        if level == 1:
            gots[0], back = lax.optimization_barrier((gots[0], back))
        if level == n_z - 1:
            break
        for g in range(GROUPS):
            states[g], sends[g] = hop_call(level, info, maps[g][1], gots[g], states[g])
    mixed, halves_ = [], []
    for g in range(GROUPS):
        keep, send = split_call(n_z - 1, info, maps[g][0], gots[g], states[g])
        got = moved(send, (0, 0, 0, 1))
        flat, w_send, w_keep = mix_call(info, g * each, *locals_[g], keep, got, back, gain, cot, span)
        mixed.append(flat)
        halves_.append([w_keep, moved(w_send, (0, 1, 0, 0))])
    output = finish_call(mixed, out_weight)
    scale = 1.0 / math.sqrt(count * n_shot * n_tm)

    flat_plane = tuple(dx * PAIR + dy for dx, dy in plane)
    flat_z = tuple(range(n_z))
    sums = range(SUMS)
    spread = []
    for g in sums:
        arrays = [a for pair in halves_[g * per_sum : (g + 1) * per_sum] for a in pair]
        spread.append(list(fold_call(info, 3, flat_plane, arrays, per_sum)))
    spread[-1][0], output = lax.optimization_barrier((spread[-1][0], output))
    met = [[p[0]] + [moved(a, (dx, 0, 0, dy)) for a, (dx, dy) in zip(p[1:], plane[1:])] for p in spread]
    spread = [fold_call(info, 2, flat_z, m, 1) for m in met]
    met = [[p[0]] + [moved(a, (0, 0, dz, 0)) for a, dz in zip(p[1:], flat_z[1:])] for p in spread]
    totals = [total_call(m) for m in met]
    along = []
    for piece, _ in totals:
        along.append(lay_call(info, 2, flat_z, [piece] + [moved(piece, (0, 0, dz, 0)) for dz in flat_z[1:]]))
    parts = []
    for piece in along:
        laid = lay_call(info, 3, flat_plane, [piece] + [moved(piece, (dx, 0, 0, dy)) for dx, dy in plane[1:]])
        parts += [laid, moved(laid, (0, 1, 0, 0))]
    weight_grad, gain_grad = join_call(info, parts, [t[1] for t in totals], scale, dims, width)
    return (output.reshape(seqs, span, width), weight_grad, gain_grad.reshape(dims))


def solution(mesh):
    placed = (P("shot", "tm", None), P(), P(), P(), P(), P(), P(), P(), P(), P("shot", "tm", None))
    return jax.shard_map(
        functools.partial(shards, mesh),
        mesh=mesh,
        in_specs=placed,
        out_specs=(P("shot", "tm", None), P(), P()),
        check_vma=False,
    )
```

```python
import functools
import math

import jax
import jax.numpy as jnp
from jax import lax
from jax.experimental import pallas as pl
from jax.experimental.pallas import tpu as pltpu
from jax.sharding import PartitionSpec as P

GROUPS = 2
SUMS = 2
CORES = 2
PAIR = 2
PER_STEP = 2
AHEAD = 3
F32 = jnp.float32
BF16 = jnp.bfloat16
MIB = 1024 * 1024


def dot(a, b):
    return lax.dot_general(a, b, (((1,), (0,)), ((), ())), preferred_element_type=F32)


def dot_nt(a, b):
    return lax.dot_general(a, b, (((1,), (1,)), ((), ())), preferred_element_type=F32)


def dot_tn(a, b):
    return lax.dot_general(a, b, (((0,), (0,)), ((), ())), preferred_element_type=F32)


def halves(a):
    high = a.astype(BF16)
    return high, (a - high.astype(F32)).astype(BF16)


def dot3(a, b):
    ah, al = halves(a)
    bh, bl = halves(b)
    return dot(ah, bh) + (dot(ah, bl) + dot(al, bh))


def params(mib):
    return pltpu.CompilerParams(vmem_limit_bytes=mib * MIB)


def smem():
    return pl.BlockSpec(memory_space=pltpu.SMEM)


def vmem():
    return pl.BlockSpec(memory_space=pltpu.VMEM)


def whole(shape):
    return pl.BlockSpec(shape, lambda *_: (0,) * len(shape))


def cost(flops, size):
    return pl.CostEstimate(flops=flops, bytes_accessed=size, transcendentals=0)


def write_gates(span, heads, x_ref, w_ref, level_ref, out_ref):
    lane = lax.broadcasted_iota(jnp.int32, (1, heads), 1)
    rate = jnp.zeros((1, heads), F32)
    bias = jnp.zeros((1, heads), F32)
    for h in range(heads):
        rate = jnp.where(lane == h, level_ref[0, h], rate)
        bias = jnp.where(lane == h, level_ref[1, h], bias)
    gates = dot_nt(x_ref[...], w_ref[...])
    raw = gates[:, :heads]
    softplus = jnp.maximum(raw, 0.0) + jnp.log1p(jnp.exp(-jnp.abs(raw)))
    logdecay = -rate * softplus
    out_ref[:, heads : 2 * heads] = jax.nn.sigmoid(gates[:, heads:] + bias)
    row = lax.broadcasted_iota(jnp.int32, (span, span), 0)
    col = lax.broadcasted_iota(jnp.int32, (span, span), 1)
    lower = jnp.where(row >= col, 1.0, 0.0).astype(F32)
    for first in range(0, x_ref.shape[0], span):
        piece = logdecay[first : first + span]
        out_ref[first : first + span, :heads] = lax.dot_general(
            lower, piece, (((1,), (0,)), ((), ())), precision=lax.Precision.HIGHEST, preferred_element_type=F32
        )


def solve_lower(systems, rights):
    span = systems[0].shape[0]
    row = lax.broadcasted_iota(jnp.int32, (span, span), 0)
    col = lax.broadcasted_iota(jnp.int32, (span, span), 1)
    apart = row ^ col
    invs = [jnp.where(row == col, 1.0, jnp.where(apart == 1, -s, 0.0)).astype(BF16) for s in systems]
    step = 2
    while step < span:
        keep = (apart >= step) & (apart < 2 * step)
        bands = [jnp.where(keep, s, 0.0).astype(BF16) for s in systems]
        inners = [dot(i, b).astype(BF16) for i, b in zip(invs, bands)]
        invs = [i - dot(n, i).astype(BF16) for n, i in zip(inners, invs)]
        step *= 2
    rounded = [r.astype(BF16) for r in rights]
    firsts = [dot(i, b) + (r - b.astype(F32)) for i, b, r in zip(invs, rounded, rights)]
    residuals = [(r - f) - dot3(s, f) for r, f, s in zip(rights, firsts, systems)]
    return [f + dot(i, r.astype(BF16)) for f, i, r in zip(firsts, invs, residuals)]


def local_kernel(first_head, heads, span, per_step, opening, info, table, x_ref, pool_ref, *refs):
    if opening:
        w_ref, level_ref, own_ref, send_ref, core_ref, query_ref, gate_ref = refs

        @pl.when(pl.program_id(0) == 0)
        def _():
            write_gates(span, heads, x_ref, w_ref, level_ref, gate_ref)

    else:
        gate_ref, own_ref, send_ref, core_ref, query_ref = refs
    members = table.shape[1]
    dims = pool_ref.shape[1]
    lane = lax.broadcasted_iota(jnp.int32, (span, 2 * heads), 1)
    wide = lax.broadcasted_iota(jnp.int32, (span, dims), 1)
    row = lax.broadcasted_iota(jnp.int32, (span, span), 0)
    col = lax.broadcasted_iota(jnp.int32, (span, span), 1)
    eye = (
        lax.broadcasted_iota(jnp.int32, (dims, dims), 0) == lax.broadcasted_iota(jnp.int32, (dims, dims), 1)
    ).astype(F32)
    where = []
    heads_in = []
    for local in range(per_step):
        head = first_head + pl.program_id(0) * per_step + local
        chosen = []
        for kind in range(3):
            target = kind * heads + head
            chosen.append(jnp.concatenate([pool_ref[table[1, j, target]] for j in range(members)], 0))
        for part in range(2):
            seq = info[0] if part == 0 else 1 - info[0]
            where.append((local, part, pl.ds(pl.multiple_of(seq * span, span), span)))
            projected = []
            for kind in range(3):
                target = kind * heads + head
                picked = [
                    x_ref[where[-1][2], pl.ds(pl.multiple_of(table[0, j, target] * dims, dims), dims)]
                    for j in range(members)
                ]
                projected.append(dot(jnp.concatenate(picked, 1), chosen[kind]).astype(BF16))
            heads_in.append((head, projected))
    kept, systems, rights = [], [], []
    for (local, part, rows), (head, (query, key, value)) in zip(where, heads_in):
        key_wide = key.astype(F32)
        gates = gate_ref[rows, :]
        cumulative = jnp.sum(jnp.where(lane == head, gates, 0.0), axis=1, keepdims=True)
        beta = jnp.sum(jnp.where(lane == heads + head, gates, 0.0), axis=1, keepdims=True)
        norm = lax.rsqrt(jnp.sum(key_wide * key_wide, axis=1, keepdims=True) + 1e-06)
        across = jnp.where(wide == 0, cumulative, norm).T
        cumulative_row, norm_row = across[0:1, :], across[1:2, :]
        ratio = jnp.where(row >= col, jnp.exp(jnp.minimum(cumulative - cumulative_row, 0.0)), 0.0) * norm_row
        attend = ratio * dot_nt(query, key)
        systems.append(jnp.where(row > col, ratio * dot_nt(key, key), 0.0) * (beta * norm))
        growth = jnp.exp(cumulative)
        rights.append(jnp.concatenate([(beta * growth * norm) * key_wide, beta * value.astype(F32)], axis=1))
        last = cumulative[span - 1 : span, :]
        kept.append((query, key, attend, growth, norm * jnp.exp(last - cumulative), jnp.exp(last)))
    solutions = solve_lower(systems, rights)
    for (local, part, rows), (query, key, attend, growth, tail, final), solved in zip(where, kept, solutions):
        high, low = halves(solved * tail)
        pushed = dot_tn(key, high) + dot_tn(key, low)
        out = own_ref if part == 0 else send_ref
        out[local, :, :dims] = final * eye - pushed[:, :dims]
        out[local, :, dims:] = pushed[:, dims:]
        seen = dot3(attend, solved)
        lanes = slice(local * dims, (local + 1) * dims)
        query_ref[rows, lanes] = growth * query.astype(F32) - seen[:, :dims]
        core_ref[rows, lanes] = seen[:, dims:]


def local_call(info, table, rows, pool, extra, first_head, count_heads, heads, span):
    count, width = rows.shape
    dims = pool.shape[1]
    opening = isinstance(extra, tuple)
    maps = jax.ShapeDtypeStruct((count_heads, dims, 2 * dims), F32)
    wide = jax.ShapeDtypeStruct((count, count_heads * dims), F32)
    gates = jax.ShapeDtypeStruct((count, 2 * heads), F32)
    map_spec = pl.BlockSpec((PER_STEP, dims, 2 * dims), lambda i, *_: (i, 0, 0))
    row_spec = pl.BlockSpec((count, PER_STEP * dims), lambda i, *_: (0, i))
    if opening:
        more_in = [whole(extra[0].shape), smem()]
        more_out, more_out_specs = (gates,), (whole(gates.shape),)
    else:
        more_in, more_out, more_out_specs, extra = [whole(gates.shape)], (), (), (extra,)
    return pl.pallas_call(
        functools.partial(local_kernel, first_head, heads, span, PER_STEP, opening),
        out_shape=(maps, maps, wide, wide) + more_out,
        grid_spec=pltpu.PrefetchScalarGridSpec(
            num_scalar_prefetch=2,
            grid=(count_heads // PER_STEP,),
            in_specs=[whole(rows.shape), whole(pool.shape)] + more_in,
            out_specs=(map_spec, map_spec, row_spec, row_spec) + more_out_specs,
        ),
        compiler_params=params(28),
        cost_estimate=cost(count_heads * 2 * 2 * span * 256 * 256 * 24, 8 * MIB),
        name="local",
    )(info, table, rows, pool, *extra)


def apply_map(maps, state):
    dims = maps.shape[0]
    return dot3(maps[:, :dims], state)


def combine_kernel(info, own_ref, got_ref, early_ref, both_ref, push_ref):
    later_is_own = info[0] == 1
    for h in range(own_ref.shape[0]):
        own, got = own_ref[h], got_ref[h]
        early = jnp.where(later_is_own, got, own)
        late = jnp.where(later_is_own, own, got)
        dims = own.shape[0]
        early_ref[h] = early
        both = apply_map(late, early)
        push = both[:, dims:] + late[:, dims:]
        both_ref[h, :, :dims] = both[:, :dims]
        both_ref[h, :, dims:] = push
        push_ref[h] = push


def combine_call(info, own, got):
    shape = jax.ShapeDtypeStruct(own.shape, F32)
    push = jax.ShapeDtypeStruct(own.shape[:2] + (own.shape[1],), F32)
    return pl.pallas_call(
        combine_kernel,
        out_shape=(shape, shape, push),
        in_specs=[smem(), vmem(), vmem()],
        compiler_params=params(12),
        cost_estimate=cost(own.shape[0] * 6 * 128 * 128 * 256, own.size * 16),
        name="combine",
    )(info, own, got)


def hop_kernel(level, info, maps_ref, got_ref, state_ref, kept_ref, out_ref):
    arrived = info[2] == level
    for h in range(maps_ref.shape[0]):
        maps = maps_ref[h]
        dims = maps.shape[0]
        state = jnp.where(arrived, got_ref[h], state_ref[h])
        kept_ref[h] = state
        out_ref[h] = apply_map(maps, state) + maps[:, dims:]


def hop_call(level, info, maps, got, state):
    shape = jax.ShapeDtypeStruct(state.shape, F32)
    return pl.pallas_call(
        functools.partial(hop_kernel, level),
        out_shape=(shape, shape),
        in_specs=[smem(), vmem(), vmem(), vmem()],
        compiler_params=params(12),
        cost_estimate=cost(maps.shape[0] * 6 * 128 * 128 * 128, maps.size * 8),
        name="hop",
    )(info, maps, got, state)


def split_kernel(level, info, maps_ref, got_ref, state_ref, keep_ref, send_ref):
    second = info[0] == 1
    arrived = info[2] == level
    for h in range(maps_ref.shape[0]):
        maps = maps_ref[h]
        state = jnp.where(arrived, got_ref[h], state_ref[h])
        dims = maps.shape[0]
        middle = apply_map(maps, state) + maps[:, dims:]
        keep_ref[h] = jnp.where(second, middle, state)
        send_ref[h] = jnp.where(second, state, middle)


def split_call(level, info, maps, got, state):
    shape = jax.ShapeDtypeStruct(state.shape, F32)
    return pl.pallas_call(
        functools.partial(split_kernel, level),
        out_shape=(shape, shape),
        in_specs=[smem(), vmem(), vmem(), vmem()],
        compiler_params=params(12),
        cost_estimate=cost(maps.shape[0] * 6 * 128 * 128 * 128, maps.size * 8),
        name="split",
    )(info, maps, got, state)


def mix_kernel(span, info, core_ref, query_ref, keep_ref, got_ref, back_ref, gain_ref, cot_ref, mixed_ref, wsend_ref, wkeep_ref):
    step = pl.program_id(0)
    half = pl.num_programs(0) // 2
    dims = gain_ref.shape[1]
    tiles = wsend_ref.shape[0] - 1
    each = tiles // half
    gain_part = jnp.zeros((8, dims), F32)
    for part in range(2):
        seq = info[0] if part == 0 else 1 - info[0]
        rows = pl.ds(pl.multiple_of(seq * span, span), span)
        state = (keep_ref if part == 0 else got_ref)[0]
        core = core_ref[rows, :] + dot3(query_ref[rows, :], state)
        normal = core * lax.rsqrt(jnp.mean(core * core, axis=1, keepdims=True) + 1e-05)
        gain_part += jnp.sum((normal * back_ref[rows, :]).reshape(-1, 8, dims), axis=0)
        mixed_ref[rows, :] = (normal * gain_ref[...]).astype(BF16)
    product = dot_tn(mixed_ref[...], cot_ref[...])
    stripe = dims // 8
    pieces = [
        product[:, first : first + 128].reshape(stripe, 8, 128) for first in range(0, product.shape[1], 128)
    ]

    @pl.when(step == 0)
    def _():
        wkeep_ref[tiles] = gain_part

    @pl.when(step > 0)
    def _():
        wkeep_ref[tiles] += gain_part

    @pl.when(step == 2 * half - 1)
    def _():
        wsend_ref[tiles] = wkeep_ref[tiles]

    @pl.when(step < half)
    def _():
        for i, piece in enumerate(pieces):
            wsend_ref[pl.ds(step * each + i * stripe, stripe)] = piece

    @pl.when(step >= half)
    def _():
        for i, piece in enumerate(pieces):
            wkeep_ref[pl.ds((step - half) * each + i * stripe, stripe)] = piece


def mix_call(info, first_head, core, query, keep, got, back, gain, cot, span):
    count, width = cot.shape
    heads_here = keep.shape[0]
    dims = gain.shape[1]
    half = heads_here // 2

    def order(i, info):
        first = jnp.where(i < half, 1 - info[1], info[1])
        return first * half + lax.rem(i, half)

    row_spec = pl.BlockSpec((count, dims), lambda i, info: (0, order(i, info)))
    back_spec = pl.BlockSpec((count, dims), lambda i, info: (0, first_head + order(i, info)))
    state_spec = pl.BlockSpec((1, dims, dims), lambda i, info: (order(i, info), 0, 0))
    weight = jax.ShapeDtypeStruct((half * dims * width // 1024 + 1, 8, 128), F32)
    return pl.pallas_call(
        functools.partial(mix_kernel, span),
        out_shape=(jax.ShapeDtypeStruct((count, heads_here * dims), BF16), weight, weight),
        grid_spec=pltpu.PrefetchScalarGridSpec(
            num_scalar_prefetch=1,
            grid=(heads_here,),
            in_specs=[row_spec, row_spec, state_spec, state_spec, back_spec, whole(gain.shape), whole(cot.shape)],
            out_specs=(row_spec, whole(weight.shape), whole(weight.shape)),
        ),
        compiler_params=params(16),
        cost_estimate=cost(heads_here * 2 * 512 * 1024 * 128, 3 * MIB),
        name="mix",
    )(info, core, query, keep, got, back, gain, cot)


def back_kernel(cot_ref, weight_ref, out_ref):
    out_ref[...] = dot_nt(cot_ref[...], weight_ref[...])


def back_call(cot, weight):
    count, width = cot.shape
    row_spec = pl.BlockSpec((128, width), lambda i: (i, 0))
    return pl.pallas_call(
        back_kernel,
        out_shape=jax.ShapeDtypeStruct((count, width), F32),
        grid=(count // 128,),
        in_specs=[row_spec, whole(weight.shape)],
        out_specs=row_spec,
        compiler_params=params(12),
        cost_estimate=cost(2 * count * width * width, 5 * MIB),
        name="back",
    )(cot, weight)


def finish_kernel(groups, *refs):
    weight_ref, out_ref = refs[groups:]
    stacked = jnp.concatenate([ref[...] for ref in refs[:groups]], axis=1)
    out_ref[...] = dot(stacked, weight_ref[...]).astype(BF16)


def finish_call(mixed, weight):
    count = mixed[0].shape[0]
    width = weight.shape[1]
    part_spec = pl.BlockSpec((128, mixed[0].shape[1]), lambda i: (i, 0))
    row_spec = pl.BlockSpec((128, width), lambda i: (i, 0))
    return pl.pallas_call(
        functools.partial(finish_kernel, len(mixed)),
        out_shape=jax.ShapeDtypeStruct((count, width), BF16),
        grid=(count // 128,),
        in_specs=[part_spec] * len(mixed) + [whole(weight.shape)],
        out_specs=row_spec,
        compiler_params=params(12),
        cost_estimate=cost(2 * count * width * width, 4 * MIB),
        name="finish",
    )(*mixed, weight)


def fold_kernel(parts, terms, where, flips, info, *refs):
    ins, outs = refs[: parts * terms], refs[parts * terms :]
    size = ins[0].shape[0] - 1
    share = outs[0].shape[0] - 1
    last = sum(ref[size] for ref in ins)
    for flip, out in zip(flips, outs):
        first = (info[where] ^ flip) * share
        if parts == 1:
            out[:share] = sum(ref[pl.ds(first, share)] for ref in ins)
        else:
            for part in range(parts):

                @pl.when((first >= part * size) & (first < (part + 1) * size))
                def _(part=part, out=out, first=first):
                    out[:share] = sum(ref[pl.ds(first - part * size, share)] for ref in ins[part * terms : (part + 1) * terms])

        out[share] = last


def fold_call(info, where, flips, arrays, parts):
    terms = len(arrays) // parts
    size = arrays[0].shape[0] - 1
    share = size * parts // len(flips)
    shape = jax.ShapeDtypeStruct((share + 1, 8, 128), F32)
    return pl.pallas_call(
        functools.partial(fold_kernel, parts, terms, where, flips),
        out_shape=[shape] * len(flips),
        in_specs=[smem()] + [vmem()] * len(arrays),
        compiler_params=params(12),
        cost_estimate=cost(size * 1024 * len(arrays), size * 4096 * (len(arrays) + 1)),
        name="fold",
    )(info, *arrays)


def total_kernel(*refs):
    ins, (piece_ref, last_ref) = refs[:-2], refs[-2:]
    size = piece_ref.shape[0]
    piece_ref[...] = sum(ref[:size] for ref in ins)
    last_ref[...] = sum(ref[size] for ref in ins)


def total_call(arrays):
    size = arrays[0].shape[0] - 1
    return pl.pallas_call(
        total_kernel,
        out_shape=(jax.ShapeDtypeStruct((size, 8, 128), F32), jax.ShapeDtypeStruct((8, 128), F32)),
        in_specs=[vmem()] * len(arrays),
        out_specs=(vmem(), vmem()),
        compiler_params=params(12),
        cost_estimate=cost(size * 4096, size * 4096 * 5),
        name="total",
    )(*arrays)


def lay_kernel(where, flips, info, *refs):
    out = refs[-1]
    share = refs[0].shape[0]
    for flip, ref in zip(flips, refs):
        out[pl.ds((info[where] ^ flip) * share, share)] = ref[...]


def lay_call(info, where, flips, arrays):
    share = arrays[0].shape[0]
    return pl.pallas_call(
        functools.partial(lay_kernel, where, flips),
        out_shape=jax.ShapeDtypeStruct((share * len(flips), 8, 128), F32),
        in_specs=[smem()] + [vmem()] * len(arrays),
        compiler_params=params(12),
        cost_estimate=cost(0, share * len(flips) * 8192),
        name="lay",
    )(info, *arrays)


def join_kernel(scale, stripe, half, info, *refs):
    sums = (len(refs) - 2) // 3
    lasts, (out_ref, gain_ref) = refs[2 * sums : 3 * sums], refs[-2:]
    columns = out_ref.shape[1] // 128
    dims = stripe * 8
    blocks = refs[0].shape[0] // (columns * stripe)
    for g in range(sums):
        for part, ref in enumerate(refs[2 * g : 2 * g + 2]):
            side = info[1] if part == 0 else 1 - info[1]
            for block in range(blocks):
                index = g * blocks + block
                head = index // half * 2 * half + side * half + index % half
                for col in range(columns):
                    first = (block * columns + col) * stripe
                    values = ref[first : first + stripe].reshape(dims, 128) * scale
                    out_ref[pl.ds(pl.multiple_of(head * dims, dims), dims), col * 128 : (col + 1) * 128] = values.astype(BF16)
    gain_ref[...] = jnp.sum(sum(ref[...] for ref in lasts), axis=0, keepdims=True) * scale


def join_call(info, parts, lasts, scale, dims, width, half):
    total = sum(p.shape[0] for p in parts) * 1024 // width
    return pl.pallas_call(
        functools.partial(join_kernel, scale, dims // 8, half),
        out_shape=(jax.ShapeDtypeStruct((total, width), BF16), jax.ShapeDtypeStruct((1, 128), F32)),
        in_specs=[smem()] + [vmem()] * (len(parts) + len(lasts)),
        out_specs=(vmem(), vmem()),
        compiler_params=params(16),
        name="join",
    )(info, *parts, *lasts)


def shards(mesh, features, weight_pool, pattern_in, pattern_pool, gate_weight, decay_rate, beta_bias, norm_gain, out_weight, cotangent):
    n_shot, n_tm = mesh.shape["shot"], mesh.shape["tm"]
    n_x, n_z = n_shot // CORES, n_tm // PAIR
    seqs, span, width = features.shape
    heads = decay_rate.shape[0]
    dims = weight_pool.shape[1]
    count = seqs * span
    both = ("shot", "tm")
    shot, tm = lax.axis_index("shot"), lax.axis_index("tm")
    x, core, z, y = shot // CORES, shot % CORES, tm // PAIR, tm % PAIR

    def place(xi, ci, zi, yi):
        return (xi * CORES + ci) * n_tm + zi * PAIR + yi

    def moved(array, shift):
        dx, dc, dz, dy = shift
        route = []
        for xi in range(n_x):
            for ci in range(CORES):
                for zi in range(n_z):
                    for yi in range(PAIR):
                        route.append((place(xi, ci, zi, yi), place(xi ^ dx, ci ^ dc, zi ^ dz, yi ^ dy)))
        return lax.ppermute(array, both, route)

    def lifted(array, level):
        ends = ((level, level + 1), (level + 1, level))
        route = [(a * PAIR + yi, b * PAIR + yi) for a, b in ends for yi in range(PAIR)]
        return lax.ppermute(array, "tm", route)

    plane = [(dx, dy) for dx in range(n_x) for dy in range(PAIR)]
    n_plane = len(plane)
    info = jnp.stack([y, core, z, x * PAIR + y]).astype(jnp.int32)
    table = jnp.stack([pattern_in.T, pattern_pool.T])
    levels = jnp.stack([decay_rate, beta_bias])
    rows = features.reshape(count, width)
    cot = cotangent.reshape(count, width)
    gain = norm_gain.reshape(1, dims)
    each = heads // GROUPS
    per_sum = GROUPS // SUMS

    gates = None
    locals_, maps = [], []
    for g in range(GROUPS):
        told = info
        if g >= AHEAD:
            told, maps[g - AHEAD] = lax.optimization_barrier((info, maps[g - AHEAD]))
        extra = (gate_weight.T, levels) if g == 0 else gates
        own, send, *rest = local_call(told, table, rows, weight_pool, extra, g * each, each, heads, span)
        if g == 0:
            gates = rest.pop()
        locals_.append(rest)
        maps.append(list(combine_call(info, own, moved(send, (0, 0, 0, 1)))))
    back = back_call(cot, out_weight)
    states = [jnp.zeros((each, dims, dims), F32)] * GROUPS
    sends = [m[2] for m in maps]
    for level in range(1, n_z):
        gots = [lifted(send, level - 1) for send in sends]
        if level == 1:
            gots[0], back = lax.optimization_barrier((gots[0], back))
        if level == n_z - 1:
            break
        for g in range(GROUPS):
            states[g], sends[g] = hop_call(level, info, maps[g][1], gots[g], states[g])
    mixed, halves_ = [], []
    for g in range(GROUPS):
        keep, send = split_call(n_z - 1, info, maps[g][0], gots[g], states[g])
        got = moved(send, (0, 0, 0, 1))
        flat, w_send, w_keep = mix_call(info, g * each, *locals_[g], keep, got, back, gain, cot, span)
        mixed.append(flat)
        halves_.append([w_keep, moved(w_send, (0, 1, 0, 0))])
    output = finish_call(mixed, out_weight)
    scale = 1.0 / math.sqrt(count * n_shot * n_tm)

    flat_plane = tuple(dx * PAIR + dy for dx, dy in plane)
    flat_z = tuple(range(n_z))
    sums = range(SUMS)
    spread = []
    for g in sums:
        arrays = [a for pair in halves_[g * per_sum : (g + 1) * per_sum] for a in pair]
        spread.append(list(fold_call(info, 3, flat_plane, arrays, per_sum)))

    def exchanged(sends, shifts):
        gots = [[moved(a, shift) for a, shift in zip(p[1:], shifts[1:])] for p in sends]
        for g in range(SUMS - 1):
            for later in range(g + 1, SUMS):
                gots[g][0], sends[later][0] = lax.optimization_barrier((gots[g][0], sends[later][0]))
        return [[p[0]] + got for p, got in zip(sends, gots)]

    across = [(dx, 0, 0, dy) for dx, dy in plane]
    upward = [(0, 0, dz, 0) for dz in flat_z]
    met = exchanged(spread, across)
    met[-1][0], output = lax.optimization_barrier((met[-1][0], output))
    met = exchanged([list(fold_call(info, 2, flat_z, m, 1)) for m in met], upward)
    totals = [total_call(m) for m in met]
    met = exchanged([[t[0]] * n_z for t in totals], upward)
    met = exchanged([[lay_call(info, 2, flat_z, m)] * n_plane for m in met], across)
    laid = [lay_call(info, 3, flat_plane, m) for m in met]
    parts = [part for piece in laid for part in (piece, moved(piece, (0, 1, 0, 0)))]
    weight_grad, gain_grad = join_call(info, parts, [t[1] for t in totals], scale, dims, width, each // 2)
    return (output.reshape(seqs, span, width), weight_grad, gain_grad.reshape(dims))


def solution(mesh):
    placed = (P("shot", "tm", None), P(), P(), P(), P(), P(), P(), P(), P(), P("shot", "tm", None))
    return jax.shard_map(
        functools.partial(shards, mesh),
        mesh=mesh,
        in_specs=placed,
        out_specs=(P("shot", "tm", None), P(), P()),
        check_vma=False,
    )
```

```python
import functools
import math

import jax
import jax.numpy as jnp
from jax import lax
from jax.experimental import pallas as pl
from jax.experimental.pallas import tpu as pltpu
from jax.sharding import PartitionSpec as P

RELAYS = (4, 2, 2)
SUMS = ((0,), (1, 2))
CORES = 2
PAIR = 2
PER_STEP = 2
F32 = jnp.float32
BF16 = jnp.bfloat16
MIB = 1024 * 1024


def dot(a, b):
    return lax.dot_general(a, b, (((1,), (0,)), ((), ())), preferred_element_type=F32)


def dot_nt(a, b):
    return lax.dot_general(a, b, (((1,), (1,)), ((), ())), preferred_element_type=F32)


def dot_tn(a, b):
    return lax.dot_general(a, b, (((0,), (0,)), ((), ())), preferred_element_type=F32)


def halves(a):
    high = a.astype(BF16)
    return high, (a - high.astype(F32)).astype(BF16)


def dot3(a, b):
    ah, al = halves(a)
    bh, bl = halves(b)
    return dot(ah, bh) + (dot(ah, bl) + dot(al, bh))


def params(mib):
    return pltpu.CompilerParams(vmem_limit_bytes=mib * MIB)


def smem():
    return pl.BlockSpec(memory_space=pltpu.SMEM)


def vmem():
    return pl.BlockSpec(memory_space=pltpu.VMEM)


def whole(shape):
    return pl.BlockSpec(shape, lambda *_: (0,) * len(shape))


def anywhere(after):
    return [pl.BlockSpec(memory_space=pl.ANY)] * len(after)


def skipping(kernel, first, after):
    return lambda *refs: kernel(*refs[:first], *refs[first + len(after) :])


def cost(flops, size):
    return pl.CostEstimate(flops=flops, bytes_accessed=size, transcendentals=0)


def write_gates(span, heads, x_ref, w_ref, level_ref, out_ref):
    lane = lax.broadcasted_iota(jnp.int32, (1, heads), 1)
    rate = jnp.zeros((1, heads), F32)
    bias = jnp.zeros((1, heads), F32)
    for h in range(heads):
        rate = jnp.where(lane == h, level_ref[0, h], rate)
        bias = jnp.where(lane == h, level_ref[1, h], bias)
    gates = dot_nt(x_ref[...], w_ref[...])
    raw = gates[:, :heads]
    softplus = jnp.maximum(raw, 0.0) + jnp.log1p(jnp.exp(-jnp.abs(raw)))
    logdecay = -rate * softplus
    out_ref[:, heads : 2 * heads] = jax.nn.sigmoid(gates[:, heads:] + bias)
    row = lax.broadcasted_iota(jnp.int32, (span, span), 0)
    col = lax.broadcasted_iota(jnp.int32, (span, span), 1)
    lower = jnp.where(row >= col, 1.0, 0.0).astype(F32)
    for first in range(0, x_ref.shape[0], span):
        piece = logdecay[first : first + span]
        out_ref[first : first + span, :heads] = lax.dot_general(
            lower, piece, (((1,), (0,)), ((), ())), precision=lax.Precision.HIGHEST, preferred_element_type=F32
        )


def solve_lower(systems, rights):
    span = systems[0].shape[0]
    row = lax.broadcasted_iota(jnp.int32, (span, span), 0)
    col = lax.broadcasted_iota(jnp.int32, (span, span), 1)
    apart = row ^ col
    invs = [jnp.where(row == col, 1.0, jnp.where(apart == 1, -s, 0.0)).astype(BF16) for s in systems]
    step = 2
    while step < span:
        keep = (apart >= step) & (apart < 2 * step)
        bands = [jnp.where(keep, s, 0.0).astype(BF16) for s in systems]
        inners = [dot(i, b).astype(BF16) for i, b in zip(invs, bands)]
        invs = [i - dot(n, i).astype(BF16) for n, i in zip(inners, invs)]
        step *= 2
    rounded = [r.astype(BF16) for r in rights]
    firsts = [dot(i, b) + (r - b.astype(F32)) for i, b, r in zip(invs, rounded, rights)]
    residuals = [(r - f) - dot3(s, f) for r, f, s in zip(rights, firsts, systems)]
    return [f + dot(i, r.astype(BF16)) for f, i, r in zip(firsts, invs, residuals)]


def local_kernel(first_head, heads, span, per_step, opening, info, table, x_ref, pool_ref, *refs):
    if opening:
        w_ref, level_ref, own_ref, send_ref, core_ref, query_ref, gate_ref = refs

        @pl.when(pl.program_id(0) == 0)
        def _():
            write_gates(span, heads, x_ref, w_ref, level_ref, gate_ref)

    else:
        gate_ref, own_ref, send_ref, core_ref, query_ref = refs
    members = table.shape[1]
    dims = pool_ref.shape[1]
    lane = lax.broadcasted_iota(jnp.int32, (span, 2 * heads), 1)
    wide = lax.broadcasted_iota(jnp.int32, (span, dims), 1)
    row = lax.broadcasted_iota(jnp.int32, (span, span), 0)
    col = lax.broadcasted_iota(jnp.int32, (span, span), 1)
    eye = (
        lax.broadcasted_iota(jnp.int32, (dims, dims), 0) == lax.broadcasted_iota(jnp.int32, (dims, dims), 1)
    ).astype(F32)
    where = []
    heads_in = []
    for local in range(per_step):
        head = first_head + pl.program_id(0) * per_step + local
        chosen = []
        for kind in range(3):
            target = kind * heads + head
            chosen.append(jnp.concatenate([pool_ref[table[1, j, target]] for j in range(members)], 0))
        for part in range(2):
            seq = info[0] if part == 0 else 1 - info[0]
            where.append((local, part, pl.ds(pl.multiple_of(seq * span, span), span)))
            projected = []
            for kind in range(3):
                target = kind * heads + head
                picked = [
                    x_ref[where[-1][2], pl.ds(pl.multiple_of(table[0, j, target] * dims, dims), dims)]
                    for j in range(members)
                ]
                projected.append(dot(jnp.concatenate(picked, 1), chosen[kind]).astype(BF16))
            heads_in.append((head, projected))
    kept, systems, rights = [], [], []
    for (local, part, rows), (head, (query, key, value)) in zip(where, heads_in):
        key_wide = key.astype(F32)
        gates = gate_ref[rows, :]
        cumulative = jnp.sum(jnp.where(lane == head, gates, 0.0), axis=1, keepdims=True)
        beta = jnp.sum(jnp.where(lane == heads + head, gates, 0.0), axis=1, keepdims=True)
        norm = lax.rsqrt(jnp.sum(key_wide * key_wide, axis=1, keepdims=True) + 1e-06)
        across = jnp.where(wide == 0, cumulative, norm).T
        cumulative_row, norm_row = across[0:1, :], across[1:2, :]
        ratio = jnp.where(row >= col, jnp.exp(jnp.minimum(cumulative - cumulative_row, 0.0)), 0.0) * norm_row
        attend = ratio * dot_nt(query, key)
        systems.append(jnp.where(row > col, ratio * dot_nt(key, key), 0.0) * (beta * norm))
        growth = jnp.exp(cumulative)
        rights.append(jnp.concatenate([(beta * growth * norm) * key_wide, beta * value.astype(F32)], axis=1))
        last = cumulative[span - 1 : span, :]
        kept.append((query, key, attend, growth, norm * jnp.exp(last - cumulative), jnp.exp(last)))
    solutions = solve_lower(systems, rights)
    for (local, part, rows), (query, key, attend, growth, tail, final), solved in zip(where, kept, solutions):
        high, low = halves(solved * tail)
        pushed = dot_tn(key, high) + dot_tn(key, low)
        out = own_ref if part == 0 else send_ref
        out[local, :, :dims] = final * eye - pushed[:, :dims]
        out[local, :, dims:] = pushed[:, dims:]
        seen = dot3(attend, solved)
        lanes = slice(local * dims, (local + 1) * dims)
        query_ref[rows, lanes] = growth * query.astype(F32) - seen[:, :dims]
        core_ref[rows, lanes] = seen[:, dims:]


def local_call(info, table, rows, pool, extra, first_head, count_heads, heads, span, after=()):
    count, width = rows.shape
    dims = pool.shape[1]
    opening = isinstance(extra, tuple)
    maps = jax.ShapeDtypeStruct((count_heads, dims, 2 * dims), F32)
    wide = jax.ShapeDtypeStruct((count, count_heads * dims), F32)
    gates = jax.ShapeDtypeStruct((count, 2 * heads), F32)
    map_spec = pl.BlockSpec((PER_STEP, dims, 2 * dims), lambda i, *_: (i, 0, 0))
    row_spec = pl.BlockSpec((count, PER_STEP * dims), lambda i, *_: (0, i))
    if opening:
        more_in = [whole(extra[0].shape), smem()]
        more_out, more_out_specs = (gates,), (whole(gates.shape),)
    else:
        more_in, more_out, more_out_specs, extra = [whole(gates.shape)], (), (), (extra,)
    return pl.pallas_call(
        skipping(functools.partial(local_kernel, first_head, heads, span, PER_STEP, opening), 4 + len(extra), after),
        out_shape=(maps, maps, wide, wide) + more_out,
        grid_spec=pltpu.PrefetchScalarGridSpec(
            num_scalar_prefetch=2,
            grid=(count_heads // PER_STEP,),
            in_specs=[whole(rows.shape), whole(pool.shape)] + more_in + anywhere(after),
            out_specs=(map_spec, map_spec, row_spec, row_spec) + more_out_specs,
        ),
        compiler_params=params(28),
        cost_estimate=cost(count_heads * 2 * 2 * span * 256 * 256 * 24, 8 * MIB),
        name="local",
    )(info, table, rows, pool, *extra, *after)


def apply_map(maps, state):
    dims = maps.shape[0]
    return dot3(maps[:, :dims], state)


def combine_kernel(info, own_ref, got_ref, early_ref, both_ref, push_ref):
    later_is_own = info[0] == 1
    for h in range(own_ref.shape[0]):
        own, got = own_ref[h], got_ref[h]
        early = jnp.where(later_is_own, got, own)
        late = jnp.where(later_is_own, own, got)
        dims = own.shape[0]
        early_ref[h] = early
        both = apply_map(late, early)
        push = both[:, dims:] + late[:, dims:]
        both_ref[h, :, :dims] = both[:, :dims]
        both_ref[h, :, dims:] = push
        push_ref[h] = push


def combine_call(info, own, got, after=()):
    shape = jax.ShapeDtypeStruct(own.shape, F32)
    push = jax.ShapeDtypeStruct(own.shape[:2] + (own.shape[1],), F32)
    return pl.pallas_call(
        skipping(combine_kernel, 3, after),
        out_shape=(shape, shape, push),
        in_specs=[smem(), vmem(), vmem()] + anywhere(after),
        compiler_params=params(12),
        cost_estimate=cost(own.shape[0] * 6 * 128 * 128 * 256, own.size * 16),
        name="combine",
    )(info, own, got, *after)


def hop_kernel(level, info, maps_ref, got_ref, state_ref, kept_ref, out_ref):
    arrived = info[2] == level
    for h in range(maps_ref.shape[0]):
        maps = maps_ref[h]
        dims = maps.shape[0]
        state = jnp.where(arrived, got_ref[h], state_ref[h])
        kept_ref[h] = state
        out_ref[h] = apply_map(maps, state) + maps[:, dims:]


def hop_call(level, info, maps, got, state, after=()):
    shape = jax.ShapeDtypeStruct(state.shape, F32)
    return pl.pallas_call(
        skipping(functools.partial(hop_kernel, level), 4, after),
        out_shape=(shape, shape),
        in_specs=[smem(), vmem(), vmem(), vmem()] + anywhere(after),
        compiler_params=params(12),
        cost_estimate=cost(maps.shape[0] * 6 * 128 * 128 * 128, maps.size * 8),
        name="hop",
    )(info, maps, got, state, *after)


def split_kernel(level, info, maps_ref, got_ref, state_ref, keep_ref, send_ref):
    second = info[0] == 1
    arrived = info[2] == level
    for h in range(maps_ref.shape[0]):
        maps = maps_ref[h]
        state = jnp.where(arrived, got_ref[h], state_ref[h])
        dims = maps.shape[0]
        middle = apply_map(maps, state) + maps[:, dims:]
        keep_ref[h] = jnp.where(second, middle, state)
        send_ref[h] = jnp.where(second, state, middle)


def split_call(level, info, maps, got, state, after=()):
    shape = jax.ShapeDtypeStruct(state.shape, F32)
    return pl.pallas_call(
        skipping(functools.partial(split_kernel, level), 4, after),
        out_shape=(shape, shape),
        in_specs=[smem(), vmem(), vmem(), vmem()] + anywhere(after),
        compiler_params=params(12),
        cost_estimate=cost(maps.shape[0] * 6 * 128 * 128 * 128, maps.size * 8),
        name="split",
    )(info, maps, got, state, *after)


def mix_kernel(span, info, core_ref, query_ref, keep_ref, got_ref, back_ref, gain_ref, cot_ref, mixed_ref, wsend_ref, wkeep_ref):
    step = pl.program_id(0)
    half = pl.num_programs(0) // 2
    dims = gain_ref.shape[1]
    tiles = wsend_ref.shape[0] - 1
    each = tiles // half
    gain_part = jnp.zeros((8, dims), F32)
    for part in range(2):
        seq = info[0] if part == 0 else 1 - info[0]
        rows = pl.ds(pl.multiple_of(seq * span, span), span)
        state = (keep_ref if part == 0 else got_ref)[0]
        core = core_ref[rows, :] + dot3(query_ref[rows, :], state)
        normal = core * lax.rsqrt(jnp.mean(core * core, axis=1, keepdims=True) + 1e-05)
        gain_part += jnp.sum((normal * back_ref[rows, :]).reshape(-1, 8, dims), axis=0)
        mixed_ref[rows, :] = (normal * gain_ref[...]).astype(BF16)
    product = dot_tn(mixed_ref[...], cot_ref[...])
    stripe = dims // 8
    pieces = [
        product[:, first : first + 128].reshape(stripe, 8, 128) for first in range(0, product.shape[1], 128)
    ]

    @pl.when(step == 0)
    def _():
        wkeep_ref[tiles] = gain_part

    @pl.when(step > 0)
    def _():
        wkeep_ref[tiles] += gain_part

    @pl.when(step == 2 * half - 1)
    def _():
        wsend_ref[tiles] = wkeep_ref[tiles]

    @pl.when(step < half)
    def _():
        for i, piece in enumerate(pieces):
            wsend_ref[pl.ds(step * each + i * stripe, stripe)] = piece

    @pl.when(step >= half)
    def _():
        for i, piece in enumerate(pieces):
            wkeep_ref[pl.ds((step - half) * each + i * stripe, stripe)] = piece


def mix_call(info, first_head, core, query, keep, got, back, gain, cot, span, after=()):
    count, width = cot.shape
    heads_here = keep.shape[0]
    dims = gain.shape[1]
    half = heads_here // 2

    def order(i, info):
        first = jnp.where(i < half, 1 - info[1], info[1])
        return first * half + lax.rem(i, half)

    row_spec = pl.BlockSpec((count, dims), lambda i, info: (0, order(i, info)))
    back_spec = pl.BlockSpec((count, dims), lambda i, info: (0, first_head + order(i, info)))
    state_spec = pl.BlockSpec((1, dims, dims), lambda i, info: (order(i, info), 0, 0))
    weight = jax.ShapeDtypeStruct((half * dims * width // 1024 + 1, 8, 128), F32)
    return pl.pallas_call(
        skipping(functools.partial(mix_kernel, span), 8, after),
        out_shape=(jax.ShapeDtypeStruct((count, heads_here * dims), BF16), weight, weight),
        grid_spec=pltpu.PrefetchScalarGridSpec(
            num_scalar_prefetch=1,
            grid=(heads_here,),
            in_specs=[row_spec, row_spec, state_spec, state_spec, back_spec, whole(gain.shape), whole(cot.shape)]
            + anywhere(after),
            out_specs=(row_spec, whole(weight.shape), whole(weight.shape)),
        ),
        compiler_params=params(16),
        cost_estimate=cost(heads_here * 2 * 512 * 1024 * 128, 3 * MIB),
        name="mix",
    )(info, core, query, keep, got, back, gain, cot, *after)


def back_kernel(cot_ref, weight_ref, out_ref):
    out_ref[...] = dot_nt(cot_ref[...], weight_ref[...])


def back_call(cot, weight):
    count, width = cot.shape
    row_spec = pl.BlockSpec((128, width), lambda i: (i, 0))
    return pl.pallas_call(
        back_kernel,
        out_shape=jax.ShapeDtypeStruct((count, width), F32),
        grid=(count // 128,),
        in_specs=[row_spec, whole(weight.shape)],
        out_specs=row_spec,
        compiler_params=params(12),
        cost_estimate=cost(2 * count * width * width, 5 * MIB),
        name="back",
    )(cot, weight)


def finish_kernel(groups, *refs):
    weight_ref, out_ref, done_ref = refs[groups:]
    done_ref[...] = jnp.zeros_like(done_ref)
    stacked = jnp.concatenate([ref[...] for ref in refs[:groups]], axis=1)
    out_ref[...] = dot(stacked, weight_ref[...]).astype(BF16)


def finish_call(mixed, weight):
    count = mixed[0].shape[0]
    width = weight.shape[1]
    row_spec = pl.BlockSpec((128, width), lambda i: (i, 0))
    return pl.pallas_call(
        functools.partial(finish_kernel, len(mixed)),
        out_shape=(jax.ShapeDtypeStruct((count, width), BF16), jax.ShapeDtypeStruct((8, 128), F32)),
        grid=(count // 128,),
        in_specs=[pl.BlockSpec((128, m.shape[1]), lambda i: (i, 0)) for m in mixed] + [whole(weight.shape)],
        out_specs=(row_spec, whole((8, 128))),
        compiler_params=params(12),
        cost_estimate=cost(2 * count * width * width, 4 * MIB),
        name="finish",
    )(*mixed, weight)


def fold_kernel(parts, terms, where, flips, info, *refs):
    ins, outs = refs[: parts * terms], refs[parts * terms :]
    size = ins[0].shape[0] - 1
    share = outs[0].shape[0] - 1
    last = sum(ref[size] for ref in ins)
    for flip, out in zip(flips, outs):
        first = (info[where] ^ flip) * share
        if parts == 1:
            out[:share] = sum(ref[pl.ds(first, share)] for ref in ins)
        else:
            for part in range(parts):

                @pl.when((first >= part * size) & (first < (part + 1) * size))
                def _(part=part, out=out, first=first):
                    out[:share] = sum(ref[pl.ds(first - part * size, share)] for ref in ins[part * terms : (part + 1) * terms])

        out[share] = last


def fold_call(info, where, flips, arrays, parts, after=()):
    terms = len(arrays) // parts
    size = arrays[0].shape[0] - 1
    share = size * parts // len(flips)
    shape = jax.ShapeDtypeStruct((share + 1, 8, 128), F32)
    return pl.pallas_call(
        skipping(functools.partial(fold_kernel, parts, terms, where, flips), 1 + len(arrays), after),
        out_shape=[shape] * len(flips),
        in_specs=[smem()] + [vmem()] * len(arrays) + anywhere(after),
        compiler_params=params(12),
        cost_estimate=cost(size * 1024 * len(arrays), size * 4096 * (len(arrays) + 1)),
        name="fold",
    )(info, *arrays, *after)


def total_kernel(*refs):
    ins, (piece_ref, last_ref) = refs[:-2], refs[-2:]
    size = piece_ref.shape[0]
    piece_ref[...] = sum(ref[:size] for ref in ins)
    last_ref[...] = sum(ref[size] for ref in ins)


def total_call(arrays):
    size = arrays[0].shape[0] - 1
    return pl.pallas_call(
        total_kernel,
        out_shape=(jax.ShapeDtypeStruct((size, 8, 128), F32), jax.ShapeDtypeStruct((8, 128), F32)),
        in_specs=[vmem()] * len(arrays),
        out_specs=(vmem(), vmem()),
        compiler_params=params(12),
        cost_estimate=cost(size * 4096, size * 4096 * 5),
        name="total",
    )(*arrays)


def lay_kernel(where, info, own_ref, got_ref, out_ref):
    share = own_ref.shape[0]
    out_ref[pl.ds(info[where] * share, share)] = own_ref[...]
    out_ref[pl.ds((1 - info[where]) * share, share)] = got_ref[...]


def lay_call(info, where, own, got, after=()):
    share = own.shape[0]
    return pl.pallas_call(
        skipping(functools.partial(lay_kernel, where), 3, after),
        out_shape=jax.ShapeDtypeStruct((share * 2, 8, 128), F32),
        in_specs=[smem(), vmem(), vmem()] + anywhere(after),
        compiler_params=params(12),
        cost_estimate=cost(0, share * 16384),
        name="lay",
    )(info, own, got, *after)


def join_kernel(scale, stripe, blocks, info, *refs):
    sums = (len(refs) - 2) // 3
    lasts, (out_ref, gain_ref) = refs[2 * sums : 3 * sums], refs[-2:]
    columns = out_ref.shape[1] // 128
    dims = stripe * 8
    for g in range(sums):
        for part, ref in enumerate(refs[2 * g : 2 * g + 2]):
            side = info[1] if part == 0 else 1 - info[1]
            for index, (base, half) in enumerate(blocks[g]):
                rows = pl.ds(pl.multiple_of((base + side * half) * dims, dims), dims)
                for col in range(columns):
                    first = (index * columns + col) * stripe
                    values = ref[first : first + stripe].reshape(dims, 128) * scale
                    out_ref[rows, col * 128 : (col + 1) * 128] = values.astype(BF16)
    gain_ref[...] = jnp.sum(sum(ref[...] for ref in lasts), axis=0, keepdims=True) * scale


def join_call(info, parts, lasts, blocks, scale, dims, width):
    total = sum(p.shape[0] for p in parts) * 1024 // width
    return pl.pallas_call(
        functools.partial(join_kernel, scale, dims // 8, blocks),
        out_shape=(jax.ShapeDtypeStruct((total, width), BF16), jax.ShapeDtypeStruct((1, 128), F32)),
        in_specs=[smem()] + [vmem()] * (len(parts) + len(lasts)),
        out_specs=(vmem(), vmem()),
        compiler_params=params(16),
        name="join",
    )(info, *parts, *lasts)


def shards(mesh, features, weight_pool, pattern_in, pattern_pool, gate_weight, decay_rate, beta_bias, norm_gain, out_weight, cotangent):
    n_shot, n_tm = mesh.shape["shot"], mesh.shape["tm"]
    n_x, n_z = n_shot // CORES, n_tm // PAIR
    seqs, span, width = features.shape
    heads = decay_rate.shape[0]
    dims = weight_pool.shape[1]
    count = seqs * span
    both = ("shot", "tm")
    shot, tm = lax.axis_index("shot"), lax.axis_index("tm")
    x, core, z, y = shot // CORES, shot % CORES, tm // PAIR, tm % PAIR

    def place(xi, ci, zi, yi):
        return (xi * CORES + ci) * n_tm + zi * PAIR + yi

    def moved(array, shift):
        dx, dc, dz, dy = shift
        route = []
        for xi in range(n_x):
            for ci in range(CORES):
                for zi in range(n_z):
                    for yi in range(PAIR):
                        route.append((place(xi, ci, zi, yi), place(xi ^ dx, ci ^ dc, zi ^ dz, yi ^ dy)))
        return lax.ppermute(array, both, route)

    def lifted(array, level):
        ends = ((level, level + 1), (level + 1, level))
        route = [(a * PAIR + yi, b * PAIR + yi) for a, b in ends for yi in range(PAIR)]
        return lax.ppermute(array, "tm", route)

    def bits(size):
        return [1 << bit for bit in range(size.bit_length() - 1)]

    steps_x = [((reach, 0, 0, 0), (x // reach) % 2) for reach in bits(n_x)]
    steps_y = [((0, 0, 0, reach), (y // reach) % 2) for reach in bits(PAIR)]
    steps_z = [((0, 0, reach, 0), (z // reach) % 2) for reach in bits(n_z)]
    labelled = [(shift, 3 + i) for i, (shift, _) in enumerate(steps_x + steps_y + steps_z)]
    on_x, on_y = labelled[: len(steps_x)], labelled[len(steps_x) : len(steps_x) + len(steps_y)]
    on_z = labelled[len(steps_x) + len(steps_y) :]
    info = jnp.stack([y, core, z] + [bit for _, bit in steps_x + steps_y + steps_z]).astype(jnp.int32)
    table = jnp.stack([pattern_in.T, pattern_pool.T])
    levels = jnp.stack([decay_rate, beta_bias])
    rows = features.reshape(count, width)
    cot = cotangent.reshape(count, width)
    gain = norm_gain.reshape(1, dims)
    relays = range(len(RELAYS))
    last = len(RELAYS) - 1
    first_of = [sum(RELAYS[:g]) for g in relays]

    extra = (gate_weight.T, levels)
    locals_ = []
    for g in relays:
        after = [locals_[-1][0]] if g else []
        out = list(local_call(info, table, rows, weight_pool, extra, first_of[g], RELAYS[g], heads, span, after))
        if g == 0:
            extra = out.pop()
        locals_.append(out)
    back = back_call(cot, out_weight)
    maps = []
    for g in relays:
        after = [locals_[last][0]] if g == 0 else [maps[-1][2]]
        if g == last:
            after.append(back)
        maps.append(combine_call(info, locals_[g][0], moved(locals_[g][1], (0, 0, 0, 1)), after))
    states = [jnp.zeros((size, dims, dims), F32) for size in RELAYS]
    sends = [m[2] for m in maps]
    for level in range(1, n_z):
        gots = [lifted(send, level - 1) for send in sends]
        after = [sends[last]]
        if level == n_z - 1:
            break
        for g in relays:
            states[g], sends[g] = hop_call(level, info, maps[g][1], gots[g], states[g], after)
            after = [sends[g]]
    mixed, kept, got, ready = [], [], [], []
    for g in relays:
        keep, send = split_call(n_z - 1, info, maps[g][0], gots[g], states[g], after)
        after = [send]
        ready.append((keep, moved(send, (0, 0, 0, 1))))
    for g in relays:
        states_g = *locals_[g][2:], *ready[g]
        flat, w_send, w_keep = mix_call(info, first_of[g], *states_g, back, gain, cot, span, after)
        after = [w_keep]
        mixed.append(flat)
        kept.append(w_keep)
        got.append(moved(w_send, (0, 1, 0, 0)))
    output, done = finish_call(mixed, out_weight)
    scale = 1.0 / math.sqrt(count * n_shot * n_tm)

    sums = range(len(SUMS))
    orders = [(on_x + on_y if g % 2 == 0 else on_y + on_x) + on_z for g in sums]
    arrays = [[a for r in SUMS[g] for a in (kept[r], got[r])] for g in sums]
    parts = [len(SUMS[g]) for g in sums]
    previous = None
    for step in range(len(orders[0])):
        for g in sums:
            shift, where = orders[g][step]
            after = [previous] if g or step else []
            if g == sums[-1] and step == 1:
                after.append(done)
            own, send = fold_call(info, where, (0, 1), arrays[g], parts[g], after)
            arrays[g], parts[g] = [own, moved(send, shift)], 1
            previous = own
    totals = [total_call(a) for a in arrays]
    pieces = [t[0] for t in totals]
    for step in reversed(range(len(orders[0]))):
        arrived = [moved(pieces[g], orders[g][step][0]) for g in sums]
        previous = pieces[-1]
        for g in sums:
            pieces[g] = previous = lay_call(info, orders[g][step][1], pieces[g], arrived[g], [previous])
    ends = [part for piece in pieces for part in (piece, moved(piece, (0, 1, 0, 0)))]
    blocks = [[(first_of[r] + i, RELAYS[r] // 2) for r in SUMS[g] for i in range(RELAYS[r] // 2)] for g in sums]
    weight_grad, gain_grad = join_call(info, ends, [t[1] for t in totals], blocks, scale, dims, width)
    return (output.reshape(seqs, span, width), weight_grad, gain_grad.reshape(dims))


def solution(mesh):
    placed = (P("shot", "tm", None), P(), P(), P(), P(), P(), P(), P(), P(), P("shot", "tm", None))
    return jax.shard_map(
        functools.partial(shards, mesh),
        mesh=mesh,
        in_specs=placed,
        out_specs=(P("shot", "tm", None), P(), P()),
        check_vma=False,
    )
```

```python
import functools
import math

import jax
import jax.numpy as jnp
from jax import lax
from jax.experimental import pallas as pl
from jax.experimental.pallas import tpu as pltpu
from jax.sharding import PartitionSpec as P

RELAYS = (4, 4)
SUMS = ((0,), (1,))
CORES = 2
PAIR = 2
PER_STEP = 2
F32 = jnp.float32
BF16 = jnp.bfloat16
MIB = 1024 * 1024


def dot(a, b):
    return lax.dot_general(a, b, (((1,), (0,)), ((), ())), preferred_element_type=F32)


def dot_nt(a, b):
    return lax.dot_general(a, b, (((1,), (1,)), ((), ())), preferred_element_type=F32)


def dot_tn(a, b):
    return lax.dot_general(a, b, (((0,), (0,)), ((), ())), preferred_element_type=F32)


def halves(a):
    high = a.astype(BF16)
    return high, (a - high.astype(F32)).astype(BF16)


def dot3(a, b):
    ah, al = halves(a)
    bh, bl = halves(b)
    return dot(ah, bh) + (dot(ah, bl) + dot(al, bh))


def params(mib):
    return pltpu.CompilerParams(vmem_limit_bytes=mib * MIB)


def smem():
    return pl.BlockSpec(memory_space=pltpu.SMEM)


def vmem():
    return pl.BlockSpec(memory_space=pltpu.VMEM)


def whole(shape):
    return pl.BlockSpec(shape, lambda *_: (0,) * len(shape))


def anywhere(after):
    return [pl.BlockSpec(memory_space=pl.ANY)] * len(after)


def skipping(kernel, first, after):
    return lambda *refs: kernel(*refs[:first], *refs[first + len(after) :])


def cost(flops, size):
    return pl.CostEstimate(flops=flops, bytes_accessed=size, transcendentals=0)


def write_gates(span, heads, x_ref, w_ref, level_ref, out_ref):
    lane = lax.broadcasted_iota(jnp.int32, (1, heads), 1)
    rate = jnp.zeros((1, heads), F32)
    bias = jnp.zeros((1, heads), F32)
    for h in range(heads):
        rate = jnp.where(lane == h, level_ref[0, h], rate)
        bias = jnp.where(lane == h, level_ref[1, h], bias)
    gates = dot_nt(x_ref[...], w_ref[...])
    raw = gates[:, :heads]
    softplus = jnp.maximum(raw, 0.0) + jnp.log1p(jnp.exp(-jnp.abs(raw)))
    logdecay = -rate * softplus
    out_ref[:, heads : 2 * heads] = jax.nn.sigmoid(gates[:, heads:] + bias)
    row = lax.broadcasted_iota(jnp.int32, (span, span), 0)
    col = lax.broadcasted_iota(jnp.int32, (span, span), 1)
    lower = jnp.where(row >= col, 1.0, 0.0).astype(F32)
    for first in range(0, x_ref.shape[0], span):
        piece = logdecay[first : first + span]
        out_ref[first : first + span, :heads] = lax.dot_general(
            lower, piece, (((1,), (0,)), ((), ())), precision=lax.Precision.HIGHEST, preferred_element_type=F32
        )


def solve_lower(systems, rights):
    span = systems[0].shape[0]
    row = lax.broadcasted_iota(jnp.int32, (span, span), 0)
    col = lax.broadcasted_iota(jnp.int32, (span, span), 1)
    apart = row ^ col
    invs = [jnp.where(row == col, 1.0, jnp.where(apart == 1, -s, 0.0)).astype(BF16) for s in systems]
    step = 2
    while step < span:
        keep = (apart >= step) & (apart < 2 * step)
        bands = [jnp.where(keep, s, 0.0).astype(BF16) for s in systems]
        inners = [dot(i, b).astype(BF16) for i, b in zip(invs, bands)]
        invs = [i - dot(n, i).astype(BF16) for n, i in zip(inners, invs)]
        step *= 2
    rounded = [r.astype(BF16) for r in rights]
    firsts = [dot(i, b) + (r - b.astype(F32)) for i, b, r in zip(invs, rounded, rights)]
    residuals = [(r - f) - dot3(s, f) for r, f, s in zip(rights, firsts, systems)]
    return [f + dot(i, r.astype(BF16)) for f, i, r in zip(firsts, invs, residuals)]


def local_kernel(first_head, heads, span, per_step, opening, info, table, x_ref, pool_ref, *refs):
    if opening:
        w_ref, level_ref, own_ref, send_ref, core_ref, query_ref, gate_ref = refs

        @pl.when(pl.program_id(0) == 0)
        def _():
            write_gates(span, heads, x_ref, w_ref, level_ref, gate_ref)

    else:
        gate_ref, own_ref, send_ref, core_ref, query_ref = refs
    members = table.shape[1]
    dims = pool_ref.shape[1]
    lane = lax.broadcasted_iota(jnp.int32, (span, 2 * heads), 1)
    wide = lax.broadcasted_iota(jnp.int32, (span, dims), 1)
    row = lax.broadcasted_iota(jnp.int32, (span, span), 0)
    col = lax.broadcasted_iota(jnp.int32, (span, span), 1)
    eye = (
        lax.broadcasted_iota(jnp.int32, (dims, dims), 0) == lax.broadcasted_iota(jnp.int32, (dims, dims), 1)
    ).astype(F32)
    where = []
    heads_in = []
    for local in range(per_step):
        head = first_head + pl.program_id(0) * per_step + local
        chosen = []
        for kind in range(3):
            target = kind * heads + head
            chosen.append(jnp.concatenate([pool_ref[table[1, j, target]] for j in range(members)], 0))
        for part in range(2):
            seq = info[0] if part == 0 else 1 - info[0]
            where.append((local, part, pl.ds(pl.multiple_of(seq * span, span), span)))
            projected = []
            for kind in range(3):
                target = kind * heads + head
                picked = [
                    x_ref[where[-1][2], pl.ds(pl.multiple_of(table[0, j, target] * dims, dims), dims)]
                    for j in range(members)
                ]
                projected.append(dot(jnp.concatenate(picked, 1), chosen[kind]).astype(BF16))
            heads_in.append((head, projected))
    kept, systems, rights = [], [], []
    for (local, part, rows), (head, (query, key, value)) in zip(where, heads_in):
        key_wide = key.astype(F32)
        gates = gate_ref[rows, :]
        cumulative = jnp.sum(jnp.where(lane == head, gates, 0.0), axis=1, keepdims=True)
        beta = jnp.sum(jnp.where(lane == heads + head, gates, 0.0), axis=1, keepdims=True)
        norm = lax.rsqrt(jnp.sum(key_wide * key_wide, axis=1, keepdims=True) + 1e-06)
        across = jnp.where(wide == 0, cumulative, norm).T
        cumulative_row, norm_row = across[0:1, :], across[1:2, :]
        ratio = jnp.where(row >= col, jnp.exp(jnp.minimum(cumulative - cumulative_row, 0.0)), 0.0) * norm_row
        attend = ratio * dot_nt(query, key)
        systems.append(jnp.where(row > col, ratio * dot_nt(key, key), 0.0) * (beta * norm))
        growth = jnp.exp(cumulative)
        rights.append(jnp.concatenate([(beta * growth * norm) * key_wide, beta * value.astype(F32)], axis=1))
        last = cumulative[span - 1 : span, :]
        kept.append((query, key, attend, growth, norm * jnp.exp(last - cumulative), jnp.exp(last)))
    solutions = solve_lower(systems, rights)
    for (local, part, rows), (query, key, attend, growth, tail, final), solved in zip(where, kept, solutions):
        high, low = halves(solved * tail)
        pushed = dot_tn(key, high) + dot_tn(key, low)
        out = own_ref if part == 0 else send_ref
        out[local, :, :dims] = final * eye - pushed[:, :dims]
        out[local, :, dims:] = pushed[:, dims:]
        seen = dot3(attend, solved)
        lanes = slice(local * dims, (local + 1) * dims)
        query_ref[rows, lanes] = growth * query.astype(F32) - seen[:, :dims]
        core_ref[rows, lanes] = seen[:, dims:]


def local_call(info, table, rows, pool, extra, first_head, count_heads, heads, span, after=()):
    count, width = rows.shape
    dims = pool.shape[1]
    opening = isinstance(extra, tuple)
    maps = jax.ShapeDtypeStruct((count_heads, dims, 2 * dims), F32)
    wide = jax.ShapeDtypeStruct((count, count_heads * dims), F32)
    gates = jax.ShapeDtypeStruct((count, 2 * heads), F32)
    map_spec = pl.BlockSpec((PER_STEP, dims, 2 * dims), lambda i, *_: (i, 0, 0))
    row_spec = pl.BlockSpec((count, PER_STEP * dims), lambda i, *_: (0, i))
    if opening:
        more_in = [whole(extra[0].shape), smem()]
        more_out, more_out_specs = (gates,), (whole(gates.shape),)
    else:
        more_in, more_out, more_out_specs, extra = [whole(gates.shape)], (), (), (extra,)
    return pl.pallas_call(
        skipping(functools.partial(local_kernel, first_head, heads, span, PER_STEP, opening), 4 + len(extra), after),
        out_shape=(maps, maps, wide, wide) + more_out,
        grid_spec=pltpu.PrefetchScalarGridSpec(
            num_scalar_prefetch=2,
            grid=(count_heads // PER_STEP,),
            in_specs=[whole(rows.shape), whole(pool.shape)] + more_in + anywhere(after),
            out_specs=(map_spec, map_spec, row_spec, row_spec) + more_out_specs,
        ),
        compiler_params=params(28),
        cost_estimate=cost(count_heads * 2 * 2 * span * 256 * 256 * 24, 8 * MIB),
        name="local",
    )(info, table, rows, pool, *extra, *after)


def apply_map(maps, state):
    dims = maps.shape[0]
    return dot3(maps[:, :dims], state)


def combine_kernel(info, own_ref, got_ref, early_ref, both_ref, push_ref):
    later_is_own = info[0] == 1
    for h in range(own_ref.shape[0]):
        own, got = own_ref[h], got_ref[h]
        early = jnp.where(later_is_own, got, own)
        late = jnp.where(later_is_own, own, got)
        dims = own.shape[0]
        early_ref[h] = early
        both = apply_map(late, early)
        push = both[:, dims:] + late[:, dims:]
        both_ref[h, :, :dims] = both[:, :dims]
        both_ref[h, :, dims:] = push
        push_ref[h] = push


def combine_call(info, own, got, after=()):
    shape = jax.ShapeDtypeStruct(own.shape, F32)
    push = jax.ShapeDtypeStruct(own.shape[:2] + (own.shape[1],), F32)
    return pl.pallas_call(
        skipping(combine_kernel, 3, after),
        out_shape=(shape, shape, push),
        in_specs=[smem(), vmem(), vmem()] + anywhere(after),
        compiler_params=params(12),
        cost_estimate=cost(own.shape[0] * 6 * 128 * 128 * 256, own.size * 16),
        name="combine",
    )(info, own, got, *after)


def hop_kernel(level, info, maps_ref, got_ref, state_ref, kept_ref, out_ref):
    arrived = info[2] == level
    for h in range(maps_ref.shape[0]):
        maps = maps_ref[h]
        dims = maps.shape[0]
        state = jnp.where(arrived, got_ref[h], state_ref[h])
        kept_ref[h] = state
        out_ref[h] = apply_map(maps, state) + maps[:, dims:]


def hop_call(level, info, maps, got, state, after=()):
    shape = jax.ShapeDtypeStruct(state.shape, F32)
    return pl.pallas_call(
        skipping(functools.partial(hop_kernel, level), 4, after),
        out_shape=(shape, shape),
        in_specs=[smem(), vmem(), vmem(), vmem()] + anywhere(after),
        compiler_params=params(12),
        cost_estimate=cost(maps.shape[0] * 6 * 128 * 128 * 128, maps.size * 8),
        name="hop",
    )(info, maps, got, state, *after)


def split_kernel(level, info, maps_ref, got_ref, state_ref, keep_ref, send_ref):
    second = info[0] == 1
    arrived = info[2] == level
    for h in range(maps_ref.shape[0]):
        maps = maps_ref[h]
        state = jnp.where(arrived, got_ref[h], state_ref[h])
        dims = maps.shape[0]
        middle = apply_map(maps, state) + maps[:, dims:]
        keep_ref[h] = jnp.where(second, middle, state)
        send_ref[h] = jnp.where(second, state, middle)


def split_call(level, info, maps, got, state, after=()):
    shape = jax.ShapeDtypeStruct(state.shape, F32)
    return pl.pallas_call(
        skipping(functools.partial(split_kernel, level), 4, after),
        out_shape=(shape, shape),
        in_specs=[smem(), vmem(), vmem(), vmem()] + anywhere(after),
        compiler_params=params(12),
        cost_estimate=cost(maps.shape[0] * 6 * 128 * 128 * 128, maps.size * 8),
        name="split",
    )(info, maps, got, state, *after)


def mix_kernel(span, info, core_ref, query_ref, keep_ref, got_ref, back_ref, gain_ref, cot_ref, mixed_ref, wsend_ref, wkeep_ref):
    step = pl.program_id(0)
    half = pl.num_programs(0) // 2
    dims = gain_ref.shape[1]
    tiles = wsend_ref.shape[0] - 1
    each = tiles // half
    gain_part = jnp.zeros((8, dims), F32)
    for part in range(2):
        seq = info[0] if part == 0 else 1 - info[0]
        rows = pl.ds(pl.multiple_of(seq * span, span), span)
        state = (keep_ref if part == 0 else got_ref)[0]
        core = core_ref[rows, :] + dot3(query_ref[rows, :], state)
        normal = core * lax.rsqrt(jnp.mean(core * core, axis=1, keepdims=True) + 1e-05)
        gain_part += jnp.sum((normal * back_ref[rows, :]).reshape(-1, 8, dims), axis=0)
        mixed_ref[rows, :] = (normal * gain_ref[...]).astype(BF16)
    product = dot_tn(mixed_ref[...], cot_ref[...])
    stripe = dims // 8
    pieces = [
        product[:, first : first + 128].reshape(stripe, 8, 128) for first in range(0, product.shape[1], 128)
    ]

    @pl.when(step == 0)
    def _():
        wkeep_ref[tiles] = gain_part

    @pl.when(step > 0)
    def _():
        wkeep_ref[tiles] += gain_part

    @pl.when(step == 2 * half - 1)
    def _():
        wsend_ref[tiles] = wkeep_ref[tiles]

    @pl.when(step < half)
    def _():
        for i, piece in enumerate(pieces):
            wsend_ref[pl.ds(step * each + i * stripe, stripe)] = piece

    @pl.when(step >= half)
    def _():
        for i, piece in enumerate(pieces):
            wkeep_ref[pl.ds((step - half) * each + i * stripe, stripe)] = piece


def mix_call(info, first_head, core, query, keep, got, back, gain, cot, span, after=()):
    count, width = cot.shape
    heads_here = keep.shape[0]
    dims = gain.shape[1]
    half = heads_here // 2

    def order(i, info):
        first = jnp.where(i < half, 1 - info[1], info[1])
        return first * half + lax.rem(i, half)

    row_spec = pl.BlockSpec((count, dims), lambda i, info: (0, order(i, info)))
    back_spec = pl.BlockSpec((count, dims), lambda i, info: (0, first_head + order(i, info)))
    state_spec = pl.BlockSpec((1, dims, dims), lambda i, info: (order(i, info), 0, 0))
    weight = jax.ShapeDtypeStruct((half * dims * width // 1024 + 1, 8, 128), F32)
    return pl.pallas_call(
        skipping(functools.partial(mix_kernel, span), 8, after),
        out_shape=(jax.ShapeDtypeStruct((count, heads_here * dims), BF16), weight, weight),
        grid_spec=pltpu.PrefetchScalarGridSpec(
            num_scalar_prefetch=1,
            grid=(heads_here,),
            in_specs=[row_spec, row_spec, state_spec, state_spec, back_spec, whole(gain.shape), whole(cot.shape)]
            + anywhere(after),
            out_specs=(row_spec, whole(weight.shape), whole(weight.shape)),
        ),
        compiler_params=params(16),
        cost_estimate=cost(heads_here * 2 * 512 * 1024 * 128, 3 * MIB),
        name="mix",
    )(info, core, query, keep, got, back, gain, cot, *after)


def back_kernel(cot_ref, weight_ref, out_ref):
    out_ref[...] = dot_nt(cot_ref[...], weight_ref[...])


def back_call(cot, weight):
    count, width = cot.shape
    row_spec = pl.BlockSpec((128, width), lambda i: (i, 0))
    return pl.pallas_call(
        back_kernel,
        out_shape=jax.ShapeDtypeStruct((count, width), F32),
        grid=(count // 128,),
        in_specs=[row_spec, whole(weight.shape)],
        out_specs=row_spec,
        compiler_params=params(12),
        cost_estimate=cost(2 * count * width * width, 5 * MIB),
        name="back",
    )(cot, weight)


def finish_kernel(groups, *refs):
    weight_ref, out_ref, done_ref = refs[groups:]
    done_ref[...] = jnp.zeros_like(done_ref)
    stacked = jnp.concatenate([ref[...] for ref in refs[:groups]], axis=1)
    out_ref[...] = dot(stacked, weight_ref[...]).astype(BF16)


def finish_call(mixed, weight):
    count = mixed[0].shape[0]
    width = weight.shape[1]
    row_spec = pl.BlockSpec((128, width), lambda i: (i, 0))
    return pl.pallas_call(
        functools.partial(finish_kernel, len(mixed)),
        out_shape=(jax.ShapeDtypeStruct((count, width), BF16), jax.ShapeDtypeStruct((8, 128), F32)),
        grid=(count // 128,),
        in_specs=[pl.BlockSpec((128, m.shape[1]), lambda i: (i, 0)) for m in mixed] + [whole(weight.shape)],
        out_specs=(row_spec, whole((8, 128))),
        compiler_params=params(12),
        cost_estimate=cost(2 * count * width * width, 4 * MIB),
        name="finish",
    )(*mixed, weight)


def fold_kernel(parts, terms, where, flips, info, *refs):
    ins, outs = refs[: parts * terms], refs[parts * terms :]
    size = ins[0].shape[0] - 1
    share = outs[0].shape[0] - 1
    last = sum(ref[size] for ref in ins)
    for flip, out in zip(flips, outs):
        first = (info[where] ^ flip) * share
        if parts == 1:
            out[:share] = sum(ref[pl.ds(first, share)] for ref in ins)
        else:
            for part in range(parts):

                @pl.when((first >= part * size) & (first < (part + 1) * size))
                def _(part=part, out=out, first=first):
                    out[:share] = sum(ref[pl.ds(first - part * size, share)] for ref in ins[part * terms : (part + 1) * terms])

        out[share] = last


def fold_call(info, where, flips, arrays, parts, after=()):
    terms = len(arrays) // parts
    size = arrays[0].shape[0] - 1
    share = size * parts // len(flips)
    shape = jax.ShapeDtypeStruct((share + 1, 8, 128), F32)
    return pl.pallas_call(
        skipping(functools.partial(fold_kernel, parts, terms, where, flips), 1 + len(arrays), after),
        out_shape=[shape] * len(flips),
        in_specs=[smem()] + [vmem()] * len(arrays) + anywhere(after),
        compiler_params=params(12),
        cost_estimate=cost(size * 1024 * len(arrays), size * 4096 * (len(arrays) + 1)),
        name="fold",
    )(info, *arrays, *after)


def total_kernel(*refs):
    ins, (piece_ref, last_ref) = refs[:-2], refs[-2:]
    size = piece_ref.shape[0]
    piece_ref[...] = sum(ref[:size] for ref in ins)
    last_ref[...] = sum(ref[size] for ref in ins)


def total_call(arrays):
    size = arrays[0].shape[0] - 1
    return pl.pallas_call(
        total_kernel,
        out_shape=(jax.ShapeDtypeStruct((size, 8, 128), F32), jax.ShapeDtypeStruct((8, 128), F32)),
        in_specs=[vmem()] * len(arrays),
        out_specs=(vmem(), vmem()),
        compiler_params=params(12),
        cost_estimate=cost(size * 4096, size * 4096 * 5),
        name="total",
    )(*arrays)


def lay_kernel(where, info, own_ref, got_ref, out_ref):
    share = own_ref.shape[0]
    out_ref[pl.ds(info[where] * share, share)] = own_ref[...]
    out_ref[pl.ds((1 - info[where]) * share, share)] = got_ref[...]


def lay_call(info, where, own, got, after=()):
    share = own.shape[0]
    return pl.pallas_call(
        skipping(functools.partial(lay_kernel, where), 3, after),
        out_shape=jax.ShapeDtypeStruct((share * 2, 8, 128), F32),
        in_specs=[smem(), vmem(), vmem()] + anywhere(after),
        compiler_params=params(12),
        cost_estimate=cost(0, share * 16384),
        name="lay",
    )(info, own, got, *after)


def join_kernel(scale, stripe, blocks, info, *refs):
    sums = (len(refs) - 2) // 3
    lasts, (out_ref, gain_ref) = refs[2 * sums : 3 * sums], refs[-2:]
    columns = out_ref.shape[1] // 128
    dims = stripe * 8
    for g in range(sums):
        for part, ref in enumerate(refs[2 * g : 2 * g + 2]):
            side = info[1] if part == 0 else 1 - info[1]
            for index, (base, half) in enumerate(blocks[g]):
                rows = pl.ds(pl.multiple_of((base + side * half) * dims, dims), dims)
                for col in range(columns):
                    first = (index * columns + col) * stripe
                    values = ref[first : first + stripe].reshape(dims, 128) * scale
                    out_ref[rows, col * 128 : (col + 1) * 128] = values.astype(BF16)
    gain_ref[...] = jnp.sum(sum(ref[...] for ref in lasts), axis=0, keepdims=True) * scale


def join_call(info, parts, lasts, blocks, scale, dims, width):
    total = sum(p.shape[0] for p in parts) * 1024 // width
    return pl.pallas_call(
        functools.partial(join_kernel, scale, dims // 8, blocks),
        out_shape=(jax.ShapeDtypeStruct((total, width), BF16), jax.ShapeDtypeStruct((1, 128), F32)),
        in_specs=[smem()] + [vmem()] * (len(parts) + len(lasts)),
        out_specs=(vmem(), vmem()),
        compiler_params=params(16),
        name="join",
    )(info, *parts, *lasts)


def shards(mesh, features, weight_pool, pattern_in, pattern_pool, gate_weight, decay_rate, beta_bias, norm_gain, out_weight, cotangent):
    n_shot, n_tm = mesh.shape["shot"], mesh.shape["tm"]
    n_x, n_z = n_shot // CORES, n_tm // PAIR
    seqs, span, width = features.shape
    heads = decay_rate.shape[0]
    dims = weight_pool.shape[1]
    count = seqs * span
    both = ("shot", "tm")
    shot, tm = lax.axis_index("shot"), lax.axis_index("tm")
    x, core, z, y = shot // CORES, shot % CORES, tm // PAIR, tm % PAIR

    def place(xi, ci, zi, yi):
        return (xi * CORES + ci) * n_tm + zi * PAIR + yi

    def moved(array, shift):
        dx, dc, dz, dy = shift
        route = []
        for xi in range(n_x):
            for ci in range(CORES):
                for zi in range(n_z):
                    for yi in range(PAIR):
                        route.append((place(xi, ci, zi, yi), place(xi ^ dx, ci ^ dc, zi ^ dz, yi ^ dy)))
        return lax.ppermute(array, both, route)

    def lifted(array, level):
        ends = ((level, level + 1), (level + 1, level))
        route = [(a * PAIR + yi, b * PAIR + yi) for a, b in ends for yi in range(PAIR)]
        return lax.ppermute(array, "tm", route)

    def bits(size):
        return [1 << bit for bit in range(size.bit_length() - 1)]

    steps_x = [((reach, 0, 0, 0), (x // reach) % 2) for reach in bits(n_x)]
    steps_y = [((0, 0, 0, reach), (y // reach) % 2) for reach in bits(PAIR)]
    steps_z = [((0, 0, reach, 0), (z // reach) % 2) for reach in bits(n_z)]
    labelled = [(shift, 3 + i) for i, (shift, _) in enumerate(steps_x + steps_y + steps_z)]
    on_x, on_y = labelled[: len(steps_x)], labelled[len(steps_x) : len(steps_x) + len(steps_y)]
    on_z = labelled[len(steps_x) + len(steps_y) :]
    info = jnp.stack([y, core, z] + [bit for _, bit in steps_x + steps_y + steps_z]).astype(jnp.int32)
    table = jnp.stack([pattern_in.T, pattern_pool.T])
    levels = jnp.stack([decay_rate, beta_bias])
    rows = features.reshape(count, width)
    cot = cotangent.reshape(count, width)
    gain = norm_gain.reshape(1, dims)
    relays = range(len(RELAYS))
    last = len(RELAYS) - 1
    first_of = [sum(RELAYS[:g]) for g in relays]

    extra = (gate_weight.T, levels)
    locals_ = []
    for g in relays:
        after = [locals_[-1][0]] if g else []
        out = list(local_call(info, table, rows, weight_pool, extra, first_of[g], RELAYS[g], heads, span, after))
        if g == 0:
            extra = out.pop()
        locals_.append(out)
    back = back_call(cot, out_weight)
    maps = []
    for g in relays:
        after = [locals_[last][0]] if g == 0 else [maps[-1][2]]
        if g == last:
            after.append(back)
        maps.append(combine_call(info, locals_[g][0], moved(locals_[g][1], (0, 0, 0, 1)), after))
    states = [jnp.zeros((size, dims, dims), F32) for size in RELAYS]
    sends = [m[2] for m in maps]
    for level in range(1, n_z):
        gots = [lifted(send, level - 1) for send in sends]
        after = [sends[last]]
        if level == n_z - 1:
            break
        for g in relays:
            states[g], sends[g] = hop_call(level, info, maps[g][1], gots[g], states[g], after)
            after = [sends[g]]
    mixed, kept, got, ready = [], [], [], []
    for g in relays:
        keep, send = split_call(n_z - 1, info, maps[g][0], gots[g], states[g], after)
        after = [send]
        ready.append((keep, moved(send, (0, 0, 0, 1))))
    for g in relays:
        states_g = *locals_[g][2:], *ready[g]
        flat, w_send, w_keep = mix_call(info, first_of[g], *states_g, back, gain, cot, span, after)
        after = [w_keep]
        mixed.append(flat)
        kept.append(w_keep)
        got.append(moved(w_send, (0, 1, 0, 0)))
    output, done = finish_call(mixed, out_weight)
    scale = 1.0 / math.sqrt(count * n_shot * n_tm)

    sums = range(len(SUMS))
    orders = [(on_x + on_y if g % 2 == 0 else on_y + on_x) + on_z for g in sums]
    arrays = [[a for r in SUMS[g] for a in (kept[r], got[r])] for g in sums]
    parts = [len(SUMS[g]) for g in sums]
    previous = None
    for step in range(len(orders[0])):
        for g in sums:
            shift, where = orders[g][step]
            after = [previous] if g or step else []
            if g == sums[-1] and step == 1:
                after.append(done)
            own, send = fold_call(info, where, (0, 1), arrays[g], parts[g], after)
            arrays[g], parts[g] = [own, moved(send, shift)], 1
            previous = own
    totals = [total_call(a) for a in arrays]
    pieces = [t[0] for t in totals]
    for step in reversed(range(len(orders[0]))):
        arrived = [moved(pieces[g], orders[g][step][0]) for g in sums]
        previous = pieces[-1]
        for g in sums:
            pieces[g] = previous = lay_call(info, orders[g][step][1], pieces[g], arrived[g], [previous])
    ends = [part for piece in pieces for part in (piece, moved(piece, (0, 1, 0, 0)))]
    blocks = [[(first_of[r] + i, RELAYS[r] // 2) for r in SUMS[g] for i in range(RELAYS[r] // 2)] for g in sums]
    weight_grad, gain_grad = join_call(info, ends, [t[1] for t in totals], blocks, scale, dims, width)
    return (output.reshape(seqs, span, width), weight_grad, gain_grad.reshape(dims))


def solution(mesh):
    placed = (P("shot", "tm", None), P(), P(), P(), P(), P(), P(), P(), P(), P("shot", "tm", None))
    return jax.shard_map(
        functools.partial(shards, mesh),
        mesh=mesh,
        in_specs=placed,
        out_specs=(P("shot", "tm", None), P(), P()),
        check_vma=False,
    )
```

```python
import functools
import math

import jax
import jax.numpy as jnp
from jax import lax
from jax.experimental import pallas as pl
from jax.experimental.pallas import tpu as pltpu
from jax.sharding import PartitionSpec as P

RELAYS = (4, 4)
SUMS = ((0,), (1,))
CORES = 2
PAIR = 2
PER_STEP = 2
F32 = jnp.float32
BF16 = jnp.bfloat16
MIB = 1024 * 1024


def dot(a, b):
    return lax.dot_general(a, b, (((1,), (0,)), ((), ())), preferred_element_type=F32)


def dot_nt(a, b):
    return lax.dot_general(a, b, (((1,), (1,)), ((), ())), preferred_element_type=F32)


def dot_tn(a, b):
    return lax.dot_general(a, b, (((0,), (0,)), ((), ())), preferred_element_type=F32)


def halves(a):
    high = a.astype(BF16)
    return high, (a - high.astype(F32)).astype(BF16)


def dot3(a, b):
    ah, al = halves(a)
    bh, bl = halves(b)
    return dot(ah, bh) + (dot(ah, bl) + dot(al, bh))


def params(mib):
    return pltpu.CompilerParams(vmem_limit_bytes=mib * MIB)


def smem():
    return pl.BlockSpec(memory_space=pltpu.SMEM)


def vmem():
    return pl.BlockSpec(memory_space=pltpu.VMEM)


def whole(shape):
    return pl.BlockSpec(shape, lambda *_: (0,) * len(shape))


def anywhere(after):
    return [pl.BlockSpec(memory_space=pl.ANY)] * len(after)


def skipping(kernel, first, after):
    return lambda *refs: kernel(*refs[:first], *refs[first + len(after) :])


def cost(flops, size):
    return pl.CostEstimate(flops=flops, bytes_accessed=size, transcendentals=0)


def write_gates(span, heads, x_ref, w_ref, level_ref, out_ref):
    lane = lax.broadcasted_iota(jnp.int32, (1, heads), 1)
    rate = jnp.zeros((1, heads), F32)
    bias = jnp.zeros((1, heads), F32)
    for h in range(heads):
        rate = jnp.where(lane == h, level_ref[0, h], rate)
        bias = jnp.where(lane == h, level_ref[1, h], bias)
    gates = dot_nt(x_ref[...], w_ref[...])
    raw = gates[:, :heads]
    softplus = jnp.maximum(raw, 0.0) + jnp.log1p(jnp.exp(-jnp.abs(raw)))
    logdecay = -rate * softplus
    out_ref[:, heads : 2 * heads] = jax.nn.sigmoid(gates[:, heads:] + bias)
    row = lax.broadcasted_iota(jnp.int32, (span, span), 0)
    col = lax.broadcasted_iota(jnp.int32, (span, span), 1)
    lower = jnp.where(row >= col, 1.0, 0.0).astype(F32)
    for first in range(0, x_ref.shape[0], span):
        piece = logdecay[first : first + span]
        out_ref[first : first + span, :heads] = lax.dot_general(
            lower, piece, (((1,), (0,)), ((), ())), precision=lax.Precision.HIGHEST, preferred_element_type=F32
        )


def solve_lower(systems, rights):
    span = systems[0].shape[0]
    row = lax.broadcasted_iota(jnp.int32, (span, span), 0)
    col = lax.broadcasted_iota(jnp.int32, (span, span), 1)
    apart = row ^ col
    invs = [jnp.where(row == col, 1.0, jnp.where(apart == 1, -s, 0.0)).astype(BF16) for s in systems]
    step = 2
    while 2 * step < span:
        keep = (apart >= step) & (apart < 2 * step)
        bands = [jnp.where(keep, s, 0.0).astype(BF16) for s in systems]
        if step < 16:
            inners = [dot(i, b).astype(BF16) for i, b in zip(invs, bands)]
            invs = [i - dot(n, i).astype(BF16) for n, i in zip(inners, invs)]
        else:
            odds = [jnp.concatenate([i[r : r + step] for r in range(step, span, 2 * step)], 0) for i in invs]
            inners = [dot(o, b).astype(BF16) for o, b in zip(odds, bands)]
            news = [o - dot(n, i).astype(BF16) for o, n, i in zip(odds, inners, invs)]
            invs = [
                jnp.concatenate(
                    [
                        piece
                        for k in range(span // (2 * step))
                        for piece in (i[2 * k * step : (2 * k + 1) * step], n[k * step : (k + 1) * step])
                    ],
                    0,
                )
                for i, n in zip(invs, news)
            ]
        step *= 2
    lows = [dot(dot(i[step:, step:], s[step:, :step].astype(BF16)).astype(BF16), i[:step, :step]) for i, s in zip(invs, systems)]
    blank = jnp.zeros((step, step), BF16)
    invs = [
        jnp.concatenate(
            [jnp.concatenate([i[:step, :step], blank], 1), jnp.concatenate([-low.astype(BF16), i[step:, step:]], 1)], 0
        )
        for i, low in zip(invs, lows)
    ]
    rounded = [r.astype(BF16) for r in rights]
    firsts = [dot(i, b) + (r - b.astype(F32)) for i, b, r in zip(invs, rounded, rights)]
    residuals = [(r - f) - dot3(s, f) for r, f, s in zip(rights, firsts, systems)]
    return [f + dot(i, r.astype(BF16)) for f, i, r in zip(firsts, invs, residuals)]


def local_kernel(first_head, heads, span, per_step, opening, info, table, x_ref, pool_ref, *refs):
    if opening:
        w_ref, level_ref, own_ref, send_ref, core_ref, query_ref, gate_ref = refs

        @pl.when(pl.program_id(0) == 0)
        def _():
            write_gates(span, heads, x_ref, w_ref, level_ref, gate_ref)

    else:
        gate_ref, own_ref, send_ref, core_ref, query_ref = refs
    members = table.shape[1]
    dims = pool_ref.shape[1]
    lane = lax.broadcasted_iota(jnp.int32, (span, 2 * heads), 1)
    wide = lax.broadcasted_iota(jnp.int32, (span, dims), 1)
    row = lax.broadcasted_iota(jnp.int32, (span, span), 0)
    col = lax.broadcasted_iota(jnp.int32, (span, span), 1)
    eye = (
        lax.broadcasted_iota(jnp.int32, (dims, dims), 0) == lax.broadcasted_iota(jnp.int32, (dims, dims), 1)
    ).astype(F32)
    where = []
    heads_in = []
    for local in range(per_step):
        head = first_head + pl.program_id(0) * per_step + local
        chosen = []
        for kind in range(3):
            target = kind * heads + head
            chosen.append(jnp.concatenate([pool_ref[table[1, j, target]] for j in range(members)], 0))
        for part in range(2):
            seq = info[0] if part == 0 else 1 - info[0]
            where.append((local, part, pl.ds(pl.multiple_of(seq * span, span), span)))
            projected = []
            for kind in range(3):
                target = kind * heads + head
                picked = [
                    x_ref[where[-1][2], pl.ds(pl.multiple_of(table[0, j, target] * dims, dims), dims)]
                    for j in range(members)
                ]
                projected.append(dot(jnp.concatenate(picked, 1), chosen[kind]).astype(BF16))
            heads_in.append((head, projected))
    kept, systems, rights = [], [], []
    for (local, part, rows), (head, (query, key, value)) in zip(where, heads_in):
        key_wide = key.astype(F32)
        gates = gate_ref[rows, :]
        cumulative = jnp.sum(jnp.where(lane == head, gates, 0.0), axis=1, keepdims=True)
        beta = jnp.sum(jnp.where(lane == heads + head, gates, 0.0), axis=1, keepdims=True)
        norm = lax.rsqrt(jnp.sum(key_wide * key_wide, axis=1, keepdims=True) + 1e-06)
        across = jnp.where(wide == 0, cumulative, norm).T
        cumulative_row, norm_row = across[0:1, :], across[1:2, :]
        ratio = jnp.where(row >= col, jnp.exp(jnp.minimum(cumulative - cumulative_row, 0.0)), 0.0) * norm_row
        attend = ratio * dot_nt(query, key)
        systems.append(jnp.where(row > col, ratio * dot_nt(key, key), 0.0) * (beta * norm))
        growth = jnp.exp(cumulative)
        rights.append(jnp.concatenate([(beta * growth * norm) * key_wide, beta * value.astype(F32)], axis=1))
        last = cumulative[span - 1 : span, :]
        kept.append((query, key, attend, growth, norm * jnp.exp(last - cumulative), jnp.exp(last)))
    solutions = solve_lower(systems, rights)
    for (local, part, rows), (query, key, attend, growth, tail, final), solved in zip(where, kept, solutions):
        high, low = halves(solved * tail)
        pushed = dot_tn(key, high) + dot_tn(key, low)
        out = own_ref if part == 0 else send_ref
        out[local, :, :dims] = final * eye - pushed[:, :dims]
        out[local, :, dims:] = pushed[:, dims:]
        seen = dot3(attend, solved)
        lanes = slice(local * dims, (local + 1) * dims)
        query_ref[rows, lanes] = growth * query.astype(F32) - seen[:, :dims]
        core_ref[rows, lanes] = seen[:, dims:]


def local_call(info, table, rows, pool, extra, first_head, count_heads, heads, span, after=()):
    count, width = rows.shape
    dims = pool.shape[1]
    opening = isinstance(extra, tuple)
    maps = jax.ShapeDtypeStruct((count_heads, dims, 2 * dims), F32)
    wide = jax.ShapeDtypeStruct((count, count_heads * dims), F32)
    gates = jax.ShapeDtypeStruct((count, 2 * heads), F32)
    map_spec = pl.BlockSpec((PER_STEP, dims, 2 * dims), lambda i, *_: (i, 0, 0))
    row_spec = pl.BlockSpec((count, PER_STEP * dims), lambda i, *_: (0, i))
    if opening:
        more_in = [whole(extra[0].shape), smem()]
        more_out, more_out_specs = (gates,), (whole(gates.shape),)
    else:
        more_in, more_out, more_out_specs, extra = [whole(gates.shape)], (), (), (extra,)
    return pl.pallas_call(
        skipping(functools.partial(local_kernel, first_head, heads, span, PER_STEP, opening), 4 + len(extra), after),
        out_shape=(maps, maps, wide, wide) + more_out,
        grid_spec=pltpu.PrefetchScalarGridSpec(
            num_scalar_prefetch=2,
            grid=(count_heads // PER_STEP,),
            in_specs=[whole(rows.shape), whole(pool.shape)] + more_in + anywhere(after),
            out_specs=(map_spec, map_spec, row_spec, row_spec) + more_out_specs,
        ),
        compiler_params=params(28),
        cost_estimate=cost(count_heads * 2 * 2 * span * 256 * 256 * 24, 8 * MIB),
        name="local",
    )(info, table, rows, pool, *extra, *after)


def apply_map(maps, state):
    dims = maps.shape[0]
    return dot3(maps[:, :dims], state)


def combine_kernel(info, own_ref, got_ref, early_ref, both_ref, push_ref):
    later_is_own = info[0] == 1
    for h in range(own_ref.shape[0]):
        own, got = own_ref[h], got_ref[h]
        early = jnp.where(later_is_own, got, own)
        late = jnp.where(later_is_own, own, got)
        dims = own.shape[0]
        early_ref[h] = early
        both = apply_map(late, early)
        push = both[:, dims:] + late[:, dims:]
        both_ref[h, :, :dims] = both[:, :dims]
        both_ref[h, :, dims:] = push
        push_ref[h] = push


def combine_call(info, own, got, after=()):
    shape = jax.ShapeDtypeStruct(own.shape, F32)
    push = jax.ShapeDtypeStruct(own.shape[:2] + (own.shape[1],), F32)
    return pl.pallas_call(
        skipping(combine_kernel, 3, after),
        out_shape=(shape, shape, push),
        in_specs=[smem(), vmem(), vmem()] + anywhere(after),
        compiler_params=params(12),
        cost_estimate=cost(own.shape[0] * 6 * 128 * 128 * 256, own.size * 16),
        name="combine",
    )(info, own, got, *after)


def hop_kernel(level, info, maps_ref, got_ref, state_ref, kept_ref, out_ref):
    arrived = info[2] == level
    for h in range(maps_ref.shape[0]):
        maps = maps_ref[h]
        dims = maps.shape[0]
        state = jnp.where(arrived, got_ref[h], state_ref[h])
        kept_ref[h] = state
        out_ref[h] = apply_map(maps, state) + maps[:, dims:]


def hop_call(level, info, maps, got, state, after=()):
    shape = jax.ShapeDtypeStruct(state.shape, F32)
    return pl.pallas_call(
        skipping(functools.partial(hop_kernel, level), 4, after),
        out_shape=(shape, shape),
        in_specs=[smem(), vmem(), vmem(), vmem()] + anywhere(after),
        compiler_params=params(12),
        cost_estimate=cost(maps.shape[0] * 6 * 128 * 128 * 128, maps.size * 8),
        name="hop",
    )(info, maps, got, state, *after)


def split_kernel(level, info, maps_ref, got_ref, state_ref, keep_ref, send_ref):
    second = info[0] == 1
    arrived = info[2] == level
    for h in range(maps_ref.shape[0]):
        maps = maps_ref[h]
        state = jnp.where(arrived, got_ref[h], state_ref[h])
        dims = maps.shape[0]
        middle = apply_map(maps, state) + maps[:, dims:]
        keep_ref[h] = jnp.where(second, middle, state)
        send_ref[h] = jnp.where(second, state, middle)


def split_call(level, info, maps, got, state, after=()):
    shape = jax.ShapeDtypeStruct(state.shape, F32)
    return pl.pallas_call(
        skipping(functools.partial(split_kernel, level), 4, after),
        out_shape=(shape, shape),
        in_specs=[smem(), vmem(), vmem(), vmem()] + anywhere(after),
        compiler_params=params(12),
        cost_estimate=cost(maps.shape[0] * 6 * 128 * 128 * 128, maps.size * 8),
        name="split",
    )(info, maps, got, state, *after)


def mix_kernel(span, first_head, info, core_ref, query_ref, keep_ref, got_ref, back_ref, gain_ref, cot_ref, mixed_ref, wsend_ref, wkeep_ref):
    count = keep_ref.shape[0]
    half = count // 2
    dims = gain_ref.shape[1]
    tiles = wsend_ref.shape[0] - 1
    each = tiles // half
    stripe = dims // 8
    gain_part = jnp.zeros((8, dims), F32)
    for part in range(2):
        seq = info[0] if part == 0 else 1 - info[0]
        rows = pl.ds(pl.multiple_of(seq * span, span), span)
        for h in range(count):
            lanes = slice(h * dims, (h + 1) * dims)
            state = (keep_ref if part == 0 else got_ref)[h]
            core = core_ref[rows, lanes] + dot3(query_ref[rows, lanes], state)
            normal = core * lax.rsqrt(jnp.mean(core * core, axis=1, keepdims=True) + 1e-05)
            back = back_ref[rows, (first_head + h) * dims : (first_head + h + 1) * dims]
            gain_part += jnp.sum((normal * back).reshape(-1, 8, dims), axis=0)
            mixed_ref[rows, lanes] = (normal * gain_ref[...]).astype(BF16)
    wkeep_ref[tiles] = gain_part
    wsend_ref[tiles] = gain_part
    product = dot_tn(mixed_ref[...], cot_ref[...])
    for h in range(count):
        first = (h % half) * each
        pieces = [
            (first + i * stripe, product[h * dims : (h + 1) * dims, i * 128 : (i + 1) * 128].reshape(stripe, 8, 128))
            for i in range(product.shape[1] // 128)
        ]
        for side, ref in ((0, wkeep_ref), (1, wsend_ref)):

            @pl.when((info[1] ^ side) == h // half)
            def _(ref=ref, pieces=pieces):
                for at, piece in pieces:
                    ref[at : at + stripe] = piece


def mix_call(info, first_head, core, query, keep, got, back, gain, cot, span, after=()):
    count, width = cot.shape
    heads_here = keep.shape[0]
    dims = gain.shape[1]
    weight = jax.ShapeDtypeStruct((heads_here // 2 * dims * width // 1024 + 1, 8, 128), F32)
    return pl.pallas_call(
        skipping(functools.partial(mix_kernel, span, first_head), 8, after),
        out_shape=(jax.ShapeDtypeStruct((count, heads_here * dims), BF16), weight, weight),
        in_specs=[smem()] + [vmem()] * 7 + anywhere(after),
        out_specs=(vmem(), vmem(), vmem()),
        compiler_params=params(20),
        cost_estimate=cost(heads_here * 2 * 512 * 1024 * 128, 3 * MIB),
        name="mix",
    )(info, core, query, keep, got, back, gain, cot, *after)


def back_kernel(cot_ref, weight_ref, out_ref):
    out_ref[...] = dot_nt(cot_ref[...], weight_ref[...])


def back_call(cot, weight):
    count, width = cot.shape
    row_spec = pl.BlockSpec((128, width), lambda i: (i, 0))
    return pl.pallas_call(
        back_kernel,
        out_shape=jax.ShapeDtypeStruct((count, width), F32),
        grid=(count // 128,),
        in_specs=[row_spec, whole(weight.shape)],
        out_specs=row_spec,
        compiler_params=params(12),
        cost_estimate=cost(2 * count * width * width, 5 * MIB),
        name="back",
    )(cot, weight)


def finish_kernel(groups, *refs):
    weight_ref, out_ref, done_ref = refs[groups:]
    done_ref[...] = jnp.zeros_like(done_ref)
    stacked = jnp.concatenate([ref[...] for ref in refs[:groups]], axis=1)
    out_ref[...] = dot(stacked, weight_ref[...]).astype(BF16)


def finish_call(mixed, weight):
    count = mixed[0].shape[0]
    width = weight.shape[1]
    row_spec = pl.BlockSpec((128, width), lambda i: (i, 0))
    return pl.pallas_call(
        functools.partial(finish_kernel, len(mixed)),
        out_shape=(jax.ShapeDtypeStruct((count, width), BF16), jax.ShapeDtypeStruct((8, 128), F32)),
        grid=(count // 128,),
        in_specs=[pl.BlockSpec((128, m.shape[1]), lambda i: (i, 0)) for m in mixed] + [whole(weight.shape)],
        out_specs=(row_spec, whole((8, 128))),
        compiler_params=params(12),
        cost_estimate=cost(2 * count * width * width, 4 * MIB),
        name="finish",
    )(*mixed, weight)


def fold_kernel(parts, terms, where, flips, info, *refs):
    ins, outs = refs[: parts * terms], refs[parts * terms :]
    size = ins[0].shape[0] - 1
    share = outs[0].shape[0] - 1
    last = sum(ref[size] for ref in ins)
    for flip, out in zip(flips, outs):
        first = (info[where] ^ flip) * share
        if parts == 1:
            out[:share] = sum(ref[pl.ds(first, share)] for ref in ins)
        else:
            for part in range(parts):

                @pl.when((first >= part * size) & (first < (part + 1) * size))
                def _(part=part, out=out, first=first):
                    out[:share] = sum(ref[pl.ds(first - part * size, share)] for ref in ins[part * terms : (part + 1) * terms])

        out[share] = last


def fold_call(info, where, flips, arrays, parts, after=()):
    terms = len(arrays) // parts
    size = arrays[0].shape[0] - 1
    share = size * parts // len(flips)
    shape = jax.ShapeDtypeStruct((share + 1, 8, 128), F32)
    return pl.pallas_call(
        skipping(functools.partial(fold_kernel, parts, terms, where, flips), 1 + len(arrays), after),
        out_shape=[shape] * len(flips),
        in_specs=[smem()] + [vmem()] * len(arrays) + anywhere(after),
        compiler_params=params(12),
        cost_estimate=cost(size * 1024 * len(arrays), size * 4096 * (len(arrays) + 1)),
        name="fold",
    )(info, *arrays, *after)


def total_kernel(*refs):
    ins, (piece_ref, last_ref) = refs[:-2], refs[-2:]
    size = piece_ref.shape[0]
    piece_ref[...] = sum(ref[:size] for ref in ins)
    last_ref[...] = sum(ref[size] for ref in ins)


def total_call(arrays):
    size = arrays[0].shape[0] - 1
    return pl.pallas_call(
        total_kernel,
        out_shape=(jax.ShapeDtypeStruct((size, 8, 128), F32), jax.ShapeDtypeStruct((8, 128), F32)),
        in_specs=[vmem()] * len(arrays),
        out_specs=(vmem(), vmem()),
        compiler_params=params(12),
        cost_estimate=cost(size * 4096, size * 4096 * 5),
        name="total",
    )(*arrays)


def lay_kernel(where, info, own_ref, got_ref, out_ref):
    share = own_ref.shape[0]
    out_ref[pl.ds(info[where] * share, share)] = own_ref[...]
    out_ref[pl.ds((1 - info[where]) * share, share)] = got_ref[...]


def lay_call(info, where, own, got, after=()):
    share = own.shape[0]
    return pl.pallas_call(
        skipping(functools.partial(lay_kernel, where), 3, after),
        out_shape=jax.ShapeDtypeStruct((share * 2, 8, 128), F32),
        in_specs=[smem(), vmem(), vmem()] + anywhere(after),
        compiler_params=params(12),
        cost_estimate=cost(0, share * 16384),
        name="lay",
    )(info, own, got, *after)


def join_kernel(scale, stripe, blocks, flags, info, *refs):
    sums = len(blocks)
    lasts, (out_ref, gain_ref) = refs[4 * sums : 5 * sums], refs[-2:]
    columns = out_ref.shape[1] // 128
    dims = stripe * 8
    size = refs[0].shape[0]
    per_half = size // stripe
    for g in range(sums):
        for part in range(2):
            side = info[1] if part == 0 else 1 - info[1]
            for flip in range(2):
                ref = refs[4 * g + 2 * part + flip]
                low = info[flags[g]] == flip
                for at in range(2):

                    @pl.when(low if at == 0 else jnp.logical_not(low))
                    def _(ref=ref, at=at, side=side, g=g):
                        for index in range(per_half):
                            block, col = divmod(at * per_half + index, columns)
                            base, half = blocks[g][block]
                            rows = pl.ds(pl.multiple_of((base + side * half) * dims, dims), dims)
                            values = ref[index * stripe : (index + 1) * stripe].reshape(dims, 128) * scale
                            out_ref[rows, col * 128 : (col + 1) * 128] = values.astype(BF16)

    gain_ref[...] = jnp.sum(sum(ref[...] for ref in lasts), axis=0, keepdims=True) * scale


def join_call(info, parts, lasts, blocks, flags, scale, dims, width):
    total = sum(p.shape[0] for p in parts) * 1024 // width
    return pl.pallas_call(
        functools.partial(join_kernel, scale, dims // 8, blocks, flags),
        out_shape=(jax.ShapeDtypeStruct((total, width), BF16), jax.ShapeDtypeStruct((1, 128), F32)),
        in_specs=[smem()] + [vmem()] * (len(parts) + len(lasts)),
        out_specs=(vmem(), vmem()),
        compiler_params=params(16),
        name="join",
    )(info, *parts, *lasts)


def shards(mesh, features, weight_pool, pattern_in, pattern_pool, gate_weight, decay_rate, beta_bias, norm_gain, out_weight, cotangent):
    n_shot, n_tm = mesh.shape["shot"], mesh.shape["tm"]
    n_x, n_z = n_shot // CORES, n_tm // PAIR
    seqs, span, width = features.shape
    heads = decay_rate.shape[0]
    dims = weight_pool.shape[1]
    count = seqs * span
    both = ("shot", "tm")
    shot, tm = lax.axis_index("shot"), lax.axis_index("tm")
    x, core, z, y = shot // CORES, shot % CORES, tm // PAIR, tm % PAIR

    def place(xi, ci, zi, yi):
        return (xi * CORES + ci) * n_tm + zi * PAIR + yi

    def moved(array, shift):
        dx, dc, dz, dy = shift
        route = []
        for xi in range(n_x):
            for ci in range(CORES):
                for zi in range(n_z):
                    for yi in range(PAIR):
                        route.append((place(xi, ci, zi, yi), place(xi ^ dx, ci ^ dc, zi ^ dz, yi ^ dy)))
        return lax.ppermute(array, both, route)

    def lifted(array, level):
        ends = ((level, level + 1), (level + 1, level))
        route = [(a * PAIR + yi, b * PAIR + yi) for a, b in ends for yi in range(PAIR)]
        return lax.ppermute(array, "tm", route)

    def bits(size):
        return [1 << bit for bit in range(size.bit_length() - 1)]

    steps_x = [((reach, 0, 0, 0), (x // reach) % 2) for reach in bits(n_x)]
    steps_y = [((0, 0, 0, reach), (y // reach) % 2) for reach in bits(PAIR)]
    steps_z = [((0, 0, reach, 0), (z // reach) % 2) for reach in bits(n_z)]
    labelled = [(shift, 3 + i) for i, (shift, _) in enumerate(steps_x + steps_y + steps_z)]
    on_x, on_y = labelled[: len(steps_x)], labelled[len(steps_x) : len(steps_x) + len(steps_y)]
    on_z = labelled[len(steps_x) + len(steps_y) :]
    info = jnp.stack([y, core, z] + [bit for _, bit in steps_x + steps_y + steps_z]).astype(jnp.int32)
    table = jnp.stack([pattern_in.T, pattern_pool.T])
    levels = jnp.stack([decay_rate, beta_bias])
    rows = features.reshape(count, width)
    cot = cotangent.reshape(count, width)
    gain = norm_gain.reshape(1, dims)
    relays = range(len(RELAYS))
    last = len(RELAYS) - 1
    first_of = [sum(RELAYS[:g]) for g in relays]

    extra = (gate_weight.T, levels)
    locals_ = []
    for g in relays:
        after = [locals_[-1][0]] if g else []
        out = list(local_call(info, table, rows, weight_pool, extra, first_of[g], RELAYS[g], heads, span, after))
        if g == 0:
            extra = out.pop()
        locals_.append(out)
    back = back_call(cot, out_weight)
    maps = []
    for g in relays:
        after = [locals_[last][0]] if g == 0 else [maps[-1][2]]
        if g == last:
            after.append(back)
        maps.append(combine_call(info, locals_[g][0], moved(locals_[g][1], (0, 0, 0, 1)), after))
    states = [jnp.zeros((size, dims, dims), F32) for size in RELAYS]
    sends = [m[2] for m in maps]
    for level in range(1, n_z):
        gots = [lifted(send, level - 1) for send in sends]
        after = [sends[last]]
        if level == n_z - 1:
            break
        for g in relays:
            states[g], sends[g] = hop_call(level, info, maps[g][1], gots[g], states[g], after)
            after = [sends[g]]
    mixed, kept, got, ready = [], [], [], []
    for g in relays:
        keep, send = split_call(n_z - 1, info, maps[g][0], gots[g], states[g], after)
        after = [send]
        ready.append((keep, moved(send, (0, 0, 0, 1))))
    for g in relays:
        states_g = *locals_[g][2:], *ready[g]
        flat, w_send, w_keep = mix_call(info, first_of[g], *states_g, back, gain, cot, span, after)
        after = [w_keep]
        mixed.append(flat)
        kept.append(w_keep)
        got.append(moved(w_send, (0, 1, 0, 0)))
    output, done = finish_call(mixed, out_weight)
    scale = 1.0 / math.sqrt(count * n_shot * n_tm)

    sums = range(len(SUMS))
    orders = [(on_x + on_y if g % 2 == 0 else on_y + on_x) + on_z for g in sums]
    arrays = [[a for r in SUMS[g] for a in (kept[r], got[r])] for g in sums]
    parts = [len(SUMS[g]) for g in sums]
    previous = None
    for step in range(len(orders[0])):
        for g in sums:
            shift, where = orders[g][step]
            after = [previous] if g or step else []
            if g == sums[-1] and step == 1:
                after.append(done)
            own, send = fold_call(info, where, (0, 1), arrays[g], parts[g], after)
            arrays[g], parts[g] = [own, moved(send, shift)], 1
            previous = own
    totals = [total_call(a) for a in arrays]
    pieces = [t[0] for t in totals]
    for step in reversed(range(1, len(orders[0]))):
        arrived = [moved(pieces[g], orders[g][step][0]) for g in sums]
        previous = pieces[-1]
        for g in sums:
            pieces[g] = previous = lay_call(info, orders[g][step][1], pieces[g], arrived[g], [previous])
    ends = []
    for g in sums:
        arrived = moved(pieces[g], orders[g][0][0])
        ends += [pieces[g], arrived, moved(pieces[g], (0, 1, 0, 0)), moved(arrived, (0, 1, 0, 0))]
    flags = [orders[g][0][1] for g in sums]
    blocks = [[(first_of[r] + i, RELAYS[r] // 2) for r in SUMS[g] for i in range(RELAYS[r] // 2)] for g in sums]
    weight_grad, gain_grad = join_call(info, ends, [t[1] for t in totals], blocks, flags, scale, dims, width)
    return (output.reshape(seqs, span, width), weight_grad, gain_grad.reshape(dims))


def solution(mesh):
    placed = (P("shot", "tm", None), P(), P(), P(), P(), P(), P(), P(), P(), P("shot", "tm", None))
    return jax.shard_map(
        functools.partial(shards, mesh),
        mesh=mesh,
        in_specs=placed,
        out_specs=(P("shot", "tm", None), P(), P()),
        check_vma=False,
    )
```

```python
import functools
import math

import jax
import jax.numpy as jnp
from jax import lax
from jax.experimental import pallas as pl
from jax.experimental.pallas import tpu as pltpu
from jax.sharding import PartitionSpec as P

RELAYS = (4, 4)
SUMS = ((0,), (1,))
CORES = 2
PAIR = 2
PER_STEP = 2
DELAYS = (0, 1)
LIGHT = False
F32 = jnp.float32
BF16 = jnp.bfloat16
MIB = 1024 * 1024


def dot(a, b):
    return lax.dot_general(a, b, (((1,), (0,)), ((), ())), preferred_element_type=F32)


def dot_nt(a, b):
    return lax.dot_general(a, b, (((1,), (1,)), ((), ())), preferred_element_type=F32)


def dot_tn(a, b):
    return lax.dot_general(a, b, (((0,), (0,)), ((), ())), preferred_element_type=F32)


def halves(a):
    high = a.astype(BF16)
    return high, (a - high.astype(F32)).astype(BF16)


def dot3(a, b):
    ah, al = halves(a)
    bh, bl = halves(b)
    return dot(ah, bh) + (dot(ah, bl) + dot(al, bh))


def params(mib):
    return pltpu.CompilerParams(vmem_limit_bytes=mib * MIB)


def smem():
    return pl.BlockSpec(memory_space=pltpu.SMEM)


def vmem():
    return pl.BlockSpec(memory_space=pltpu.VMEM)


def whole(shape):
    return pl.BlockSpec(shape, lambda *_: (0,) * len(shape))


def anywhere(after):
    return [pl.BlockSpec(memory_space=pl.ANY)] * len(after)


def skipping(kernel, first, after):
    return lambda *refs: kernel(*refs[:first], *refs[first + len(after) :])


def light(flops, size):
    return cost(1, 1) if LIGHT else cost(flops, size)


def cost(flops, size):
    return pl.CostEstimate(flops=flops, bytes_accessed=size, transcendentals=0)


def write_gates(span, heads, x_ref, w_ref, level_ref, out_ref):
    lane = lax.broadcasted_iota(jnp.int32, (1, heads), 1)
    rate = jnp.zeros((1, heads), F32)
    bias = jnp.zeros((1, heads), F32)
    for h in range(heads):
        rate = jnp.where(lane == h, level_ref[0, h], rate)
        bias = jnp.where(lane == h, level_ref[1, h], bias)
    gates = dot_nt(x_ref[...], w_ref[...])
    raw = gates[:, :heads]
    softplus = jnp.maximum(raw, 0.0) + jnp.log1p(jnp.exp(-jnp.abs(raw)))
    logdecay = -rate * softplus
    out_ref[:, heads : 2 * heads] = jax.nn.sigmoid(gates[:, heads:] + bias)
    row = lax.broadcasted_iota(jnp.int32, (span, span), 0)
    col = lax.broadcasted_iota(jnp.int32, (span, span), 1)
    lower = jnp.where(row >= col, 1.0, 0.0).astype(F32)
    for first in range(0, x_ref.shape[0], span):
        piece = logdecay[first : first + span]
        out_ref[first : first + span, :heads] = lax.dot_general(
            lower, piece, (((1,), (0,)), ((), ())), precision=lax.Precision.HIGHEST, preferred_element_type=F32
        )


def solve_lower(systems, rights):
    span = systems[0].shape[0]
    row = lax.broadcasted_iota(jnp.int32, (span, span), 0)
    col = lax.broadcasted_iota(jnp.int32, (span, span), 1)
    apart = row ^ col
    invs = [jnp.where(row == col, 1.0, jnp.where(apart == 1, -s, 0.0)).astype(BF16) for s in systems]
    step = 2
    while 2 * step < span:
        keep = (apart >= step) & (apart < 2 * step)
        bands = [jnp.where(keep, s, 0.0).astype(BF16) for s in systems]
        if step < 16:
            inners = [dot(i, b).astype(BF16) for i, b in zip(invs, bands)]
            invs = [i - dot(n, i).astype(BF16) for n, i in zip(inners, invs)]
        else:
            odds = [jnp.concatenate([i[r : r + step] for r in range(step, span, 2 * step)], 0) for i in invs]
            inners = [dot(o, b).astype(BF16) for o, b in zip(odds, bands)]
            news = [o - dot(n, i).astype(BF16) for o, n, i in zip(odds, inners, invs)]
            invs = [
                jnp.concatenate(
                    [
                        piece
                        for k in range(span // (2 * step))
                        for piece in (i[2 * k * step : (2 * k + 1) * step], n[k * step : (k + 1) * step])
                    ],
                    0,
                )
                for i, n in zip(invs, news)
            ]
        step *= 2
    lows = [dot(dot(i[step:, step:], s[step:, :step].astype(BF16)).astype(BF16), i[:step, :step]) for i, s in zip(invs, systems)]
    blank = jnp.zeros((step, step), BF16)
    invs = [
        jnp.concatenate(
            [jnp.concatenate([i[:step, :step], blank], 1), jnp.concatenate([-low.astype(BF16), i[step:, step:]], 1)], 0
        )
        for i, low in zip(invs, lows)
    ]
    rounded = [r.astype(BF16) for r in rights]
    firsts = [dot(i, b) + (r - b.astype(F32)) for i, b, r in zip(invs, rounded, rights)]
    residuals = [(r - f) - dot3(s, f) for r, f, s in zip(rights, firsts, systems)]
    return [f + dot(i, r.astype(BF16)) for f, i, r in zip(firsts, invs, residuals)]


def local_kernel(first_head, heads, span, per_step, opening, info, table, x_ref, pool_ref, *refs):
    if opening:
        w_ref, level_ref, own_ref, send_ref, core_ref, query_ref, gate_ref = refs

        @pl.when(pl.program_id(0) == 0)
        def _():
            write_gates(span, heads, x_ref, w_ref, level_ref, gate_ref)

    else:
        gate_ref, own_ref, send_ref, core_ref, query_ref = refs
    members = table.shape[1]
    dims = pool_ref.shape[1]
    lane = lax.broadcasted_iota(jnp.int32, (span, 2 * heads), 1)
    wide = lax.broadcasted_iota(jnp.int32, (span, dims), 1)
    row = lax.broadcasted_iota(jnp.int32, (span, span), 0)
    col = lax.broadcasted_iota(jnp.int32, (span, span), 1)
    eye = (
        lax.broadcasted_iota(jnp.int32, (dims, dims), 0) == lax.broadcasted_iota(jnp.int32, (dims, dims), 1)
    ).astype(F32)
    where = []
    heads_in = []
    for local in range(per_step):
        head = first_head + pl.program_id(0) * per_step + local
        chosen = []
        for kind in range(3):
            target = kind * heads + head
            chosen.append(jnp.concatenate([pool_ref[table[1, j, target]] for j in range(members)], 0))
        for part in range(2):
            seq = info[0] if part == 0 else 1 - info[0]
            where.append((local, part, pl.ds(pl.multiple_of(seq * span, span), span)))
            projected = []
            for kind in range(3):
                target = kind * heads + head
                picked = [
                    x_ref[where[-1][2], pl.ds(pl.multiple_of(table[0, j, target] * dims, dims), dims)]
                    for j in range(members)
                ]
                projected.append(dot(jnp.concatenate(picked, 1), chosen[kind]).astype(BF16))
            heads_in.append((head, projected))
    kept, systems, rights = [], [], []
    for (local, part, rows), (head, (query, key, value)) in zip(where, heads_in):
        key_wide = key.astype(F32)
        gates = gate_ref[rows, :]
        cumulative = jnp.sum(jnp.where(lane == head, gates, 0.0), axis=1, keepdims=True)
        beta = jnp.sum(jnp.where(lane == heads + head, gates, 0.0), axis=1, keepdims=True)
        norm = lax.rsqrt(jnp.sum(key_wide * key_wide, axis=1, keepdims=True) + 1e-06)
        across = jnp.where(wide == 0, cumulative, norm).T
        cumulative_row, norm_row = across[0:1, :], across[1:2, :]
        ratio = jnp.where(row >= col, jnp.exp(jnp.minimum(cumulative - cumulative_row, 0.0)), 0.0) * norm_row
        attend = ratio * dot_nt(query, key)
        systems.append(jnp.where(row > col, ratio * dot_nt(key, key), 0.0) * (beta * norm))
        growth = jnp.exp(cumulative)
        rights.append(jnp.concatenate([(beta * growth * norm) * key_wide, beta * value.astype(F32)], axis=1))
        last = cumulative[span - 1 : span, :]
        kept.append((query, key, attend, growth, norm * jnp.exp(last - cumulative), jnp.exp(last)))
    solutions = solve_lower(systems, rights)
    for (local, part, rows), (query, key, attend, growth, tail, final), solved in zip(where, kept, solutions):
        high, low = halves(solved * tail)
        pushed = dot_tn(key, high) + dot_tn(key, low)
        out = own_ref if part == 0 else send_ref
        out[local, :, :dims] = final * eye - pushed[:, :dims]
        out[local, :, dims:] = pushed[:, dims:]
        seen = dot3(attend, solved)
        lanes = slice(local * dims, (local + 1) * dims)
        query_ref[rows, lanes] = growth * query.astype(F32) - seen[:, :dims]
        core_ref[rows, lanes] = seen[:, dims:]


def local_call(info, table, rows, pool, extra, first_head, count_heads, heads, span, after=()):
    count, width = rows.shape
    dims = pool.shape[1]
    opening = isinstance(extra, tuple)
    maps = jax.ShapeDtypeStruct((count_heads, dims, 2 * dims), F32)
    wide = jax.ShapeDtypeStruct((count, count_heads * dims), F32)
    gates = jax.ShapeDtypeStruct((count, 2 * heads), F32)
    map_spec = pl.BlockSpec((PER_STEP, dims, 2 * dims), lambda i, *_: (i, 0, 0))
    row_spec = pl.BlockSpec((count, PER_STEP * dims), lambda i, *_: (0, i))
    if opening:
        more_in = [whole(extra[0].shape), smem()]
        more_out, more_out_specs = (gates,), (whole(gates.shape),)
    else:
        more_in, more_out, more_out_specs, extra = [whole(gates.shape)], (), (), (extra,)
    return pl.pallas_call(
        skipping(functools.partial(local_kernel, first_head, heads, span, PER_STEP, opening), 4 + len(extra), after),
        out_shape=(maps, maps, wide, wide) + more_out,
        grid_spec=pltpu.PrefetchScalarGridSpec(
            num_scalar_prefetch=2,
            grid=(count_heads // PER_STEP,),
            in_specs=[whole(rows.shape), whole(pool.shape)] + more_in + anywhere(after),
            out_specs=(map_spec, map_spec, row_spec, row_spec) + more_out_specs,
        ),
        compiler_params=params(28),
        cost_estimate=cost(count_heads * 2 * 2 * span * 256 * 256 * 24, 8 * MIB),
        name="local",
    )(info, table, rows, pool, *extra, *after)


def apply_map(maps, state):
    dims = maps.shape[0]
    return dot3(maps[:, :dims], state)


def combine_kernel(info, own_ref, got_ref, early_ref, both_ref, push_ref):
    later_is_own = info[0] == 1
    for h in range(own_ref.shape[0]):
        own, got = own_ref[h], got_ref[h]
        early = jnp.where(later_is_own, got, own)
        late = jnp.where(later_is_own, own, got)
        dims = own.shape[0]
        early_ref[h] = early
        both = apply_map(late, early)
        push = both[:, dims:] + late[:, dims:]
        both_ref[h, :, :dims] = both[:, :dims]
        both_ref[h, :, dims:] = push
        push_ref[h] = push


def combine_call(info, own, got, after=()):
    shape = jax.ShapeDtypeStruct(own.shape, F32)
    push = jax.ShapeDtypeStruct(own.shape[:2] + (own.shape[1],), F32)
    return pl.pallas_call(
        skipping(combine_kernel, 3, after),
        out_shape=(shape, shape, push),
        in_specs=[smem(), vmem(), vmem()] + anywhere(after),
        compiler_params=params(12),
        cost_estimate=light(own.shape[0] * 6 * 128 * 128 * 256, own.size * 16),
        name="combine",
    )(info, own, got, *after)


def hop_kernel(level, info, maps_ref, got_ref, state_ref, kept_ref, out_ref):
    arrived = info[2] == level
    for h in range(maps_ref.shape[0]):
        maps = maps_ref[h]
        dims = maps.shape[0]
        state = jnp.where(arrived, got_ref[h], state_ref[h])
        kept_ref[h] = state
        out_ref[h] = apply_map(maps, state) + maps[:, dims:]


def hop_call(level, info, maps, got, state, after=()):
    shape = jax.ShapeDtypeStruct(state.shape, F32)
    return pl.pallas_call(
        skipping(functools.partial(hop_kernel, level), 4, after),
        out_shape=(shape, shape),
        in_specs=[smem(), vmem(), vmem(), vmem()] + anywhere(after),
        compiler_params=params(12),
        cost_estimate=light(maps.shape[0] * 6 * 128 * 128 * 128, maps.size * 8),
        name="hop",
    )(info, maps, got, state, *after)


def split_kernel(level, info, maps_ref, got_ref, state_ref, keep_ref, send_ref):
    second = info[0] == 1
    arrived = info[2] == level
    for h in range(maps_ref.shape[0]):
        maps = maps_ref[h]
        state = jnp.where(arrived, got_ref[h], state_ref[h])
        dims = maps.shape[0]
        middle = apply_map(maps, state) + maps[:, dims:]
        keep_ref[h] = jnp.where(second, middle, state)
        send_ref[h] = jnp.where(second, state, middle)


def split_call(level, info, maps, got, state, after=()):
    shape = jax.ShapeDtypeStruct(state.shape, F32)
    return pl.pallas_call(
        skipping(functools.partial(split_kernel, level), 4, after),
        out_shape=(shape, shape),
        in_specs=[smem(), vmem(), vmem(), vmem()] + anywhere(after),
        compiler_params=params(12),
        cost_estimate=light(maps.shape[0] * 6 * 128 * 128 * 128, maps.size * 8),
        name="split",
    )(info, maps, got, state, *after)


def mix_kernel(span, first_head, info, core_ref, query_ref, keep_ref, got_ref, back_ref, gain_ref, cot_ref, mixed_ref, wsend_ref, wkeep_ref):
    count = keep_ref.shape[0]
    half = count // 2
    dims = gain_ref.shape[1]
    tiles = wsend_ref.shape[0] - 1
    each = tiles // half
    stripe = dims // 8
    gain_part = jnp.zeros((8, dims), F32)
    for part in range(2):
        seq = info[0] if part == 0 else 1 - info[0]
        rows = pl.ds(pl.multiple_of(seq * span, span), span)
        for h in range(count):
            lanes = slice(h * dims, (h + 1) * dims)
            state = (keep_ref if part == 0 else got_ref)[h]
            core = core_ref[rows, lanes] + dot3(query_ref[rows, lanes], state)
            normal = core * lax.rsqrt(jnp.mean(core * core, axis=1, keepdims=True) + 1e-05)
            back = back_ref[rows, (first_head + h) * dims : (first_head + h + 1) * dims]
            gain_part += jnp.sum((normal * back).reshape(-1, 8, dims), axis=0)
            mixed_ref[rows, lanes] = (normal * gain_ref[...]).astype(BF16)
    wkeep_ref[tiles] = gain_part
    wsend_ref[tiles] = gain_part
    product = dot_tn(mixed_ref[...], cot_ref[...])
    for h in range(count):
        first = (h % half) * each
        pieces = [
            (first + i * stripe, product[h * dims : (h + 1) * dims, i * 128 : (i + 1) * 128].reshape(stripe, 8, 128))
            for i in range(product.shape[1] // 128)
        ]
        for side, ref in ((0, wkeep_ref), (1, wsend_ref)):

            @pl.when((info[1] ^ side) == h // half)
            def _(ref=ref, pieces=pieces):
                for at, piece in pieces:
                    ref[at : at + stripe] = piece


def mix_call(info, first_head, core, query, keep, got, back, gain, cot, span, after=()):
    count, width = cot.shape
    heads_here = keep.shape[0]
    dims = gain.shape[1]
    weight = jax.ShapeDtypeStruct((heads_here // 2 * dims * width // 1024 + 1, 8, 128), F32)
    return pl.pallas_call(
        skipping(functools.partial(mix_kernel, span, first_head), 8, after),
        out_shape=(jax.ShapeDtypeStruct((count, heads_here * dims), BF16), weight, weight),
        in_specs=[smem()] + [vmem()] * 7 + anywhere(after),
        out_specs=(vmem(), vmem(), vmem()),
        compiler_params=params(20),
        cost_estimate=cost(heads_here * 2 * 512 * 1024 * 128, 3 * MIB),
        name="mix",
    )(info, core, query, keep, got, back, gain, cot, *after)


def back_kernel(cot_ref, weight_ref, out_ref):
    out_ref[...] = dot_nt(cot_ref[...], weight_ref[...])


def back_call(cot, weight):
    count, width = cot.shape
    row_spec = pl.BlockSpec((128, width), lambda i: (i, 0))
    return pl.pallas_call(
        back_kernel,
        out_shape=jax.ShapeDtypeStruct((count, width), F32),
        grid=(count // 128,),
        in_specs=[row_spec, whole(weight.shape)],
        out_specs=row_spec,
        compiler_params=params(12),
        cost_estimate=cost(2 * count * width * width, 5 * MIB),
        name="back",
    )(cot, weight)


def finish_kernel(groups, *refs):
    weight_ref, out_ref, done_ref = refs[groups:]
    done_ref[...] = jnp.zeros_like(done_ref)
    stacked = jnp.concatenate([ref[...] for ref in refs[:groups]], axis=1)
    out_ref[...] = dot(stacked, weight_ref[...]).astype(BF16)


def finish_call(mixed, weight):
    count = mixed[0].shape[0]
    width = weight.shape[1]
    row_spec = pl.BlockSpec((128, width), lambda i: (i, 0))
    return pl.pallas_call(
        functools.partial(finish_kernel, len(mixed)),
        out_shape=(jax.ShapeDtypeStruct((count, width), BF16), jax.ShapeDtypeStruct((8, 128), F32)),
        grid=(count // 128,),
        in_specs=[pl.BlockSpec((128, m.shape[1]), lambda i: (i, 0)) for m in mixed] + [whole(weight.shape)],
        out_specs=(row_spec, whole((8, 128))),
        compiler_params=params(12),
        cost_estimate=cost(2 * count * width * width, 4 * MIB),
        name="finish",
    )(*mixed, weight)


def fold_kernel(parts, terms, where, flips, info, *refs):
    ins, outs = refs[: parts * terms], refs[parts * terms :]
    size = ins[0].shape[0] - 1
    share = outs[0].shape[0] - 1
    last = sum(ref[size] for ref in ins)
    for flip, out in zip(flips, outs):
        first = (info[where] ^ flip) * share
        if parts == 1:
            out[:share] = sum(ref[pl.ds(first, share)] for ref in ins)
        else:
            for part in range(parts):

                @pl.when((first >= part * size) & (first < (part + 1) * size))
                def _(part=part, out=out, first=first):
                    out[:share] = sum(ref[pl.ds(first - part * size, share)] for ref in ins[part * terms : (part + 1) * terms])

        out[share] = last


def fold_call(info, where, flips, arrays, parts, after=()):
    terms = len(arrays) // parts
    size = arrays[0].shape[0] - 1
    share = size * parts // len(flips)
    shape = jax.ShapeDtypeStruct((share + 1, 8, 128), F32)
    return pl.pallas_call(
        skipping(functools.partial(fold_kernel, parts, terms, where, flips), 1 + len(arrays), after),
        out_shape=[shape] * len(flips),
        in_specs=[smem()] + [vmem()] * len(arrays) + anywhere(after),
        compiler_params=params(12),
        cost_estimate=light(size * 1024 * len(arrays), size * 4096 * (len(arrays) + 1)),
        name="fold",
    )(info, *arrays, *after)


def total_kernel(*refs):
    ins, (piece_ref, last_ref) = refs[:-2], refs[-2:]
    size = piece_ref.shape[0]
    piece_ref[...] = sum(ref[:size] for ref in ins)
    last_ref[...] = sum(ref[size] for ref in ins)


def total_call(arrays):
    size = arrays[0].shape[0] - 1
    return pl.pallas_call(
        total_kernel,
        out_shape=(jax.ShapeDtypeStruct((size, 8, 128), F32), jax.ShapeDtypeStruct((8, 128), F32)),
        in_specs=[vmem()] * len(arrays),
        out_specs=(vmem(), vmem()),
        compiler_params=params(12),
        cost_estimate=light(size * 4096, size * 4096 * 5),
        name="total",
    )(*arrays)


def lay_kernel(where, info, own_ref, got_ref, out_ref):
    share = own_ref.shape[0]
    out_ref[pl.ds(info[where] * share, share)] = own_ref[...]
    out_ref[pl.ds((1 - info[where]) * share, share)] = got_ref[...]


def lay_call(info, where, own, got, after=()):
    share = own.shape[0]
    return pl.pallas_call(
        skipping(functools.partial(lay_kernel, where), 3, after),
        out_shape=jax.ShapeDtypeStruct((share * 2, 8, 128), F32),
        in_specs=[smem(), vmem(), vmem()] + anywhere(after),
        compiler_params=params(12),
        cost_estimate=light(0, share * 16384),
        name="lay",
    )(info, own, got, *after)


def join_kernel(scale, stripe, blocks, flags, info, *refs):
    sums = len(blocks)
    lasts, (out_ref, gain_ref) = refs[4 * sums : 5 * sums], refs[-2:]
    columns = out_ref.shape[1] // 128
    dims = stripe * 8
    size = refs[0].shape[0]
    per_half = size // stripe
    for g in range(sums):
        for part in range(2):
            side = info[1] if part == 0 else 1 - info[1]
            for flip in range(2):
                ref = refs[4 * g + 2 * part + flip]
                low = info[flags[g]] == flip
                for at in range(2):

                    @pl.when(low if at == 0 else jnp.logical_not(low))
                    def _(ref=ref, at=at, side=side, g=g):
                        for index in range(per_half):
                            block, col = divmod(at * per_half + index, columns)
                            base, half = blocks[g][block]
                            rows = pl.ds(pl.multiple_of((base + side * half) * dims, dims), dims)
                            values = ref[index * stripe : (index + 1) * stripe].reshape(dims, 128) * scale
                            out_ref[rows, col * 128 : (col + 1) * 128] = values.astype(BF16)

    gain_ref[...] = jnp.sum(sum(ref[...] for ref in lasts), axis=0, keepdims=True) * scale


def join_call(info, parts, lasts, blocks, flags, scale, dims, width):
    total = sum(p.shape[0] for p in parts) * 1024 // width
    return pl.pallas_call(
        functools.partial(join_kernel, scale, dims // 8, blocks, flags),
        out_shape=(jax.ShapeDtypeStruct((total, width), BF16), jax.ShapeDtypeStruct((1, 128), F32)),
        in_specs=[smem()] + [vmem()] * (len(parts) + len(lasts)),
        out_specs=(vmem(), vmem()),
        compiler_params=params(16),
        name="join",
    )(info, *parts, *lasts)


def shards(mesh, features, weight_pool, pattern_in, pattern_pool, gate_weight, decay_rate, beta_bias, norm_gain, out_weight, cotangent):
    n_shot, n_tm = mesh.shape["shot"], mesh.shape["tm"]
    n_x, n_z = n_shot // CORES, n_tm // PAIR
    seqs, span, width = features.shape
    heads = decay_rate.shape[0]
    dims = weight_pool.shape[1]
    count = seqs * span
    both = ("shot", "tm")
    shot, tm = lax.axis_index("shot"), lax.axis_index("tm")
    x, core, z, y = shot // CORES, shot % CORES, tm // PAIR, tm % PAIR

    def place(xi, ci, zi, yi):
        return (xi * CORES + ci) * n_tm + zi * PAIR + yi

    def moved(array, shift):
        dx, dc, dz, dy = shift
        route = []
        for xi in range(n_x):
            for ci in range(CORES):
                for zi in range(n_z):
                    for yi in range(PAIR):
                        route.append((place(xi, ci, zi, yi), place(xi ^ dx, ci ^ dc, zi ^ dz, yi ^ dy)))
        return lax.ppermute(array, both, route)

    def lifted(array, level):
        ends = ((level, level + 1), (level + 1, level))
        route = [(a * PAIR + yi, b * PAIR + yi) for a, b in ends for yi in range(PAIR)]
        return lax.ppermute(array, "tm", route)

    def bits(size):
        return [1 << bit for bit in range(size.bit_length() - 1)]

    steps_x = [((reach, 0, 0, 0), (x // reach) % 2) for reach in bits(n_x)]
    steps_y = [((0, 0, 0, reach), (y // reach) % 2) for reach in bits(PAIR)]
    steps_z = [((0, 0, reach, 0), (z // reach) % 2) for reach in bits(n_z)]
    labelled = [(shift, 3 + i) for i, (shift, _) in enumerate(steps_x + steps_y + steps_z)]
    on_x, on_y = labelled[: len(steps_x)], labelled[len(steps_x) : len(steps_x) + len(steps_y)]
    on_z = labelled[len(steps_x) + len(steps_y) :]
    info = jnp.stack([y, core, z] + [bit for _, bit in steps_x + steps_y + steps_z]).astype(jnp.int32)
    table = jnp.stack([pattern_in.T, pattern_pool.T])
    levels = jnp.stack([decay_rate, beta_bias])
    rows = features.reshape(count, width)
    cot = cotangent.reshape(count, width)
    gain = norm_gain.reshape(1, dims)
    relays = range(len(RELAYS))
    last = len(RELAYS) - 1
    first_of = [sum(RELAYS[:g]) for g in relays]

    extra = (gate_weight.T, levels)
    locals_ = []
    for g in relays:
        after = [locals_[-1][0]] if g else []
        out = list(local_call(info, table, rows, weight_pool, extra, first_of[g], RELAYS[g], heads, span, after))
        if g == 0:
            extra = out.pop()
        locals_.append(out)
    back = back_call(cot, out_weight)
    maps = [None] * len(RELAYS)
    states = [jnp.zeros((size, dims, dims), F32) for size in RELAYS]
    sends = [None] * len(RELAYS)
    ready = [None] * len(RELAYS)
    turns = sorted((stage + DELAYS[g], g, stage) for g in relays for stage in range(n_z))
    after = [locals_[last][0]]
    for _, g, stage in turns:
        if stage == 0:
            if g == last:
                after.append(back)
            maps[g] = combine_call(info, locals_[g][0], moved(locals_[g][1], (0, 0, 0, 1)), after)
            sends[g] = maps[g][2]
        else:
            came = lifted(sends[g], stage - 1)
            if stage < n_z - 1:
                states[g], sends[g] = hop_call(stage, info, maps[g][1], came, states[g], after)
            else:
                keep, sends[g] = split_call(stage, info, maps[g][0], came, states[g], after)
                ready[g] = (keep, moved(sends[g], (0, 0, 0, 1)))
        after = [sends[g]]
    sums = range(len(SUMS))
    orders = [(on_x + on_y if g % 2 == 0 else on_y + on_x) + on_z for g in sums]
    mixed, arrays, parts = [], [], []
    for group in SUMS:
        terms = []
        for g in group:
            states_g = *locals_[g][2:], *ready[g]
            flat, w_send, w_keep = mix_call(info, first_of[g], *states_g, back, gain, cot, span, after)
            after = [w_keep]
            mixed.append(flat)
            terms += [w_keep, moved(w_send, (0, 1, 0, 0))]
        arrays.append(terms)
    for g in sums:
        shift, where = orders[g][0]
        own, send = fold_call(info, where, (0, 1), arrays[g], len(SUMS[g]), after)
        after = [own]
        arrays[g] = [own, moved(send, shift)]
    output, done = finish_call(mixed, out_weight)
    scale = 1.0 / math.sqrt(count * n_shot * n_tm)

    previous = after[0]
    for step in range(1, len(orders[0])):
        for g in sums:
            shift, where = orders[g][step]
            after = [previous]
            if g == sums[-1] and step == 1:
                after.append(done)
            own, send = fold_call(info, where, (0, 1), arrays[g], 1, after)
            arrays[g] = [own, moved(send, shift)]
            previous = own
    totals = [total_call(a) for a in arrays]
    pieces = [t[0] for t in totals]
    for step in reversed(range(1, len(orders[0]))):
        arrived = [moved(pieces[g], orders[g][step][0]) for g in sums]
        previous = pieces[-1]
        for g in sums:
            pieces[g] = previous = lay_call(info, orders[g][step][1], pieces[g], arrived[g], [previous])
    ends = []
    for g in sums:
        arrived = moved(pieces[g], orders[g][0][0])
        ends += [pieces[g], arrived, moved(pieces[g], (0, 1, 0, 0)), moved(arrived, (0, 1, 0, 0))]
    flags = [orders[g][0][1] for g in sums]
    blocks = [[(first_of[r] + i, RELAYS[r] // 2) for r in SUMS[g] for i in range(RELAYS[r] // 2)] for g in sums]
    weight_grad, gain_grad = join_call(info, ends, [t[1] for t in totals], blocks, flags, scale, dims, width)
    return (output.reshape(seqs, span, width), weight_grad, gain_grad.reshape(dims))


def solution(mesh):
    placed = (P("shot", "tm", None), P(), P(), P(), P(), P(), P(), P(), P(), P("shot", "tm", None))
    return jax.shard_map(
        functools.partial(shards, mesh),
        mesh=mesh,
        in_specs=placed,
        out_specs=(P("shot", "tm", None), P(), P()),
        check_vma=False,
    )
```

```python
import functools
import math

import jax
import jax.numpy as jnp
from jax import lax
from jax.experimental import pallas as pl
from jax.experimental.pallas import tpu as pltpu
from jax.sharding import PartitionSpec as P

RELAYS = (4, 4)
SUMS = ((0,), (1,))
CORES = 2
PAIR = 2
PER_STEP = 2
DELAYS = (0, 1)
LIGHT = False
F32 = jnp.float32
BF16 = jnp.bfloat16
MIB = 1024 * 1024


def dot(a, b):
    return lax.dot_general(a, b, (((1,), (0,)), ((), ())), preferred_element_type=F32)


def dot_nt(a, b):
    return lax.dot_general(a, b, (((1,), (1,)), ((), ())), preferred_element_type=F32)


def dot_tn(a, b):
    return lax.dot_general(a, b, (((0,), (0,)), ((), ())), preferred_element_type=F32)


def halves(a):
    high = a.astype(BF16)
    return high, (a - high.astype(F32)).astype(BF16)


def dot3(a, b):
    ah, al = halves(a)
    bh, bl = halves(b)
    return dot(ah, bh) + (dot(ah, bl) + dot(al, bh))


def params(mib):
    return pltpu.CompilerParams(vmem_limit_bytes=mib * MIB)


def smem():
    return pl.BlockSpec(memory_space=pltpu.SMEM)


def vmem():
    return pl.BlockSpec(memory_space=pltpu.VMEM)


def whole(shape):
    return pl.BlockSpec(shape, lambda *_: (0,) * len(shape))


def anywhere(after):
    return [pl.BlockSpec(memory_space=pl.ANY)] * len(after)


def skipping(kernel, first, after):
    return lambda *refs: kernel(*refs[:first], *refs[first + len(after) :])


def light(flops, size):
    return cost(1, 1) if LIGHT else cost(flops, size)


def cost(flops, size):
    return pl.CostEstimate(flops=flops, bytes_accessed=size, transcendentals=0)


def write_gates(span, heads, x_ref, w_ref, level_ref, out_ref):
    lane = lax.broadcasted_iota(jnp.int32, (1, heads), 1)
    rate = jnp.zeros((1, heads), F32)
    bias = jnp.zeros((1, heads), F32)
    for h in range(heads):
        rate = jnp.where(lane == h, level_ref[0, h], rate)
        bias = jnp.where(lane == h, level_ref[1, h], bias)
    gates = dot_nt(x_ref[...], w_ref[...])
    raw = gates[:, :heads]
    softplus = jnp.maximum(raw, 0.0) + jnp.log1p(jnp.exp(-jnp.abs(raw)))
    logdecay = -rate * softplus
    out_ref[:, heads : 2 * heads] = jax.nn.sigmoid(gates[:, heads:] + bias)
    row = lax.broadcasted_iota(jnp.int32, (span, span), 0)
    col = lax.broadcasted_iota(jnp.int32, (span, span), 1)
    lower = jnp.where(row >= col, 1.0, 0.0).astype(BF16)
    high, rest = halves(logdecay)
    low = (logdecay - high.astype(F32) - rest.astype(F32)).astype(BF16)
    for first in range(0, x_ref.shape[0], span):
        here = slice(first, first + span)
        out_ref[here, :heads] = dot(lower, high[here]) + (dot(lower, rest[here]) + dot(lower, low[here]))


def solve_lower(systems, rights):
    span = systems[0].shape[0]
    row = lax.broadcasted_iota(jnp.int32, (span, span), 0)
    col = lax.broadcasted_iota(jnp.int32, (span, span), 1)
    apart = row ^ col
    invs = [jnp.where(row == col, 1.0, jnp.where(apart == 1, -s, 0.0)).astype(BF16) for s in systems]
    step = 2
    while 2 * step < span:
        keep = (apart >= step) & (apart < 2 * step)
        bands = [jnp.where(keep, s, 0.0).astype(BF16) for s in systems]
        if step < 16:
            inners = [dot(i, b).astype(BF16) for i, b in zip(invs, bands)]
            invs = [i - dot(n, i).astype(BF16) for n, i in zip(inners, invs)]
        else:
            odds = [jnp.concatenate([i[r : r + step] for r in range(step, span, 2 * step)], 0) for i in invs]
            inners = [dot(o, b).astype(BF16) for o, b in zip(odds, bands)]
            news = [o - dot(n, i).astype(BF16) for o, n, i in zip(odds, inners, invs)]
            invs = [
                jnp.concatenate(
                    [
                        piece
                        for k in range(span // (2 * step))
                        for piece in (i[2 * k * step : (2 * k + 1) * step], n[k * step : (k + 1) * step])
                    ],
                    0,
                )
                for i, n in zip(invs, news)
            ]
        step *= 2
    lows = [dot(dot(i[step:, step:], s[step:, :step].astype(BF16)).astype(BF16), i[:step, :step]) for i, s in zip(invs, systems)]
    blank = jnp.zeros((step, step), BF16)
    invs = [
        jnp.concatenate(
            [jnp.concatenate([i[:step, :step], blank], 1), jnp.concatenate([-low.astype(BF16), i[step:, step:]], 1)], 0
        )
        for i, low in zip(invs, lows)
    ]
    rounded = [r.astype(BF16) for r in rights]
    firsts = [dot(i, b) + (r - b.astype(F32)) for i, b, r in zip(invs, rounded, rights)]
    residuals = [(r - f) - dot3(s, f) for r, f, s in zip(rights, firsts, systems)]
    return [f + dot(i, r.astype(BF16)) for f, i, r in zip(firsts, invs, residuals)]


def local_kernel(first_head, heads, span, per_step, opening, info, table, x_ref, pool_ref, *refs):
    if opening:
        w_ref, level_ref, own_ref, send_ref, core_ref, query_ref, gate_ref = refs

        @pl.when(pl.program_id(0) == 0)
        def _():
            write_gates(span, heads, x_ref, w_ref, level_ref, gate_ref)

    else:
        gate_ref, own_ref, send_ref, core_ref, query_ref = refs
    members = table.shape[1]
    dims = pool_ref.shape[1]
    lane = lax.broadcasted_iota(jnp.int32, (span, 2 * heads), 1)
    wide = lax.broadcasted_iota(jnp.int32, (span, dims), 1)
    row = lax.broadcasted_iota(jnp.int32, (span, span), 0)
    col = lax.broadcasted_iota(jnp.int32, (span, span), 1)
    eye = (
        lax.broadcasted_iota(jnp.int32, (dims, dims), 0) == lax.broadcasted_iota(jnp.int32, (dims, dims), 1)
    ).astype(F32)
    where = []
    heads_in = []
    for local in range(per_step):
        head = first_head + pl.program_id(0) * per_step + local
        chosen = []
        for kind in range(3):
            target = kind * heads + head
            chosen.append(jnp.concatenate([pool_ref[table[1, j, target]] for j in range(members)], 0))
        for part in range(2):
            seq = info[0] if part == 0 else 1 - info[0]
            where.append((local, part, pl.ds(pl.multiple_of(seq * span, span), span)))
            projected = []
            for kind in range(3):
                target = kind * heads + head
                picked = [
                    x_ref[where[-1][2], pl.ds(pl.multiple_of(table[0, j, target] * dims, dims), dims)]
                    for j in range(members)
                ]
                projected.append(dot(jnp.concatenate(picked, 1), chosen[kind]).astype(BF16))
            heads_in.append((head, projected))
    kept, systems, rights = [], [], []
    for (local, part, rows), (head, (query, key, value)) in zip(where, heads_in):
        key_wide = key.astype(F32)
        gates = gate_ref[rows, :]
        cumulative = jnp.sum(jnp.where(lane == head, gates, 0.0), axis=1, keepdims=True)
        beta = jnp.sum(jnp.where(lane == heads + head, gates, 0.0), axis=1, keepdims=True)
        norm = lax.rsqrt(jnp.sum(key_wide * key_wide, axis=1, keepdims=True) + 1e-06)
        across = jnp.where(wide == 0, cumulative, norm).T
        cumulative_row, norm_row = across[0:1, :], across[1:2, :]
        ratio = jnp.where(row >= col, jnp.exp(jnp.minimum(cumulative - cumulative_row, 0.0)), 0.0) * norm_row
        attend = ratio * dot_nt(query, key)
        systems.append(jnp.where(row > col, ratio * dot_nt(key, key), 0.0) * (beta * norm))
        growth = jnp.exp(cumulative)
        rights.append(jnp.concatenate([(beta * growth * norm) * key_wide, beta * value.astype(F32)], axis=1))
        last = cumulative[span - 1 : span, :]
        kept.append((query, key, attend, growth, norm * jnp.exp(last - cumulative), jnp.exp(last)))
    solutions = solve_lower(systems, rights)
    for (local, part, rows), (query, key, attend, growth, tail, final), solved in zip(where, kept, solutions):
        high, low = halves(solved * tail)
        pushed = dot_tn(key, high) + dot_tn(key, low)
        out = own_ref if part == 0 else send_ref
        out[local, :, :dims] = final * eye - pushed[:, :dims]
        out[local, :, dims:] = pushed[:, dims:]
        seen = dot3(attend, solved)
        lanes = slice(local * dims, (local + 1) * dims)
        query_ref[rows, lanes] = growth * query.astype(F32) - seen[:, :dims]
        core_ref[rows, lanes] = seen[:, dims:]


def local_call(info, table, rows, pool, extra, first_head, count_heads, heads, span, after=()):
    count, width = rows.shape
    dims = pool.shape[1]
    opening = isinstance(extra, tuple)
    maps = jax.ShapeDtypeStruct((count_heads, dims, 2 * dims), F32)
    wide = jax.ShapeDtypeStruct((count, count_heads * dims), F32)
    gates = jax.ShapeDtypeStruct((count, 2 * heads), F32)
    map_spec = pl.BlockSpec((PER_STEP, dims, 2 * dims), lambda i, *_: (i, 0, 0))
    row_spec = pl.BlockSpec((count, PER_STEP * dims), lambda i, *_: (0, i))
    if opening:
        more_in = [whole(extra[0].shape), smem()]
        more_out, more_out_specs = (gates,), (whole(gates.shape),)
    else:
        more_in, more_out, more_out_specs, extra = [whole(gates.shape)], (), (), (extra,)
    return pl.pallas_call(
        skipping(functools.partial(local_kernel, first_head, heads, span, PER_STEP, opening), 4 + len(extra), after),
        out_shape=(maps, maps, wide, wide) + more_out,
        grid_spec=pltpu.PrefetchScalarGridSpec(
            num_scalar_prefetch=2,
            grid=(count_heads // PER_STEP,),
            in_specs=[whole(rows.shape), whole(pool.shape)] + more_in + anywhere(after),
            out_specs=(map_spec, map_spec, row_spec, row_spec) + more_out_specs,
        ),
        compiler_params=params(28),
        cost_estimate=cost(count_heads * 2 * 2 * span * 256 * 256 * 24, 8 * MIB),
        name="local",
    )(info, table, rows, pool, *extra, *after)


def apply_map(maps, state):
    dims = maps.shape[0]
    return dot3(maps[:, :dims], state)


def combine_kernel(info, own_ref, got_ref, early_ref, both_ref, push_ref):
    later_is_own = info[0] == 1
    for h in range(own_ref.shape[0]):
        own, got = own_ref[h], got_ref[h]
        early = jnp.where(later_is_own, got, own)
        late = jnp.where(later_is_own, own, got)
        dims = own.shape[0]
        early_ref[h] = early
        both = apply_map(late, early)
        push = both[:, dims:] + late[:, dims:]
        both_ref[h, :, :dims] = both[:, :dims]
        both_ref[h, :, dims:] = push
        push_ref[h] = push


def combine_call(info, own, got, after=()):
    shape = jax.ShapeDtypeStruct(own.shape, F32)
    push = jax.ShapeDtypeStruct(own.shape[:2] + (own.shape[1],), F32)
    return pl.pallas_call(
        skipping(combine_kernel, 3, after),
        out_shape=(shape, shape, push),
        in_specs=[smem(), vmem(), vmem()] + anywhere(after),
        compiler_params=params(12),
        cost_estimate=light(own.shape[0] * 6 * 128 * 128 * 256, own.size * 16),
        name="combine",
    )(info, own, got, *after)


def hop_kernel(level, info, maps_ref, got_ref, state_ref, kept_ref, out_ref):
    arrived = info[2] == level
    for h in range(maps_ref.shape[0]):
        maps = maps_ref[h]
        dims = maps.shape[0]
        state = jnp.where(arrived, got_ref[h], state_ref[h])
        kept_ref[h] = state
        out_ref[h] = apply_map(maps, state) + maps[:, dims:]


def hop_call(level, info, maps, got, state, after=()):
    shape = jax.ShapeDtypeStruct(state.shape, F32)
    return pl.pallas_call(
        skipping(functools.partial(hop_kernel, level), 4, after),
        out_shape=(shape, shape),
        in_specs=[smem(), vmem(), vmem(), vmem()] + anywhere(after),
        compiler_params=params(12),
        cost_estimate=light(maps.shape[0] * 6 * 128 * 128 * 128, maps.size * 8),
        name="hop",
    )(info, maps, got, state, *after)


def split_kernel(level, info, maps_ref, got_ref, state_ref, keep_ref, send_ref):
    second = info[0] == 1
    arrived = info[2] == level
    for h in range(maps_ref.shape[0]):
        maps = maps_ref[h]
        state = jnp.where(arrived, got_ref[h], state_ref[h])
        dims = maps.shape[0]
        middle = apply_map(maps, state) + maps[:, dims:]
        keep_ref[h] = jnp.where(second, middle, state)
        send_ref[h] = jnp.where(second, state, middle)


def split_call(level, info, maps, got, state, after=()):
    shape = jax.ShapeDtypeStruct(state.shape, F32)
    return pl.pallas_call(
        skipping(functools.partial(split_kernel, level), 4, after),
        out_shape=(shape, shape),
        in_specs=[smem(), vmem(), vmem(), vmem()] + anywhere(after),
        compiler_params=params(12),
        cost_estimate=light(maps.shape[0] * 6 * 128 * 128 * 128, maps.size * 8),
        name="split",
    )(info, maps, got, state, *after)


def mix_kernel(span, first_head, info, core_ref, query_ref, keep_ref, got_ref, back_ref, gain_ref, cot_ref, mixed_ref, wsend_ref, wkeep_ref):
    count = keep_ref.shape[0]
    half = count // 2
    dims = gain_ref.shape[1]
    tiles = wsend_ref.shape[0] - 1
    each = tiles // half
    stripe = dims // 8
    gain_part = jnp.zeros((8, dims), F32)
    for part in range(2):
        seq = info[0] if part == 0 else 1 - info[0]
        rows = pl.ds(pl.multiple_of(seq * span, span), span)
        for h in range(count):
            lanes = slice(h * dims, (h + 1) * dims)
            state = (keep_ref if part == 0 else got_ref)[h]
            core = core_ref[rows, lanes] + dot3(query_ref[rows, lanes], state)
            normal = core * lax.rsqrt(jnp.mean(core * core, axis=1, keepdims=True) + 1e-05)
            back = back_ref[rows, (first_head + h) * dims : (first_head + h + 1) * dims]
            gain_part += jnp.sum((normal * back).reshape(-1, 8, dims), axis=0)
            mixed_ref[rows, lanes] = (normal * gain_ref[...]).astype(BF16)
    wkeep_ref[tiles] = gain_part
    wsend_ref[tiles] = gain_part
    product = dot_tn(mixed_ref[...], cot_ref[...])
    for h in range(count):
        first = (h % half) * each
        pieces = [
            (first + i * stripe, product[h * dims : (h + 1) * dims, i * 128 : (i + 1) * 128].reshape(stripe, 8, 128))
            for i in range(product.shape[1] // 128)
        ]
        for side, ref in ((0, wkeep_ref), (1, wsend_ref)):

            @pl.when((info[1] ^ side) == h // half)
            def _(ref=ref, pieces=pieces):
                for at, piece in pieces:
                    ref[at : at + stripe] = piece


def mix_call(info, first_head, core, query, keep, got, back, gain, cot, span, after=()):
    count, width = cot.shape
    heads_here = keep.shape[0]
    dims = gain.shape[1]
    weight = jax.ShapeDtypeStruct((heads_here // 2 * dims * width // 1024 + 1, 8, 128), F32)
    return pl.pallas_call(
        skipping(functools.partial(mix_kernel, span, first_head), 8, after),
        out_shape=(jax.ShapeDtypeStruct((count, heads_here * dims), BF16), weight, weight),
        in_specs=[smem()] + [vmem()] * 7 + anywhere(after),
        out_specs=(vmem(), vmem(), vmem()),
        compiler_params=params(20),
        cost_estimate=cost(heads_here * 2 * 512 * 1024 * 128, 3 * MIB),
        name="mix",
    )(info, core, query, keep, got, back, gain, cot, *after)


def back_kernel(cot_ref, weight_ref, out_ref):
    out_ref[...] = dot_nt(cot_ref[...], weight_ref[...])


def back_call(cot, weight):
    count, width = cot.shape
    row_spec = pl.BlockSpec((128, width), lambda i: (i, 0))
    return pl.pallas_call(
        back_kernel,
        out_shape=jax.ShapeDtypeStruct((count, width), F32),
        grid=(count // 128,),
        in_specs=[row_spec, whole(weight.shape)],
        out_specs=row_spec,
        compiler_params=params(12),
        cost_estimate=cost(2 * count * width * width, 5 * MIB),
        name="back",
    )(cot, weight)


def finish_kernel(groups, *refs):
    weight_ref, out_ref, done_ref = refs[groups:]
    done_ref[...] = jnp.zeros_like(done_ref)
    stacked = jnp.concatenate([ref[...] for ref in refs[:groups]], axis=1)
    out_ref[...] = dot(stacked, weight_ref[...]).astype(BF16)


def finish_call(mixed, weight):
    count = mixed[0].shape[0]
    width = weight.shape[1]
    row_spec = pl.BlockSpec((128, width), lambda i: (i, 0))
    return pl.pallas_call(
        functools.partial(finish_kernel, len(mixed)),
        out_shape=(jax.ShapeDtypeStruct((count, width), BF16), jax.ShapeDtypeStruct((8, 128), F32)),
        grid=(count // 128,),
        in_specs=[pl.BlockSpec((128, m.shape[1]), lambda i: (i, 0)) for m in mixed] + [whole(weight.shape)],
        out_specs=(row_spec, whole((8, 128))),
        compiler_params=params(12),
        cost_estimate=cost(2 * count * width * width, 4 * MIB),
        name="finish",
    )(*mixed, weight)


def fold_kernel(parts, terms, where, flips, info, *refs):
    ins, outs = refs[: parts * terms], refs[parts * terms :]
    size = ins[0].shape[0] - 1
    share = outs[0].shape[0] - 1
    last = sum(ref[size] for ref in ins)
    for flip, out in zip(flips, outs):
        first = (info[where] ^ flip) * share
        if parts == 1:
            out[:share] = sum(ref[pl.ds(first, share)] for ref in ins)
        else:
            for part in range(parts):

                @pl.when((first >= part * size) & (first < (part + 1) * size))
                def _(part=part, out=out, first=first):
                    out[:share] = sum(ref[pl.ds(first - part * size, share)] for ref in ins[part * terms : (part + 1) * terms])

        out[share] = last


def fold_call(info, where, flips, arrays, parts, after=()):
    terms = len(arrays) // parts
    size = arrays[0].shape[0] - 1
    share = size * parts // len(flips)
    shape = jax.ShapeDtypeStruct((share + 1, 8, 128), F32)
    return pl.pallas_call(
        skipping(functools.partial(fold_kernel, parts, terms, where, flips), 1 + len(arrays), after),
        out_shape=[shape] * len(flips),
        in_specs=[smem()] + [vmem()] * len(arrays) + anywhere(after),
        compiler_params=params(12),
        cost_estimate=light(size * 1024 * len(arrays), size * 4096 * (len(arrays) + 1)),
        name="fold",
    )(info, *arrays, *after)


def total_kernel(*refs):
    ins, (piece_ref, last_ref) = refs[:-2], refs[-2:]
    size = piece_ref.shape[0]
    piece_ref[...] = sum(ref[:size] for ref in ins)
    last_ref[...] = sum(ref[size] for ref in ins)


def total_call(arrays):
    size = arrays[0].shape[0] - 1
    return pl.pallas_call(
        total_kernel,
        out_shape=(jax.ShapeDtypeStruct((size, 8, 128), F32), jax.ShapeDtypeStruct((8, 128), F32)),
        in_specs=[vmem()] * len(arrays),
        out_specs=(vmem(), vmem()),
        compiler_params=params(12),
        cost_estimate=light(size * 4096, size * 4096 * 5),
        name="total",
    )(*arrays)


def lay_kernel(where, info, own_ref, got_ref, out_ref):
    share = own_ref.shape[0]
    out_ref[pl.ds(info[where] * share, share)] = own_ref[...]
    out_ref[pl.ds((1 - info[where]) * share, share)] = got_ref[...]


def lay_call(info, where, own, got, after=()):
    share = own.shape[0]
    return pl.pallas_call(
        skipping(functools.partial(lay_kernel, where), 3, after),
        out_shape=jax.ShapeDtypeStruct((share * 2, 8, 128), F32),
        in_specs=[smem(), vmem(), vmem()] + anywhere(after),
        compiler_params=params(12),
        cost_estimate=light(0, share * 16384),
        name="lay",
    )(info, own, got, *after)


def join_kernel(scale, stripe, blocks, flags, info, *refs):
    sums = len(blocks)
    lasts, (out_ref, gain_ref) = refs[4 * sums : 5 * sums], refs[-2:]
    columns = out_ref.shape[1] // 128
    dims = stripe * 8
    size = refs[0].shape[0]
    per_half = size // stripe
    for g in range(sums):
        for part in range(2):
            side = info[1] if part == 0 else 1 - info[1]
            for flip in range(2):
                ref = refs[4 * g + 2 * part + flip]
                low = info[flags[g]] == flip
                for at in range(2):

                    @pl.when(low if at == 0 else jnp.logical_not(low))
                    def _(ref=ref, at=at, side=side, g=g):
                        for index in range(per_half):
                            block, col = divmod(at * per_half + index, columns)
                            base, half = blocks[g][block]
                            rows = pl.ds(pl.multiple_of((base + side * half) * dims, dims), dims)
                            values = ref[index * stripe : (index + 1) * stripe].reshape(dims, 128) * scale
                            out_ref[rows, col * 128 : (col + 1) * 128] = values.astype(BF16)

    gain_ref[...] = jnp.sum(sum(ref[...] for ref in lasts), axis=0, keepdims=True) * scale


def join_call(info, parts, lasts, blocks, flags, scale, dims, width):
    total = sum(p.shape[0] for p in parts) * 1024 // width
    return pl.pallas_call(
        functools.partial(join_kernel, scale, dims // 8, blocks, flags),
        out_shape=(jax.ShapeDtypeStruct((total, width), BF16), jax.ShapeDtypeStruct((1, 128), F32)),
        in_specs=[smem()] + [vmem()] * (len(parts) + len(lasts)),
        out_specs=(vmem(), vmem()),
        compiler_params=params(16),
        name="join",
    )(info, *parts, *lasts)


def shards(mesh, features, weight_pool, pattern_in, pattern_pool, gate_weight, decay_rate, beta_bias, norm_gain, out_weight, cotangent):
    n_shot, n_tm = mesh.shape["shot"], mesh.shape["tm"]
    n_x, n_z = n_shot // CORES, n_tm // PAIR
    seqs, span, width = features.shape
    heads = decay_rate.shape[0]
    dims = weight_pool.shape[1]
    count = seqs * span
    both = ("shot", "tm")
    shot, tm = lax.axis_index("shot"), lax.axis_index("tm")
    x, core, z, y = shot // CORES, shot % CORES, tm // PAIR, tm % PAIR

    def place(xi, ci, zi, yi):
        return (xi * CORES + ci) * n_tm + zi * PAIR + yi

    def moved(array, shift):
        dx, dc, dz, dy = shift
        route = []
        for xi in range(n_x):
            for ci in range(CORES):
                for zi in range(n_z):
                    for yi in range(PAIR):
                        route.append((place(xi, ci, zi, yi), place(xi ^ dx, ci ^ dc, zi ^ dz, yi ^ dy)))
        return lax.ppermute(array, both, route)

    def lifted(array, level):
        ends = ((level, level + 1), (level + 1, level))
        route = [(a * PAIR + yi, b * PAIR + yi) for a, b in ends for yi in range(PAIR)]
        return lax.ppermute(array, "tm", route)

    def bits(size):
        return [1 << bit for bit in range(size.bit_length() - 1)]

    steps_x = [((reach, 0, 0, 0), (x // reach) % 2) for reach in bits(n_x)]
    steps_y = [((0, 0, 0, reach), (y // reach) % 2) for reach in bits(PAIR)]
    steps_z = [((0, 0, reach, 0), (z // reach) % 2) for reach in bits(n_z)]
    labelled = [(shift, 3 + i) for i, (shift, _) in enumerate(steps_x + steps_y + steps_z)]
    on_x, on_y = labelled[: len(steps_x)], labelled[len(steps_x) : len(steps_x) + len(steps_y)]
    on_z = labelled[len(steps_x) + len(steps_y) :]
    info = jnp.stack([y, core, z] + [bit for _, bit in steps_x + steps_y + steps_z]).astype(jnp.int32)
    table = jnp.stack([pattern_in.T, pattern_pool.T])
    levels = jnp.stack([decay_rate, beta_bias])
    rows = features.reshape(count, width)
    cot = cotangent.reshape(count, width)
    gain = norm_gain.reshape(1, dims)
    relays = range(len(RELAYS))
    last = len(RELAYS) - 1
    first_of = [sum(RELAYS[:g]) for g in relays]

    extra = (gate_weight.T, levels)
    locals_ = []
    for g in relays:
        after = [locals_[-1][0]] if g else []
        out = list(local_call(info, table, rows, weight_pool, extra, first_of[g], RELAYS[g], heads, span, after))
        if g == 0:
            extra = out.pop()
        locals_.append(out)
    back = back_call(cot, out_weight)
    maps = [None] * len(RELAYS)
    states = [jnp.zeros((size, dims, dims), F32) for size in RELAYS]
    sends = [None] * len(RELAYS)
    ready = [None] * len(RELAYS)
    turns = sorted((stage + DELAYS[g], g, stage) for g in relays for stage in range(n_z))
    after = [locals_[last][0]]
    for _, g, stage in turns:
        if stage == 0:
            if g == last:
                after.append(back)
            maps[g] = combine_call(info, locals_[g][0], moved(locals_[g][1], (0, 0, 0, 1)), after)
            sends[g] = maps[g][2]
        else:
            came = lifted(sends[g], stage - 1)
            if stage < n_z - 1:
                states[g], sends[g] = hop_call(stage, info, maps[g][1], came, states[g], after)
            else:
                keep, sends[g] = split_call(stage, info, maps[g][0], came, states[g], after)
                ready[g] = (keep, moved(sends[g], (0, 0, 0, 1)))
        after = [sends[g]]
    sums = range(len(SUMS))
    orders = [on_x + on_y + on_z if g % 2 == 0 else on_y + on_z + on_x for g in sums]
    mixed, arrays, parts = [], [], []
    for group in SUMS:
        terms = []
        for g in group:
            states_g = *locals_[g][2:], *ready[g]
            flat, w_send, w_keep = mix_call(info, first_of[g], *states_g, back, gain, cot, span, after)
            after = [w_keep]
            mixed.append(flat)
            terms += [w_keep, moved(w_send, (0, 1, 0, 0))]
        arrays.append(terms)
    for g in sums:
        shift, where = orders[g][0]
        own, send = fold_call(info, where, (0, 1), arrays[g], len(SUMS[g]), after)
        after = [own]
        arrays[g] = [own, moved(send, shift)]
    output, done = finish_call(mixed, out_weight)
    scale = 1.0 / math.sqrt(count * n_shot * n_tm)

    previous = after[0]
    for step in range(1, len(orders[0])):
        for g in sums:
            shift, where = orders[g][step]
            after = [previous]
            if g == sums[-1] and step == 1:
                after.append(done)
            own, send = fold_call(info, where, (0, 1), arrays[g], 1, after)
            arrays[g] = [own, moved(send, shift)]
            previous = own
    totals = [total_call(a) for a in arrays]
    pieces = [t[0] for t in totals]
    for step in reversed(range(1, len(orders[0]))):
        arrived = [moved(pieces[g], orders[g][step][0]) for g in sums]
        previous = pieces[-1]
        for g in sums:
            pieces[g] = previous = lay_call(info, orders[g][step][1], pieces[g], arrived[g], [previous])
    ends = []
    for g in sums:
        arrived = moved(pieces[g], orders[g][0][0])
        ends += [pieces[g], arrived, moved(pieces[g], (0, 1, 0, 0)), moved(arrived, (0, 1, 0, 0))]
    flags = [orders[g][0][1] for g in sums]
    blocks = [[(first_of[r] + i, RELAYS[r] // 2) for r in SUMS[g] for i in range(RELAYS[r] // 2)] for g in sums]
    weight_grad, gain_grad = join_call(info, ends, [t[1] for t in totals], blocks, flags, scale, dims, width)
    return (output.reshape(seqs, span, width), weight_grad, gain_grad.reshape(dims))


def solution(mesh):
    placed = (P("shot", "tm", None), P(), P(), P(), P(), P(), P(), P(), P(), P("shot", "tm", None))
    return jax.shard_map(
        functools.partial(shards, mesh),
        mesh=mesh,
        in_specs=placed,
        out_specs=(P("shot", "tm", None), P(), P()),
        check_vma=False,
    )
```
